32 devices in a mesh: dp: 16 (over z, x, core), tensor: 2 (over y).
Axes of the slice: x: 2, y: 2, z: 4, core: 2. Of those that a mesh axis runs over, the one named last changes fastest.
Arguments:
- tokens: bfloat16 [16384, 1024], P('dp'), may hold values from -6 to 6
- lengths: int32 [16, 64], P('dp'), may hold values from 1 to 60, 1024 in all within a row
- w_qkv: bfloat16 [2, 1024, 3, 1024], P(None, None, None, 'tensor'), may hold values from -0.1875 to 0.1875
- w_out: bfloat16 [2, 1024, 1024], P(None, None, 'tensor'), may hold values from -0.5 to 0.5
- w_up: bfloat16 [2, 1024, 2048], P(None, None, 'tensor'), may hold values from -0.1875 to 0.1875
- w_down: bfloat16 [2, 1024, 2048], P(None, None, 'tensor'), may hold values from -0.125 to 0.125
- norm_gain: float32 [2, 2, 1024], replicated, may hold values from 0.5 to 1.5
- norm_bias: float32 [2, 2, 1024], replicated, may hold values from -1 to 1
- cotangent: bfloat16 [16384, 1024], P('dp'), may hold values from -6 to 6
Outputs:
- output: bfloat16 [16384, 1024], P('dp')
- grad_tokens: float32 [16384, 1024], P('dp')
- grad_qkv: float32 [2, 1024, 3, 1024], P(None, 'dp', None, 'tensor')
- grad_out: float32 [2, 1024, 1024], P(None, 'dp', 'tensor')
- grad_up: float32 [2, 1024, 2048], P(None, 'dp', 'tensor')
- grad_down: float32 [2, 1024, 2048], P(None, 'dp', 'tensor')
- grad_gain: float32 [2, 2, 1024], P(None, None, 'dp')
- grad_bias: float32 [2, 2, 1024], P(None, None, 'dp')
The draws below stay inside these ranges and needn't reach their ends.
Inputs may be any that keep to these rules, and one draw needn't show every extreme that they name: `lengths`: each row sums to 1024, and some item of every row has exactly 60 tokens.
All inputs are finite; a program needn't handle non-finite values.
Results may differ from the reference program's by a relative error of at most 0.025.
Values may be sent and summed in bfloat16 or wider, within the bound.
A program may use at most 192 MiB of HBM per device.

```python
import math
import jax
import jax.numpy as jnp
import numpy as np
from jax import lax

D = 1024
HEADS = 8
HEAD_DIM = 128
FF = 2048
LAYERS = 2
LONGEST = 60
TOK_DEV = 1024
ITEMS = 64
TOKENS = 16384
N_DP = 16
N_TENSOR = 2


def levels(own_key, dims, shards, low, high):
    factor_of = 1.0
    for axis_at, shards_of in shards:
        heights = jax.random.uniform(jax.random.fold_in(jax.random.fold_in(own_key, 6), axis_at), (shards_of,), jnp.float32, low / len(shards), high / len(shards))
        factor_of = factor_of * jnp.repeat(jnp.exp(heights), dims[axis_at] // shards_of).reshape((-1,) + (1,) * (len(dims) - 1 - axis_at))
    return factor_of


def length_profile(count, total, reach, slope):
    loads = [(1 << 20) // math.isqrt(grade ** slope) + 1 for grade in range(2, count + 1)]
    rest, given = total - reach - (count - 1), [1] * (count - 1)
    while rest > 0:
        free = [i for i in range(count - 1) if given[i] < reach]
        whole, remaining = sum([loads[i] for i in free]), rest
        for i in free:
            extra = min(reach - given[i], max(1, remaining * loads[i] // whole), rest)
            given[i] = given[i] + extra
            rest = rest - extra
    return np.array([reach] + given)


def uneven_parts(key, number_of, total, bound, slope):
    if number_of == 2:
        one = jax.random.randint(key, (), max(1, total - bound), min(bound, total - 1) + 1)
        return jnp.stack([one, total - one])
    tallies = jnp.asarray(length_profile(number_of, total, bound, slope), jnp.int32)
    couples = (number_of - 1) // 2
    donor, receiver = tallies[1:1 + 2 * couples:2], tallies[2:2 + 2 * couples:2]
    margin = jnp.minimum(donor - 1, bound - receiver)
    moved = jax.random.randint(jax.random.fold_in(key, 1), (couples,), 0, 1 << 20) % (margin + 1)
    tallies = tallies.at[1:1 + 2 * couples:2].set(donor - moved).at[2:2 + 2 * couples:2].set(receiver + moved)
    return tallies[jax.random.permutation(jax.random.fold_in(key, 2), number_of)]


def bell_draw(stream_key, shape, width, limit, cuts=(), held_as=jnp.bfloat16):
    level = levels(stream_key, shape, cuts, -0.22, 0.18) if cuts else 1.0
    result = jax.random.normal(stream_key, shape, jnp.float32) * width * level
    return jnp.minimum(jnp.maximum(result, -limit), limit).astype(held_as)


def setup_inputs(seed: int = 0) -> dict:
    key_list = jax.random.split(jax.random.key(seed), 10)
    return {
        "tokens": bell_draw(key_list[0], (TOKENS, D), 1.0, 6.0, ((0, 16),)),
        "lengths": jax.vmap(lambda own: uneven_parts(own, ITEMS, TOK_DEV, LONGEST, 2))(jax.random.split(key_list[1], N_DP)).reshape((N_DP, ITEMS)).astype(jnp.int32),
        "w_qkv": bell_draw(key_list[2], (LAYERS, D, 3, D), D ** -0.5, 0.1875, ((3, 2),)),
        "w_out": bell_draw(key_list[3], (LAYERS, D, D), (D // 8) ** -0.5, 0.5, ((2, 2),)),
        "w_up": bell_draw(key_list[4], (LAYERS, D, FF), D ** -0.5, 0.1875, ((2, 2),)),
        "w_down": bell_draw(key_list[5], (LAYERS, D, FF), FF ** -0.5, 0.125, ((2, 2),)),
        "norm_gain": jnp.clip(1.0 + 0.1 * jax.random.normal(key_list[6], (LAYERS, 2, D), jnp.float32), 0.5, 1.5),
        "norm_bias": bell_draw(key_list[7], (LAYERS, 2, D), 0.2, 1.0, (), jnp.float32),
        "cotangent": bell_draw(key_list[8], (TOKENS, D), 1.0, 6.0, ((0, 16),)),
    }


@jax.custom_vjp
def low(v):
    return lax.optimization_barrier(v.astype(jnp.bfloat16)).astype(jnp.float32)

@jax.custom_vjp
def low_back(v):
    return v

def low_keep(v):
    return (low(v), None)

def low_pass(kept, grad):
    return (grad,)

def back_keep(v):
    return (v, None)

def back_low(kept, grad):
    return (low(grad),)
low.defvjp(low_keep, low_pass)
low_back.defvjp(back_keep, back_low)
epsilon = 1e-05
highest = lax.Precision.HIGHEST

def matmul(left, right):
    return jnp.dot(left, right, precision=highest, preferred_element_type=jnp.float32)

def norm_rows(values, gain, shift):
    center = values - lax.optimization_barrier(jnp.mean(values, axis=-1, keepdims=True))
    spread = lax.optimization_barrier(jnp.mean(center * center, axis=-1, keepdims=True))
    return center * lax.rsqrt(spread + epsilon) * gain + shift

def attend(items):
    query, keys, values, segment = items
    place = jnp.arange(segment.shape[0], dtype=jnp.int32)
    allowed = (segment[:, None] == segment[None, :]) & (place[None, :] <= place[:, None])
    scores = jnp.einsum('qhd,khd->hqk', query, keys, precision=highest) * HEAD_DIM ** (-0.5)
    scores = low_back(scores)
    scores = jnp.where(allowed[None], scores, -1e+30)
    shifted = scores - lax.optimization_barrier(jnp.max(scores, axis=-1, keepdims=True))
    weights = jnp.exp(shifted)
    probs = low(weights / lax.optimization_barrier(jnp.sum(weights, axis=-1, keepdims=True)))
    return jnp.einsum('hqk,khd->qhd', probs, values, precision=highest)

def forward(stream, w_qkv, w_out, w_up, w_down, norm_gain, norm_bias, segment):
    group = HEADS // N_TENSOR
    cols = group * HEAD_DIM
    hidden = FF // N_TENSOR
    for layer in range(LAYERS):
        normed = low(norm_rows(stream, norm_gain[layer, 0], norm_bias[layer, 0]))
        total = None
        for part in range(N_TENSOR):
            entry = low_back(normed)
            weight = w_qkv[layer][:, :, part * cols:(part + 1) * cols].reshape(D, 3 * cols)
            projected = low_back(low(matmul(entry, weight)))
            shape = (N_DP, TOK_DEV, group, HEAD_DIM)
            query = projected[:, :cols].reshape(shape)
            keys = projected[:, cols:2 * cols].reshape(shape)
            values = projected[:, 2 * cols:].reshape(shape)
            mixed = lax.map(jax.checkpoint(attend), (query, keys, values, segment))
            mixed = low_back(low(mixed.reshape(TOKENS, cols)))
            term = low(matmul(mixed, w_out[layer][:, part * cols:(part + 1) * cols].T))
            total = term if total is None else total + term
        stream = stream + low_back(total)
        normed_two = low(norm_rows(stream, norm_gain[layer, 1], norm_bias[layer, 1]))
        total = None
        for part in range(N_TENSOR):
            entry = low_back(normed_two)
            upward = low_back(matmul(entry, w_up[layer][:, part * hidden:(part + 1) * hidden]))
            active = low(jax.nn.gelu(upward, approximate=False))
            term = low(matmul(active, w_down[layer][:, part * hidden:(part + 1) * hidden].T))
            total = term if total is None else total + term
        stream = stream + low_back(total)
    return stream

def reference(tokens, lengths, w_qkv, w_out, w_up, w_down, norm_gain, norm_bias, cotangent):
    ends = jnp.cumsum(lengths, axis=1).astype(jnp.int32)
    place = jnp.arange(TOK_DEV, dtype=jnp.int32)
    segment = lax.optimization_barrier(jnp.sum((place[None, :, None] >= ends[:, None, :]).astype(jnp.int32), axis=-1)).astype(jnp.int32)

    def run(a, b, c, d, e, f, g):
        return forward(a, b, c, d, e, f, g, segment)
    output, pull = jax.vjp(run, tokens.astype(jnp.float32), w_qkv.astype(jnp.float32), w_out.astype(jnp.float32), w_up.astype(jnp.float32), w_down.astype(jnp.float32), norm_gain, norm_bias)
    grads = pull(cotangent.astype(jnp.float32))
    return (output.astype(jnp.bfloat16), grads[0], grads[1], grads[2], grads[3], grads[4], grads[5], grads[6])
```

```python
import functools
from types import SimpleNamespace

import jax
import jax.numpy as jnp
from jax import lax
from jax.experimental import pallas as pl
from jax.experimental.pallas import tpu as pltpu
from jax.sharding import PartitionSpec as P

HEAD_DIM = 128
TILE = 64
EPS = 1e-05
MASKED = -1e30
MESH = pl.DeviceIdType.MESH
VMEM = pltpu.VMEM
ANY = pl.ANY
F32 = jnp.float32
BF16 = jnp.bfloat16
SCALE = HEAD_DIM**-0.5
VMEM_LIMIT = 62 << 20
GROUP = 16
CHUNK = 32

ERFC = (
    0.22567586600780487,
    0.22566960752010345,
    0.20784251391887665,
    0.16854380071163177,
    0.14142295718193054,
    -0.005586510524153709,
    0.1690569967031479,
    -0.18288171291351318,
    0.05025661736726761,
)


def dot_nn(a, b):
    return lax.dot_general(a, b, (((1,), (0,)), ((), ())), preferred_element_type=F32)


def dot_nt(a, b):
    return lax.dot_general(a, b, (((1,), (1,)), ((), ())), preferred_element_type=F32)


def dot_tn(a, b):
    return lax.dot_general(a, b, (((0,), (0,)), ((), ())), preferred_element_type=F32)


def rows_at(index, size):
    return pl.ds(pl.multiple_of(index * size, size), size)


def flip(value, bit):
    return value + bit * (1 - 2 * lax.rem(value // bit, 2))


def normalize(x):
    center = x - jnp.mean(x, axis=-1, keepdims=True)
    spread = lax.rsqrt(jnp.mean(center * center, axis=-1, keepdims=True) + EPS)
    return center * spread, spread


def gelu_parts(u):
    t = 1.0 / (1.0 + (0.4 * 0.7071067811865476) * jnp.abs(u))
    q = jnp.full_like(t, ERFC[-1])
    for c in ERFC[-2::-1]:
        q = q * t + c
    e = jnp.exp(-0.5 * (u * u))
    tail = 0.5 * (t * q) * e
    cdf = jnp.where(u >= 0, 1.0 - tail, tail)
    return u * cdf, cdf + u * (e * 0.3989422804014327)


class Copies:
    def __init__(self, sems):
        self.sems, self.n, self.open = sems, 0, []

    def start(self, src, dst):
        assert self.n < self.sems.shape[0]
        copy = pltpu.make_async_copy(src, dst, self.sems.at[self.n])
        self.n += 1
        copy.start()
        return copy

    def save(self, src, dst):
        self.open.append(self.start(src, dst))
        return self.open[-1]

    def settle(self, copy):
        self.open.remove(copy)
        copy.wait()

    def finish(self):
        for copy in self.open:
            copy.wait()


class Remote:
    def __init__(self, send, recv):
        self.send, self.recv, self.n, self.sent = send, recv, 0, []

    def start(self, src, dst, device):
        assert self.n < self.send.shape[0]
        copy = pltpu.make_async_remote_copy(
            src_ref=src,
            dst_ref=dst,
            send_sem=self.send.at[self.n],
            recv_sem=self.recv.at[self.n],
            device_id=device,
            device_id_type=MESH,
        )
        self.n += 1
        copy.start()
        self.sent.append(copy)
        return copy

    def finish(self):
        for copy in self.sent:
            copy.wait_send()


def greet(devices):
    barrier = pltpu.get_barrier_semaphore()
    for device in devices:
        pl.semaphore_signal(barrier, inc=1, device_id=device, device_id_type=MESH)
    pl.semaphore_wait(barrier, len(devices))


class Gather:
    def __init__(self, remote, own, other, order):
        self.remote, self.own, self.other, self.order = remote, own, other, order
        me, t = lax.axis_index("dp"), lax.axis_index("tensor")
        self.me, self.t = me, t
        self.have = [lax.rem(me, 8)]
        self.stage = 0
        self.flying = []

    def block(self, ref, index):
        size = ref.shape[0] // 8
        return ref.at[rows_at(index, size), :]

    def first(self):
        b = self.have[0]
        self.flying = [
            self.remote.start(
                self.block(self.own, b), self.block(self.other, b), (self.me, 1 - self.t)
            )
        ]

    def step(self):
        for copy in self.flying:
            copy.wait_recv()
        if self.stage == 3:
            return
        if self.stage > 0:
            bit = self.order[self.stage - 1]
            self.have = self.have + [flip(b, bit) for b in self.have]
        bit = self.order[self.stage]
        self.stage += 1
        device = (flip(self.me, bit), self.t)
        self.flying = [
            self.remote.start(self.block(self.other, b), self.block(self.other, b), device)
            for b in self.have
        ]


class Scatter:
    BITS = (1, 2, 4, 8)

    def __init__(self, remote, grad, recvs, stage=0):
        self.remote, self.grad, self.recvs, self.stage = remote, grad, recvs, stage
        self.me, self.t = lax.axis_index("dp"), lax.axis_index("tensor")
        self.base = 0
        self.count = 16 >> stage

    def send(self):
        bit = self.BITS[self.stage]
        mine = lax.rem(self.me // bit, 2)
        half = self.count // 2
        out = self.base + (1 - mine) * half
        self.base = self.base + mine * half
        self.count = half
        self.flying = self.remote.start(
            self.grad.at[pl.ds(out, half)],
            self.recvs[self.stage],
            (flip(self.me, bit), self.t),
        )

    def add(self):
        self.flying.wait_recv()
        recv = self.recvs[self.stage]
        self.stage += 1

        def body(i, carry):
            at = self.base + i
            self.grad[at] = (self.grad[at].astype(F32) + recv[i].astype(F32)).astype(BF16)
            return carry

        lax.fori_loop(0, self.count, body, 0)

    def step(self):
        self.add()
        self.send()

    def last(self):
        self.flying.wait_recv()
        return self.grad[self.base].astype(F32) + self.recvs[self.stage][0].astype(F32)


def forward_kernel(layer, names, *args):
    r = SimpleNamespace(**dict(zip(names, args)))
    copies = Copies(r.sem)
    remote = Remote(r.send, r.recv)
    me, t = lax.axis_index("dp"), lax.axis_index("tensor")
    rows, width = r.x.shape
    cols = r.qkv_own.shape[-1]
    heads = cols // HEAD_DIM
    half = r.up_own.shape[-1]
    pieces = width // cols

    x_load = copies.start(r.x_in, r.x_raw if layer == 0 else r.x)
    greet([(me, 1 - t), (flip(me, 2), t), (flip(me, 4), t), (flip(me, 1), t)])

    own = [r.qkv_own.at[layer, j] for j in range(3)]
    one, two = (2, 4, 1), (4, 2, 1)
    if layer == 0:
        other = [r.qkv_oth.at[j] for j in range(3)]
        gq = [Gather(remote, own[j], other[j], two if j == 1 else one) for j in range(3)]
        go = Gather(remote, r.out_own.at[0], r.out_oth, two)
        gu = Gather(remote, r.up_own.at[0], r.up_oth, one)
        gd = Gather(remote, r.dn_own.at[0], r.dn_oth, two)
        nq = [
            Gather(remote, r.qkv_own.at[1, j], r.qkv_nxt.at[j], one if j == 1 else two)
            for j in range(3)
        ]
        no = Gather(remote, r.out_own.at[1], r.out_nxt, one)
        for g in (*gq, go, gu, gd):
            g.first()
    else:
        gu = Gather(remote, r.up_own.at[1], r.up_oth, one)
        gd = Gather(remote, r.dn_own.at[1], r.dn_oth, two)
        gu.first()
        gd.first()

    w_load = [copies.start(own[j], r.wq.at[j]) for j in range(3)]
    bias_load = copies.start(r.bias, r.mask)
    wo_load = [copies.start(r.out_own.at[layer], r.wo.at[0]), None]
    wu_load = [copies.start(r.up_own.at[layer], r.wu.at[0]), None]
    wd_load = [copies.start(r.dn_own.at[layer], r.wd.at[0]), None]
    if layer == 1:
        w_load += [copies.start(r.qkv_oth.at[j], r.wq.at[3 + j]) for j in range(3)]
        wo_load[1] = copies.start(r.out_oth, r.wo.at[1])

    x = r.x

    def norm(which, h, xh, spread, source=None):
        gain = r.gain[which : which + 1, :]
        shift = r.shift[which : which + 1, :]

        def body(i, carry):
            at = rows_at(i, CHUNK)
            if source is not None:
                values = source[at, :].astype(F32)
                x[at, :] = values
            else:
                values = x[at, :]
            hat, rs = normalize(values)
            xh[at, :] = hat.astype(BF16)
            h[at, :] = (hat * gain + shift).astype(BF16)
            spread[at, :] = jnp.broadcast_to(rs, (CHUNK, HEAD_DIM))
            return carry

        lax.fori_loop(0, rows // CHUNK, body, 0)

    x_load.wait()
    norm(0, r.h1, r.xh1, r.r1, r.x_raw if layer == 0 else None)
    h1_save = copies.save(r.h1, r.h1_out)
    copies.save(r.xh1, r.xh1_out)
    copies.save(r.r1, r.r1_out)

    qkv, wq = r.qkv, r.wq

    def project(j):
        qkv[j] = dot_nn(r.h1[...], wq[j]).astype(BF16)

    def attend(group, start, stop):
        lane = lax.broadcasted_iota(jnp.int32, (TILE, HEAD_DIM), 1)

        def body(i, carry):
            q_at = rows_at(i, TILE)
            k_at = pl.ds(pl.multiple_of(jnp.maximum(i - 1, 0) * TILE, TILE), 2 * TILE)
            mask = r.mask[q_at, :]
            kept = jnp.zeros((TILE, HEAD_DIM), F32)
            for head in range(heads):
                c = slice(head * HEAD_DIM, (head + 1) * HEAD_DIM)
                s = dot_nt(qkv[3 * group, q_at, c], qkv[3 * group + 1, k_at, c]) * SCALE + mask
                top = jnp.max(s, axis=-1, keepdims=True)
                e = jnp.exp(s - top)
                total = jnp.sum(e, axis=-1, keepdims=True)
                p = (e * (1.0 / total)).astype(BF16)
                mixed = dot_nn(p, qkv[3 * group + 2, k_at, c])
                r.o[group, q_at, c] = mixed.astype(BF16)
                kept = jnp.where(lane == head, top + jnp.log(total), kept)
            r.lse[group, q_at, :] = kept
            return carry

        lax.fori_loop(start, stop, body, 0)

    def out_project(group):
        def body(n, carry):
            at = rows_at(n, cols)
            x[:, at] += dot_nt(r.o[group], r.wo[group, at, :])
            return carry

        lax.fori_loop(0, pieces, body, 0)

    tiles = rows // TILE
    quarter = tiles // 4
    for j in range(3):
        w_load[j].wait()
        project(j)
        if layer == 0:
            if j == 0:
                gq[0].step()
            if j == 2:
                gq[1].step()
    bias_load.wait()
    for i in range(4):
        attend(0, i * quarter, (i + 1) * quarter)
        if layer == 0:
            (lambda: gq[0].step(), lambda: gq[2].step(), lambda: gq[1].step(), lambda: go.step())[i]()
    copies.save(r.o.at[0], r.o_out)
    wo_load[0].wait()
    out_project(0)

    if layer == 0:
        gq[2].step()
        gq[0].step()
        gu.step()
        gq[1].step()
        gq[0].step()
        w_load.append(copies.start(other[0], wq.at[3]))
        go.step()
        gq[2].step()
        for g in nq:
            g.first()
        no.first()
    w_load[3].wait()
    project(3)
    if layer == 0:
        gq[1].step()
        w_load.append(copies.start(other[1], wq.at[4]))
        gu.step()
        gd.step()
    w_load[4].wait()
    project(4)
    if layer == 0:
        gq[2].step()
        w_load.append(copies.start(other[2], wq.at[5]))
        go.step()
    w_load[5].wait()
    project(5)
    if layer == 1:
        gu.step()
        gd.step()
    copies.save(qkv, r.qkv_out)
    for i in range(4):
        attend(1, i * quarter, (i + 1) * quarter)
        if layer == 0:
            if i == 0:
                go.step()
                wo_load[1] = copies.start(r.out_oth, r.wo.at[1])
                gu.step()
            if i == 1:
                gd.step()
            if i == 2:
                gu.step()
                wu_load[1] = copies.start(r.up_oth, r.wu.at[1])
                nq[0].step()
            if i == 3:
                gd.step()
        else:
            if i == 0:
                gu.step()
            if i == 1:
                gd.step()
            if i == 2:
                gu.step()
            if i == 3:
                gd.step()
    copies.save(r.lse, r.lse_out)
    wo_load[1].wait()
    out_project(1)
    if layer == 0:
        gd.step()
        wd_load[1] = copies.start(r.dn_oth, r.wd.at[1])
        nq[1].step()
    else:
        gu.step()
        wu_load[1] = copies.start(r.up_oth, r.wu.at[1])
        gd.step()
        wd_load[1] = copies.start(r.dn_oth, r.wd.at[1])

    norm(1, r.h2, r.xh2, r.r2)
    copies.save(r.h2, r.h2_out)
    copies.save(r.xh2, r.xh2_out)
    copies.save(r.r2, r.r2_out)
    if layer == 0:
        nq[2].step()
        nq[0].step()

    def up(group):
        def body(n, carry):
            at = rows_at(n, cols)
            r.u[...] = dot_nn(r.h2[...], r.wu[group, :, at])

            def inner(i, carry):
                i_at = rows_at(i, CHUNK)
                a, d = gelu_parts(r.u[i_at, :])
                r.a[group, i_at, at] = a.astype(BF16)
                r.d[group, i_at, at] = d.astype(BF16)
                return carry

            return lax.fori_loop(0, rows // CHUNK, inner, carry)

        lax.fori_loop(0, half // cols, body, 0)
        if group == 0:
            copies.save(r.a.at[0], r.a_out)
        copies.save(r.d.at[group], r.d_out.at[group])

    def down(group):
        def body(n, carry):
            at = rows_at(n, cols)
            x[:, at] += dot_nt(r.a[group], r.wd[group, at, :])
            return carry

        lax.fori_loop(0, pieces, body, 0)

    wu_load[0].wait()
    up(0)
    if layer == 0:
        no.step()
        nq[1].step()
        nq[0].step()
    wu_load[1].wait()
    up(1)
    if layer == 0:
        nq[2].step()
        no.step()
        nq[1].step()
        nq[0].step()
    wd_load[0].wait()
    down(0)
    if layer == 0:
        nq[2].step()
        no.step()
        nq[1].step()
    wd_load[1].wait()
    down(1)
    if layer == 0:
        copies.save(x, r.y_out)
        nq[2].step()
        no.step()
    else:
        copies.settle(h1_save)

        def body(i, carry):
            at = rows_at(i, CHUNK)
            r.h1[at, :] = x[at, :].astype(BF16)
            return carry

        lax.fori_loop(0, rows // CHUNK, body, 0)
        copies.save(r.h1, r.y_out)
    copies.finish()
    remote.finish()


def backward_kernel(layer, reduce, names, *args):
    r = SimpleNamespace(**dict(zip(names, args)))
    copies = Copies(r.sem)
    me, t = lax.axis_index("dp"), lax.axis_index("tensor")
    L, g, dh = r.L, r.g, r.dh
    rows, width = g.shape
    cols = r.qkv_own.shape[-1]
    heads = cols // HEAD_DIM
    half = r.up_own.shape[-1]
    pieces = width // cols

    if reduce:
        remote = Remote(r.send, r.recv)
        if layer == 1:
            greet([(flip(me, b), t) for b in (1, 2, 4, 8)])
        else:
            low = lax.rem(me, GROUP)
            greet([(me - low + lax.rem(low + o, GROUP), t) for o in range(1, GROUP)])
        s_dn = Scatter(remote, r.dn_g, [r.dn_r0, r.dn_r1, r.dn_r2, r.dn_r3])
        s_up = Scatter(remote, r.up_g, [r.up_r0, r.up_r1, r.up_r2, r.up_r3])
        s_out = Scatter(remote, r.out_g, [r.out_r0, r.out_r1, r.out_r2, r.out_r3])
        if layer == 0:
            s_qkv = Scatter(remote, r.qkv_g, [r.qkv_r0, r.qkv_r1, r.qkv_r2, r.qkv_r3])
            s_old = Scatter(remote, r.old_g, [None, r.old_r1, r.old_r2, r.old_r3], 1)
        else:
            s_qkv = Scatter(remote, r.qkv_g, [r.qkv_r0])

    g_load = copies.start(r.g_in, L.at[0] if layer == 1 else g)
    if reduce and layer == 0:
        old_load = copies.start(r.old_in, r.old_g)
    halves = [slice(i * cols, (i + 1) * cols) for i in range(pieces)]
    wd_load = [
        copies.start(r.dn_own.at[layer], L.at[3]),
        copies.start(r.dn_oth, L.at[4]),
    ]
    d_load = [copies.start(r.d.at[i], L.at[5 + i]) for i in range(2)]
    a_load = copies.start(r.a, L.at[7])
    h2_load = copies.start(r.h2, L.at[8])
    wu_load = [
        copies.start(r.up_own.at[layer], L.at[9]),
        copies.start(r.up_oth, L.at[10]),
    ]
    xh_load = copies.start(r.xh2, L.at[11])
    r2_load = copies.start(r.r2, r.spread)
    wo_load = [
        copies.start(r.out_own.at[layer], L.at[12, :, halves[0]]),
        copies.start(r.out_oth, L.at[12, :, halves[1]]),
    ]
    o_load = copies.start(r.o, L.at[13, :, halves[0]])
    mask_load = copies.start(r.bias, r.mask)
    lse_load = copies.start(r.lse, r.lse_v)

    def zero(i, carry):
        r.sums[i] = jnp.zeros((8, width), F32)
        return carry

    lax.fori_loop(0, 4, zero, 0)

    g_load.wait()

    def begin(i, carry):
        at = rows_at(i, CHUNK)
        if layer == 1:
            g[at, :] = L[0, at, :].astype(F32)
        else:
            L[0, at, :] = g[at, :].astype(BF16)
        return carry

    lax.fori_loop(0, rows // CHUNK, begin, 0)
    if reduce and layer == 0:
        old_load.wait()
        s_old.send()

    def du(group):
        def body(n, carry):
            at = rows_at(n, cols)
            da = dot_nn(L[0], L[3 + group, :, at])
            L[1 + group, :, at] = (da * L[5 + group, :, at].astype(F32)).astype(BF16)
            return carry

        lax.fori_loop(0, half // cols, body, 0)

    def weight_grad(lhs, rhs, out, at):
        full = dot_tn(lhs, rhs)
        size = width // GROUP
        for d in range(GROUP):
            pos = (d % 2) * 8 + (d // 2 % 2) * 4 + (d // 4 % 2) * 2 + d // 8
            out[pos, :, at] = full[d * size : (d + 1) * size].astype(BF16)

    for i in range(2):
        wd_load[i].wait()
        d_load[i].wait()
        du(i)
    qkv_load = [
        copies.start(r.qkv.at[j], L.at[3 + j // 2, :, halves[j % 2]]) for j in range(6)
    ]

    a_load.wait()

    def down_grad(n, carry):
        at = rows_at(n, cols)
        weight_grad(L[0], L[7, :, at], r.dn_g, at)
        return carry

    lax.fori_loop(0, half // cols, down_grad, 0)
    if reduce:
        s_dn.send()
    h2_load.wait()

    def up_grad(n, carry):
        at = rows_at(n, cols)
        weight_grad(L[8], L[1, :, at], r.up_g, at)
        return carry

    lax.fori_loop(0, half // cols, up_grad, 0)
    h1_load = copies.start(r.h1, L.at[8])
    if reduce:
        if layer == 0:
            s_old.step()
        s_dn.step()
        s_up.send()

    for i in range(2):
        wu_load[i].wait()

    def dh2(n, carry):
        at = rows_at(n, cols)
        dh[:, at] = dot_nt(L[1], L[9, at, :]) + dot_nt(L[2], L[10, at, :])
        return carry

    lax.fori_loop(0, pieces, dh2, 0)
    wq_load = [
        copies.start(
            r.qkv_own.at[layer, j] if j < 3 else r.qkv_oth.at[j - 3],
            L.at[9 + j // 2, :, halves[j % 2]],
        )
        for j in range(4)
    ]
    if reduce:
        s_up.step()

    def norm_back(which, spread):
        gain = r.gain[which : which + 1, :]

        def body(i, carry):
            at = rows_at(i, CHUNK)
            hat = L[11, at, :].astype(F32)
            grad = dh[at, :]
            rs = spread[at, 0:1]
            e = grad * gain
            prod = grad * hat
            m1 = jnp.mean(e, axis=-1, keepdims=True)
            m2 = jnp.mean(e * hat, axis=-1, keepdims=True)
            new = g[at, :] + rs * (e - m1 - hat * m2)
            g[at, :] = new
            L[0, at, :] = new.astype(BF16)
            r.sums[which] += jnp.sum(prod.reshape(CHUNK // 8, 8, width), axis=0)
            r.sums[2 + which] += jnp.sum(grad.reshape(CHUNK // 8, 8, width), axis=0)
            return carry

        lax.fori_loop(0, rows // CHUNK, body, 0)

    xh_load.wait()
    r2_load.wait()
    norm_back(1, r.spread)
    xh1_load = copies.start(r.xh1, L.at[11])
    r1_load = copies.start(r.r1, r.spread)

    for i in range(2):
        wo_load[i].wait()
        L[6, :, halves[i]] = dot_nn(L[0], L[12, :, halves[i]]).astype(BF16)
    wq_load += [
        copies.start(r.qkv_oth.at[j - 3], L.at[12, :, halves[j % 2]]) for j in range(4, 6)
    ]
    if reduce:
        if layer == 0:
            s_old.step()
        s_dn.step()
    o_load.wait()
    weight_grad(L[0], L[13, :, halves[0]], r.out_g, slice(0, cols))
    if reduce:
        s_out.send()

    place = [(3, 0), (3, 1), (4, 0), (4, 1), (5, 0), (5, 1)]
    to = [(1, 0), (1, 1), (2, 0), (2, 1), (7, 0), (7, 1)]

    def clear(i, carry):
        dh[rows_at(i, CHUNK), :] = jnp.zeros((CHUNK, width), F32)
        return carry

    def attend(group, start, stop):
        def part(j, at, head):
            slot, side = place[3 * group + j]
            begin_at = side * cols + head * HEAD_DIM
            return L[slot, at, begin_at : begin_at + HEAD_DIM]

        def body(i, carry):
            q_at = rows_at(i, TILE)
            k_at = pl.ds(pl.multiple_of(jnp.maximum(i - 1, 0) * TILE, TILE), 2 * TILE)
            mask = r.mask[q_at, :]
            kept = r.lse_v[group, q_at, :]
            for head in range(heads):
                q, k, v = part(0, q_at, head), part(1, k_at, head), part(2, k_at, head)
                at = group * cols + head * HEAD_DIM
                do = L[6, q_at, at : at + HEAD_DIM]
                s = dot_nt(q, k) * SCALE + mask
                p = jnp.exp(s - kept[:, head : head + 1])
                dp = dot_nt(do, v)
                inner = jnp.sum(dp * p, axis=-1, keepdims=True)
                ds = (p * (dp - inner)).astype(BF16)
                dq = dot_nn(ds, k) * SCALE
                slot, side = to[3 * group]
                at = side * cols + head * HEAD_DIM
                L[slot, q_at, at : at + HEAD_DIM] = dq.astype(BF16)
                at = head * HEAD_DIM
                dh[k_at, at : at + HEAD_DIM] += dot_tn(ds, q)
                at = cols + head * HEAD_DIM
                dh[k_at, at : at + HEAD_DIM] += dot_tn(p.astype(BF16), do)
            return carry

        lax.fori_loop(start, stop, body, 0)

    def settle(group):
        def body(i, carry):
            at = rows_at(i, CHUNK)
            slot, side = to[3 * group + 1]
            L[slot, at, halves[side]] = (dh[at, halves[0]] * SCALE).astype(BF16)
            slot, side = to[3 * group + 2]
            L[slot, at, halves[side]] = dh[at, halves[1]].astype(BF16)
            return carry

        lax.fori_loop(0, rows // CHUNK, body, 0)

    for load in (*qkv_load, mask_load, lse_load):
        load.wait()
    tiles = rows // TILE
    mid = tiles // 2
    lax.fori_loop(0, rows // CHUNK, clear, 0)
    attend(0, 0, mid)
    if reduce:
        s_up.step()
        s_out.step()
    attend(0, mid, tiles)
    settle(0)
    h1_load.wait()
    for j in range(3):
        slot, side = to[j]
        weight_grad(L[8], L[slot, :, halves[side]], r.qkv_g, slice(j * cols, (j + 1) * cols))
    if reduce:
        s_qkv.send()
        s_dn.step()
        if layer == 0:
            finish_old = s_old.last()
            for j in range(3):
                r.old_f[j] = finish_old[:, j * cols : (j + 1) * cols]
            copies.save(r.old_f, r.old_out)

    lax.fori_loop(0, rows // CHUNK, clear, 0)
    attend(1, 0, mid)
    if reduce:
        s_out.step()
        if layer == 0:
            s_qkv.step()
        else:
            s_qkv.add()
            copies.save(r.qkv_g.at[pl.ds(s_qkv.base, 8)], r.qkv_out)
        s_up.step()
        r.dn_f[...] = s_dn.last()
        copies.save(r.dn_f, r.dn_out)
    attend(1, mid, tiles)
    settle(1)
    if reduce:
        s_out.step()
    for load in wq_load:
        load.wait()

    def dh1(n, carry):
        at = rows_at(n, cols)
        dh[:, at] = (
            dot_nt(L[1], L[9, at, :]) + dot_nt(L[2], L[10, at, :]) + dot_nt(L[7], L[12, at, :])
        )
        return carry

    lax.fori_loop(0, pieces, dh1, 0)
    if reduce:
        if layer == 0:
            s_qkv.step()
        r.up_f[...] = s_up.last()
        copies.save(r.up_f, r.up_out)
    xh1_load.wait()
    r1_load.wait()
    norm_back(0, r.spread)
    copies.save(g, r.g_out)
    for k in range(4):
        r.flat[k : k + 1, :] = jnp.sum(r.sums[k], axis=0, keepdims=True)
    if not reduce:
        copies.save(r.dn_g, r.dn_out)
        copies.save(r.up_g, r.up_out)
        copies.save(r.out_g, r.out_out)
        copies.save(r.qkv_g, r.qkv_out)
        copies.save(r.flat, r.flat_out)
        copies.finish()
        return
    r.out_f[...] = s_out.last()
    copies.save(r.out_f, r.out_out)
    if layer == 1:
        copies.save(r.flat, r.flat_out)
    else:
        r.both[0:4, :] = r.flat[...]
        r.both[4:8, :] = r.flat_in[...]
        sends = []
        for o in range(1, GROUP):
            to_dev = lax.rem(low + o, GROUP)
            sends.append(
                remote.start(
                    r.both.at[:, rows_at(to_dev // 2, 128)],
                    r.slots.at[o],
                    (me - low + to_dev, t),
                )
            )
        s_qkv.step()
        total = r.both[:, rows_at(low // 2, 128)]
        for o, copy in enumerate(sends):
            copy.wait_recv()
            total = total + r.slots[o + 1]
        r.flat_f[...] = total
        copies.save(r.flat_f, r.flat_out)
        done = s_qkv.last()
        for j in range(3):
            r.qkv_f[j] = done[:, j * cols : (j + 1) * cols]
        copies.save(r.qkv_f, r.qkv_out)
    copies.finish()
    remote.finish()


def call(kernel, ins, outs, scratch, name, collective, flops):
    split = lambda v: v if isinstance(v, tuple) else (v, ANY)
    in_items = {k: split(v) for k, v in ins.items()}
    out_items = {k: split(v) for k, v in outs.items()}
    names = (*in_items, *out_items, *scratch)
    params = dict(vmem_limit_bytes=VMEM_LIMIT, has_side_effects=True)
    if collective is not None:
        params.update(collective_id=collective)
    made = pl.pallas_call(
        functools.partial(kernel, names),
        out_shape=tuple(v for v, _ in out_items.values()),
        in_specs=[pl.BlockSpec(memory_space=s) for _, s in in_items.values()],
        out_specs=tuple(pl.BlockSpec(memory_space=s) for _, s in out_items.values()),
        scratch_shapes=list(scratch.values()),
        compiler_params=pltpu.CompilerParams(**params),
        cost_estimate=pl.CostEstimate(flops=flops, bytes_accessed=60 << 20, transcendentals=0),
        name=name,
    )(*(v for v, _ in in_items.values()))
    return SimpleNamespace(**dict(zip(out_items, made)))


def forward(layer, x, bias, gain, shift, weights, other):
    rows, width = x.shape
    w_qkv, w_out, w_up, w_dn = weights
    cols, half = w_qkv.shape[-1], w_up.shape[-1]
    shape = jax.ShapeDtypeStruct
    wide, slab = (rows, width), (rows, cols)
    ins = dict(
        x_in=x, bias=bias, gain=(gain, VMEM), shift=(shift, VMEM),
        qkv_own=w_qkv, out_own=w_out, up_own=w_up, dn_own=w_dn,
    )
    outs = {}
    qkv_s, out_s = shape(w_qkv.shape[1:], BF16), shape(w_out.shape[1:], BF16)
    up_s, dn_s = shape(w_up.shape[1:], BF16), shape(w_dn.shape[1:], BF16)
    if layer == 0:
        outs.update(qkv_oth=qkv_s, out_oth=out_s, qkv_nxt=qkv_s, out_nxt=out_s)
    else:
        ins.update(qkv_oth=other.qkv_nxt, out_oth=other.out_nxt)
    outs.update(
        up_oth=up_s, dn_oth=dn_s,
        h1_out=shape(wide, BF16), xh1_out=shape(wide, BF16), r1_out=shape((rows, 128), F32),
        qkv_out=shape((6, *slab), BF16), lse_out=shape((2, rows, 128), F32), o_out=shape(slab, BF16),
        h2_out=shape(wide, BF16), xh2_out=shape(wide, BF16), r2_out=shape((rows, 128), F32),
        a_out=shape((rows, half), BF16), d_out=shape((2, rows, half), BF16),
        y_out=shape(wide, F32 if layer == 0 else BF16),
    )
    copies = 128 if layer == 0 else 16
    scratch = dict(
        x=VMEM(wide, F32), h1=VMEM(wide, BF16), xh1=VMEM(wide, BF16), r1=VMEM((rows, 128), F32),
        h2=VMEM(wide, BF16), xh2=VMEM(wide, BF16), r2=VMEM((rows, 128), F32),
        qkv=VMEM((6, *slab), BF16), o=VMEM((2, *slab), BF16), lse=VMEM((2, rows, 128), F32),
        mask=VMEM((rows, 128), F32), u=VMEM(slab, F32),
        a=VMEM((2, rows, half), BF16), d=VMEM((2, rows, half), BF16),
        wq=VMEM((6, width, cols), BF16), wo=VMEM((2, width, cols), BF16),
        wu=VMEM((2, width, half), BF16), wd=VMEM((2, width, half), BF16),
        sem=pltpu.SemaphoreType.DMA((40,)),
        send=pltpu.SemaphoreType.DMA((copies,)), recv=pltpu.SemaphoreType.DMA((copies,)),
    )
    if layer == 0:
        scratch.update(x_raw=VMEM(wide, BF16))
    flops = 2 * rows * (6 * cols * width + 2 * cols * width + 4 * half * width)
    return call(
        functools.partial(forward_kernel, layer), ins, outs, scratch, "forward", layer, flops
    )


def backward(layer, reduce, g, bias, gain, weights, other, kept, before):
    rows, width = g.shape
    w_qkv, w_out, w_up, w_dn = weights
    cols, half = w_qkv.shape[-1], w_up.shape[-1]
    shape = jax.ShapeDtypeStruct
    wide = (rows, width)
    block = width // GROUP
    ins = dict(
        g_in=g, bias=bias, gain=(gain, VMEM),
        qkv_own=w_qkv, out_own=w_out, up_own=w_up, dn_own=w_dn,
        qkv_oth=other.qkv, out_oth=other.out, up_oth=other.up, dn_oth=other.dn,
    )
    ins.update(
        h1=kept.h1_out, xh1=kept.xh1_out, r1=kept.r1_out, qkv=kept.qkv_out, lse=kept.lse_out, o=kept.o_out,
        h2=kept.h2_out, xh2=kept.xh2_out, r2=kept.r2_out, a=kept.a_out, d=kept.d_out,
    )
    outs = dict(g_out=shape(wide, F32))
    grad = lambda n: VMEM((GROUP, block, n), BF16)
    recv = lambda k, n: VMEM((GROUP >> (k + 1), block, n), BF16)
    done = lambda n: VMEM((block, n), F32)
    all3 = 3 * cols
    scratch = dict(
        L=VMEM((14, *wide), BF16), g=VMEM(wide, F32), dh=VMEM(wide, F32),
        mask=VMEM((rows, 128), F32), lse_v=VMEM((2, rows, 128), F32), spread=VMEM((rows, 128), F32),
        sums=VMEM((4, 8, width), F32), flat=VMEM((4, width), F32),
        sem=pltpu.SemaphoreType.DMA((56,)),
        dn_g=grad(half), up_g=grad(half), out_g=grad(cols), qkv_g=grad(all3),
    )
    if not reduce:
        full = lambda n: shape((GROUP, block, n), BF16)
        outs.update(dn_out=full(half), up_out=full(half), out_out=full(cols), qkv_out=full(all3))
        outs.update(flat_out=shape((4, width), F32))
    else:
        copies = 4 * 4 + 3 + GROUP
        part = lambda n: shape((block, n), F32)
        outs.update(dn_out=part(half), up_out=part(half), out_out=part(cols))
        scratch.update(
            send=pltpu.SemaphoreType.DMA((copies,)), recv=pltpu.SemaphoreType.DMA((copies,)),
            dn_f=done(half), up_f=done(half), out_f=done(cols), qkv_r0=recv(0, all3),
            dn_r0=recv(0, half), dn_r1=recv(1, half), dn_r2=recv(2, half), dn_r3=recv(3, half),
            up_r0=recv(0, half), up_r1=recv(1, half), up_r2=recv(2, half), up_r3=recv(3, half),
            out_r0=recv(0, cols), out_r1=recv(1, cols), out_r2=recv(2, cols), out_r3=recv(3, cols),
        )
        if layer == 1:
            outs.update(flat_out=shape((4, width), F32), qkv_out=shape((8, block, all3), BF16))
        else:
            three = shape((3, block, cols), F32)
            outs.update(flat_out=shape((8, 128), F32), qkv_out=three, old_out=three)
            ins.update(old_in=before.qkv_out, flat_in=(before.flat_out, VMEM))
            scratch.update(
                qkv_r1=recv(1, all3), qkv_r2=recv(2, all3), qkv_r3=recv(3, all3),
                old_g=VMEM((8, block, all3), BF16),
                old_r1=recv(1, all3), old_r2=recv(2, all3), old_r3=recv(3, all3),
                old_f=VMEM((3, block, cols), F32), qkv_f=VMEM((3, block, cols), F32),
                both=VMEM((8, width), F32), slots=VMEM((GROUP, 8, 128), F32), flat_f=VMEM((8, 128), F32),
            )
    flops = 2 * rows * (2 * 6 * cols * width + 3 * cols * width + 6 * half * width)
    return call(
        functools.partial(backward_kernel, layer, reduce), ins, outs, scratch,
        "backward", 2 + layer if reduce else None, flops,
    )


def local(n_dp, tokens, lengths, w_qkv, w_out, w_up, w_down, norm_gain, norm_bias, cotangent):
    rows, width = tokens.shape
    cols = w_qkv.shape[3]
    items = lengths.shape[1]
    order = jnp.arange(items, dtype=jnp.int32)
    ends = jnp.sum(jnp.where(order[:, None] >= order[None, :], lengths, 0), axis=1)
    place = jnp.arange(rows, dtype=jnp.int32)
    start = jnp.max(jnp.where(ends[None, :] <= place[:, None], ends[None, :], 0), axis=1)
    window = jnp.maximum(place // TILE - 1, 0) * TILE
    key = window[:, None] + jnp.arange(2 * TILE, dtype=jnp.int32)[None, :]
    allowed = (key >= start[:, None]) & (key <= place[:, None])
    bias = jnp.where(allowed, 0.0, MASKED).astype(F32)

    weights = (jnp.transpose(w_qkv, (0, 2, 1, 3)), w_out, w_up, w_down)
    f0 = forward(0, tokens, bias, norm_gain[0], norm_bias[0], weights, None)
    f1 = forward(1, f0.y_out, bias, norm_gain[1], norm_bias[1], weights, f0)
    output = f1.y_out
    reduce = n_dp == GROUP
    oth0 = SimpleNamespace(qkv=f0.qkv_oth, out=f0.out_oth, up=f0.up_oth, dn=f0.dn_oth)
    oth1 = SimpleNamespace(qkv=f0.qkv_nxt, out=f0.out_nxt, up=f1.up_oth, dn=f1.dn_oth)
    b1 = backward(1, reduce, cotangent, bias, norm_gain[1], weights, oth1, f1, None)
    b0 = backward(0, reduce, b1.g_out, bias, norm_gain[0], weights, oth0, f0, b1)
    grad = b0.g_out
    out, up, dn = (
        jnp.stack(v)
        for v in ((b0.out_out, b1.out_out), (b0.up_out, b1.up_out), (b0.dn_out, b1.dn_out))
    )
    if reduce:
        qkv = jnp.transpose(jnp.stack([b0.qkv_out, b0.old_out]), (0, 2, 1, 3))
        side = lax.rem(lax.axis_index("dp"), 2)
        block = width // GROUP
        flat = b0.flat_out.reshape(2, 4, 128)
        flat = lax.dynamic_slice_in_dim(flat, side * block, block, axis=2)
    else:

        def total(both):
            n = both.shape[-1]
            both = both.astype(F32).reshape(2, 2, 2, 2, 2, width // GROUP, n)
            both = jnp.transpose(both, (0, 4, 3, 2, 1, 5, 6)).reshape(2, width, n)
            return lax.psum_scatter(both, "dp", scatter_dimension=1, tiled=True)

        out, up, dn = total(out), total(up), total(dn)
        qkv = total(jnp.stack([b0.qkv_out, b1.qkv_out]))
        qkv = qkv.reshape(*qkv.shape[:2], 3, cols)
        flat = jnp.stack([b0.flat_out, b1.flat_out])
        flat = lax.psum_scatter(flat, "dp", scatter_dimension=2, tiled=True)
    gain, shift = flat[:, :2], flat[:, 2:]
    return (output, grad, qkv, out, up, dn, gain, shift)


def solution(mesh):
    placed = (
        P("dp", None),
        P("dp", None),
        P(None, None, None, "tensor"),
        P(None, None, "tensor"),
        P(None, None, "tensor"),
        P(None, None, "tensor"),
        P(),
        P(),
        P("dp", None),
    )
    return jax.shard_map(
        functools.partial(local, mesh.shape["dp"]),
        mesh=mesh,
        in_specs=placed,
        out_specs=(
            P("dp", None),
            P("dp", None),
            P(None, "dp", None, "tensor"),
            P(None, "dp", "tensor"),
            P(None, "dp", "tensor"),
            P(None, "dp", "tensor"),
            P(None, None, "dp"),
            P(None, None, "dp"),
        ),
        check_vma=False,
    )
```

```python
import functools
from types import SimpleNamespace

import jax
import jax.numpy as jnp
from jax import lax
from jax.experimental import pallas as pl
from jax.experimental.pallas import tpu as pltpu
from jax.sharding import PartitionSpec as P

HEAD_DIM = 128
TILE = 64
EPS = 1e-05
MASKED = -1e30
MESH = pl.DeviceIdType.MESH
VMEM = pltpu.VMEM
ANY = pl.ANY
F32 = jnp.float32
BF16 = jnp.bfloat16
SCALE = HEAD_DIM**-0.5
VMEM_LIMIT = 62 << 20
SLOT = "L"
GROUP = 16
CHUNK = 256

ERFC = (
    0.22567586600780487,
    0.22566960752010345,
    0.20784251391887665,
    0.16854380071163177,
    0.14142295718193054,
    -0.005586510524153709,
    0.1690569967031479,
    -0.18288171291351318,
    0.05025661736726761,
)


def dot_nn(a, b):
    return lax.dot_general(a, b, (((1,), (0,)), ((), ())), preferred_element_type=F32)


def dot_nt(a, b):
    return lax.dot_general(a, b, (((1,), (1,)), ((), ())), preferred_element_type=F32)


def dot_tn(a, b):
    return lax.dot_general(a, b, (((0,), (0,)), ((), ())), preferred_element_type=F32)


def rows_at(index, size):
    return pl.ds(pl.multiple_of(index * size, size), size)


def own_rows(step):
    return slice(step * TILE, (step + 1) * TILE)


def key_rows(step):
    first = max(step - 1, 0) * TILE
    return slice(first, first + 2 * TILE)


def flip(value, bit):
    return value + bit * (1 - 2 * lax.rem(value // bit, 2))


def normalize(x):
    center = x - jnp.mean(x, axis=-1, keepdims=True)
    spread = lax.rsqrt(jnp.mean(center * center, axis=-1, keepdims=True) + EPS)
    return center * spread, spread


def gelu_parts(u):
    t = 1.0 / (1.0 + (0.4 * 0.7071067811865476) * jnp.abs(u))
    q = jnp.full_like(t, ERFC[-1])
    for c in ERFC[-2::-1]:
        q = q * t + c
    e = jnp.exp(-0.5 * (u * u))
    tail = 0.5 * (t * q) * e
    cdf = jnp.where(u >= 0, 1.0 - tail, tail)
    return u * cdf, cdf + u * (e * 0.3989422804014327)


class Copies:
    def __init__(self, sems):
        self.sems, self.n, self.open = sems, 0, []

    def start(self, src, dst):
        assert self.n < self.sems.shape[0]
        copy = pltpu.make_async_copy(src, dst, self.sems.at[self.n])
        self.n += 1
        copy.start()
        return copy

    def save(self, src, dst):
        self.open.append(self.start(src, dst))
        return self.open[-1]

    def settle(self, copy):
        self.open.remove(copy)
        copy.wait()

    def finish(self):
        for copy in self.open:
            copy.wait()


class Remote:
    def __init__(self, send, recv):
        self.send, self.recv, self.n, self.sent = send, recv, 0, []

    def start(self, src, dst, device):
        assert self.n < self.send.shape[0]
        copy = pltpu.make_async_remote_copy(
            src_ref=src,
            dst_ref=dst,
            send_sem=self.send.at[self.n],
            recv_sem=self.recv.at[self.n],
            device_id=device,
            device_id_type=MESH,
        )
        self.n += 1
        copy.start()
        self.sent.append(copy)
        return copy

    def finish(self):
        for copy in self.sent:
            copy.wait_send()


def greet(devices):
    barrier = pltpu.get_barrier_semaphore()
    for device in devices:
        pl.semaphore_signal(barrier, inc=1, device_id=device, device_id_type=MESH)
    pl.semaphore_wait(barrier, len(devices))


class Gather:
    def __init__(self, remote, own, other, order):
        self.remote, self.own, self.other, self.order = remote, own, other, order
        me, t = lax.axis_index("dp"), lax.axis_index("tensor")
        self.me, self.t = me, t
        self.have = [lax.rem(me, 8)]
        self.stage = 0
        self.flying = []

    def block(self, ref, index):
        size = ref.shape[0] // 8
        return ref.at[rows_at(index, size), :]

    def first(self):
        b = self.have[0]
        self.flying = [
            self.remote.start(
                self.block(self.own, b), self.block(self.other, b), (self.me, 1 - self.t)
            )
        ]

    def step(self):
        for copy in self.flying:
            copy.wait_recv()
        if self.stage == 3:
            return
        if self.stage > 0:
            bit = self.order[self.stage - 1]
            self.have = self.have + [flip(b, bit) for b in self.have]
        bit = self.order[self.stage]
        self.stage += 1
        device = (flip(self.me, bit), self.t)
        self.flying = [
            self.remote.start(self.block(self.other, b), self.block(self.other, b), device)
            for b in self.have
        ]


class Scatter:
    BITS = (1, 2, 4, 8)

    def __init__(self, remote, grad, recvs, stage=0):
        self.remote, self.grad, self.recvs, self.stage = remote, grad, recvs, stage
        self.me, self.t = lax.axis_index("dp"), lax.axis_index("tensor")
        self.base = 0
        self.count = 16 >> stage

    def send(self):
        bit = self.BITS[self.stage]
        mine = lax.rem(self.me // bit, 2)
        half = self.count // 2
        out = self.base + (1 - mine) * half
        self.base = self.base + mine * half
        self.count = half
        self.flying = self.remote.start(
            self.grad.at[pl.ds(out, half)],
            self.recvs[self.stage],
            (flip(self.me, bit), self.t),
        )

    def add(self):
        self.flying.wait_recv()
        recv = self.recvs[self.stage]
        self.stage += 1

        def body(i, carry):
            at = self.base + i
            self.grad[at] = (self.grad[at].astype(F32) + recv[i].astype(F32)).astype(BF16)
            return carry

        lax.fori_loop(0, self.count, body, 0)

    def step(self):
        self.add()
        self.send()

    def last(self):
        self.flying.wait_recv()
        return self.grad[self.base].astype(F32) + self.recvs[self.stage][0].astype(F32)


def forward_kernel(layer, names, *args):
    r = SimpleNamespace(**dict(zip(names, args)))
    copies = Copies(r.sem)
    remote = Remote(r.send, r.recv)
    me, t = lax.axis_index("dp"), lax.axis_index("tensor")
    rows, width = r.x.shape
    cols = r.qkv_own.shape[-1]
    heads = cols // HEAD_DIM
    half = r.up_own.shape[-1]
    pieces = width // cols

    x_load = copies.start(r.x_in, r.x_raw if layer == 0 else r.x)
    greet([(me, 1 - t), (flip(me, 2), t), (flip(me, 4), t), (flip(me, 1), t)])

    own = [r.qkv_own.at[layer, j] for j in range(3)]
    one, two = (2, 4, 1), (4, 2, 1)
    if layer == 0:
        other = [r.qkv_oth.at[j] for j in range(3)]
        gq = [Gather(remote, own[j], other[j], two if j == 1 else one) for j in range(3)]
        go = Gather(remote, r.out_own.at[0], r.out_oth, two)
        gu = Gather(remote, r.up_own.at[0], r.up_oth, one)
        gd = Gather(remote, r.dn_own.at[0], r.dn_oth, two)
        nq = [
            Gather(remote, r.qkv_own.at[1, j], r.qkv_nxt.at[j], one if j == 1 else two)
            for j in range(3)
        ]
        no = Gather(remote, r.out_own.at[1], r.out_nxt, one)
        for g in (*gq, go, gu, gd):
            g.first()
    else:
        gu = Gather(remote, r.up_own.at[1], r.up_oth, one)
        gd = Gather(remote, r.dn_own.at[1], r.dn_oth, two)
        gu.first()
        gd.first()

    w_load = [copies.start(own[j], r.wq.at[j]) for j in range(3)]
    bias_load = copies.start(r.bias, r.mask)
    wo_load = [copies.start(r.out_own.at[layer], r.wo.at[0]), None]
    wu_load = [copies.start(r.up_own.at[layer], r.wu.at[0]), None]
    wd_load = [copies.start(r.dn_own.at[layer], r.wd.at[0]), None]
    if layer == 1:
        w_load += [copies.start(r.qkv_oth.at[j], r.wq.at[3 + j]) for j in range(3)]
        wo_load[1] = copies.start(r.out_oth, r.wo.at[1])

    x = r.x

    def norm(which, h, xh, spread, source=None):
        gain = r.gain[which : which + 1, :]
        shift = r.shift[which : which + 1, :]

        def body(i, carry):
            at = rows_at(i, CHUNK)
            if source is not None:
                values = source[at, :].astype(F32)
                x[at, :] = values
            else:
                values = x[at, :]
            hat, rs = normalize(values)
            xh[at, :] = hat.astype(BF16)
            h[at, :] = (hat * gain + shift).astype(BF16)
            spread[at, :] = jnp.broadcast_to(rs, (CHUNK, HEAD_DIM))
            return carry

        lax.fori_loop(0, rows // CHUNK, body, 0)

    x_load.wait()
    norm(0, r.h1, r.xh1, r.r1, r.x_raw if layer == 0 else None)
    h1_save = copies.save(r.h1, r.h1_out)
    copies.save(r.xh1, r.xh1_out)
    copies.save(r.r1, r.r1_out)

    qkv, wq = r.qkv, r.wq

    def project(j):
        qkv[j] = dot_nn(r.h1[...], wq[j]).astype(BF16)

    def attend(group, start, stop):
        q_ref, k_ref, v_ref = (qkv.at[3 * group + j] for j in range(3))
        steps = range(rows // TILE)

        def body(head, carry):
            c = rows_at(head, HEAD_DIM)
            s = [
                dot_nt(q_ref[own_rows(i), c], k_ref[key_rows(i), c]) * SCALE + r.mask[own_rows(i), :]
                for i in steps
            ]
            top = [jnp.max(v, axis=-1, keepdims=True) for v in s]
            e = [jnp.exp(v - m) for v, m in zip(s, top)]
            total = [jnp.sum(v, axis=-1, keepdims=True) for v in e]
            p = [(v * (1.0 / m)).astype(BF16) for v, m in zip(e, total)]
            mixed = [dot_nn(v, v_ref[key_rows(i), c]) for v, i in zip(p, steps)]
            for i in steps:
                r.p[group, own_rows(i), c] = p[i]
                r.o[group, own_rows(i), c] = mixed[i].astype(BF16)
            return carry

        lax.fori_loop(start, stop, body, 0)

    def out_project(group):
        def body(n, carry):
            at = rows_at(n, cols)
            x[:, at] += dot_nt(r.o[group], r.wo[group, at, :])
            return carry

        lax.fori_loop(0, pieces, body, 0)

    for j in range(3):
        w_load[j].wait()
        project(j)
        if layer == 0:
            if j == 0:
                gq[0].step()
            if j == 2:
                gq[1].step()
    bias_load.wait()
    for i in range(4):
        attend(0, i, i + 1)
        if layer == 0:
            (lambda: gq[0].step(), lambda: gq[2].step(), lambda: gq[1].step(), lambda: go.step())[i]()
    copies.save(r.o.at[0], r.o_out)
    wo_load[0].wait()
    out_project(0)

    if layer == 0:
        gq[2].step()
        gq[0].step()
        gu.step()
        gq[1].step()
        gq[0].step()
        w_load.append(copies.start(other[0], wq.at[3]))
        go.step()
        gq[2].step()
        for g in nq:
            g.first()
        no.first()
    w_load[3].wait()
    project(3)
    if layer == 0:
        gq[1].step()
        w_load.append(copies.start(other[1], wq.at[4]))
        gu.step()
        gd.step()
    w_load[4].wait()
    project(4)
    if layer == 0:
        gq[2].step()
        w_load.append(copies.start(other[2], wq.at[5]))
        go.step()
    w_load[5].wait()
    project(5)
    if layer == 1:
        gu.step()
        gd.step()
    copies.save(qkv, r.qkv_out)
    for i in range(4):
        attend(1, i, i + 1)
        if layer == 0:
            if i == 0:
                go.step()
                wo_load[1] = copies.start(r.out_oth, r.wo.at[1])
                gu.step()
            if i == 1:
                gd.step()
            if i == 2:
                gu.step()
                wu_load[1] = copies.start(r.up_oth, r.wu.at[1])
                nq[0].step()
            if i == 3:
                gd.step()
        else:
            if i == 0:
                gu.step()
            if i == 1:
                gd.step()
            if i == 2:
                gu.step()
            if i == 3:
                gd.step()
    copies.save(r.p, r.p_out)
    wo_load[1].wait()
    out_project(1)
    if layer == 0:
        gd.step()
        wd_load[1] = copies.start(r.dn_oth, r.wd.at[1])
        nq[1].step()
    else:
        gu.step()
        wu_load[1] = copies.start(r.up_oth, r.wu.at[1])
        gd.step()
        wd_load[1] = copies.start(r.dn_oth, r.wd.at[1])

    norm(1, r.h2, r.xh2, r.r2)
    copies.save(r.h2, r.h2_out)
    copies.save(r.xh2, r.xh2_out)
    copies.save(r.r2, r.r2_out)
    if layer == 0:
        nq[2].step()
        nq[0].step()

    def up(group):
        def body(n, carry):
            at = rows_at(n, cols)
            r.u[...] = dot_nn(r.h2[...], r.wu[group, :, at])

            def inner(i, carry):
                i_at = rows_at(i, CHUNK // 2)
                a, d = gelu_parts(r.u[i_at, :])
                r.a[group, i_at, at] = a.astype(BF16)
                r.d[group, i_at, at] = d.astype(BF16)
                return carry

            return lax.fori_loop(0, 2 * rows // CHUNK, inner, carry)

        lax.fori_loop(0, half // cols, body, 0)
        if group == 0:
            copies.save(r.a.at[0], r.a_out)
        copies.save(r.d.at[group], r.d_out.at[group])

    def down(group):
        def body(n, carry):
            at = rows_at(n, cols)
            x[:, at] += dot_nt(r.a[group], r.wd[group, at, :])
            return carry

        lax.fori_loop(0, pieces, body, 0)

    wu_load[0].wait()
    up(0)
    if layer == 0:
        no.step()
        nq[1].step()
        nq[0].step()
    wu_load[1].wait()
    up(1)
    if layer == 0:
        nq[2].step()
        no.step()
        nq[1].step()
        nq[0].step()
    wd_load[0].wait()
    down(0)
    if layer == 0:
        nq[2].step()
        no.step()
        nq[1].step()
    wd_load[1].wait()
    down(1)
    if layer == 0:
        copies.save(x, r.y_out)
        nq[2].step()
        no.step()
    else:
        copies.settle(h1_save)

        def body(i, carry):
            at = rows_at(i, CHUNK)
            r.h1[at, :] = x[at, :].astype(BF16)
            return carry

        lax.fori_loop(0, rows // CHUNK, body, 0)
        copies.save(r.h1, r.y_out)
    copies.finish()
    remote.finish()


def backward_kernel(layer, reduce, names, *args):
    r = SimpleNamespace(**dict(zip(names, args)))
    copies = Copies(r.sem)
    me, t = lax.axis_index("dp"), lax.axis_index("tensor")
    g, dh = r.g, r.dh
    L = [v for k, v in zip(names, args) if k[0] == SLOT]
    rows, width = g.shape
    cols = r.qkv_own.shape[-1]
    heads = cols // HEAD_DIM
    half = r.up_own.shape[-1]
    pieces = width // cols

    if reduce:
        remote = Remote(r.send, r.recv)
        if layer == 1:
            greet([(flip(me, b), t) for b in (1, 2, 4, 8)])
        else:
            low = lax.rem(me, GROUP)
            greet([(me - low + lax.rem(low + o, GROUP), t) for o in range(1, GROUP)])
        s_dn = Scatter(remote, r.dn_g, [r.dn_r0, r.dn_r1, r.dn_r2, r.dn_r3])
        s_up = Scatter(remote, r.up_g, [r.up_r0, r.up_r1, r.up_r2, r.up_r3])
        s_out = Scatter(remote, r.out_g, [r.out_r0, r.out_r1, r.out_r2, r.out_r3])
        if layer == 0:
            s_qkv = Scatter(remote, r.qkv_g, [r.qkv_r0, r.qkv_r1, r.qkv_r2, r.qkv_r3])
            s_old = Scatter(remote, r.old_g, [None, r.old_r1, r.old_r2, r.old_r3], 1)
        else:
            s_qkv = Scatter(remote, r.qkv_g, [r.qkv_r0])

    g_load = copies.start(r.g_in, L[0] if layer == 1 else g)
    if reduce and layer == 0:
        old_load = copies.start(r.old_in, r.old_g)
    halves = [slice(i * cols, (i + 1) * cols) for i in range(pieces)]
    wd_load = [
        copies.start(r.dn_own.at[layer], L[3]),
        copies.start(r.dn_oth, L[4]),
    ]
    d_load = [copies.start(r.d.at[i], L[5 + i]) for i in range(2)]
    a_load = copies.start(r.a, L[7])
    h2_load = copies.start(r.h2, L[8])
    wu_load = [
        copies.start(r.up_own.at[layer], L[9]),
        copies.start(r.up_oth, L[10]),
    ]
    xh_load = copies.start(r.xh2, L[11])
    r2_load = copies.start(r.r2, r.spread)
    wo_load = [
        copies.start(r.out_own.at[layer], L[12].at[:, halves[0]]),
        copies.start(r.out_oth, L[12].at[:, halves[1]]),
    ]
    o_load = copies.start(r.o, L[13].at[:, halves[0]])
    p_load = [copies.start(r.p.at[i], L[14].at[:, halves[i]]) for i in range(2)]

    def zero(i, carry):
        r.sums[i] = jnp.zeros((8, width), F32)
        return carry

    lax.fori_loop(0, 4, zero, 0)

    g_load.wait()

    def begin(i, carry):
        at = rows_at(i, CHUNK)
        if layer == 1:
            g[at, :] = L[0][at, :].astype(F32)
        else:
            L[0][at, :] = g[at, :].astype(BF16)
        return carry

    lax.fori_loop(0, rows // CHUNK, begin, 0)
    if reduce and layer == 0:
        old_load.wait()
        s_old.send()

    def du(group):
        def body(n, carry):
            at = rows_at(n, cols)
            da = dot_nn(L[0][...], L[3 + group][:, at])
            L[1 + group][:, at] = (da * L[5 + group][:, at].astype(F32)).astype(BF16)
            return carry

        lax.fori_loop(0, half // cols, body, 0)

    def weight_grad(lhs, rhs, out, at):
        full = dot_tn(lhs, rhs)
        size = width // GROUP
        for d in range(GROUP):
            pos = (d % 2) * 8 + (d // 2 % 2) * 4 + (d // 4 % 2) * 2 + d // 8
            out[pos, :, at] = full[d * size : (d + 1) * size].astype(BF16)

    for i in range(2):
        wd_load[i].wait()
        d_load[i].wait()
        du(i)
    qkv_load = [
        copies.start(r.qkv.at[j], L[3 + j // 2].at[:, halves[j % 2]]) for j in range(6)
    ]

    a_load.wait()

    def down_grad(n, carry):
        at = rows_at(n, cols)
        weight_grad(L[0][...], L[7][:, at], r.dn_g, at)
        return carry

    lax.fori_loop(0, half // cols, down_grad, 0)
    if reduce:
        s_dn.send()
    h2_load.wait()

    def up_grad(n, carry):
        at = rows_at(n, cols)
        weight_grad(L[8][...], L[1][:, at], r.up_g, at)
        return carry

    lax.fori_loop(0, half // cols, up_grad, 0)
    h1_load = copies.start(r.h1, L[8])
    if reduce:
        if layer == 0:
            s_old.step()
        s_dn.step()
        s_up.send()

    for i in range(2):
        wu_load[i].wait()

    def dh2(n, carry):
        at = rows_at(n, cols)
        dh[:, at] = dot_nt(L[1][...], L[9][at, :]) + dot_nt(L[2][...], L[10][at, :])
        return carry

    lax.fori_loop(0, pieces, dh2, 0)
    wq_load = [
        copies.start(
            r.qkv_own.at[layer, j] if j < 3 else r.qkv_oth.at[j - 3],
            L[9 + j // 2].at[:, halves[j % 2]],
        )
        for j in range(4)
    ]
    if reduce:
        s_up.step()

    def norm_back(which, spread):
        gain = r.gain[which : which + 1, :]

        def body(i, carry):
            at = rows_at(i, CHUNK)
            hat = L[11][at, :].astype(F32)
            grad = dh[at, :]
            rs = spread[at, 0:1]
            e = grad * gain
            prod = grad * hat
            m1 = jnp.mean(e, axis=-1, keepdims=True)
            m2 = jnp.mean(e * hat, axis=-1, keepdims=True)
            new = g[at, :] + rs * (e - m1 - hat * m2)
            g[at, :] = new
            L[0][at, :] = new.astype(BF16)
            r.sums[which] += jnp.sum(prod.reshape(CHUNK // 8, 8, width), axis=0)
            r.sums[2 + which] += jnp.sum(grad.reshape(CHUNK // 8, 8, width), axis=0)
            return carry

        lax.fori_loop(0, rows // CHUNK, body, 0)

    xh_load.wait()
    r2_load.wait()
    norm_back(1, r.spread)
    xh1_load = copies.start(r.xh1, L[11])
    r1_load = copies.start(r.r1, r.spread)

    for i in range(2):
        wo_load[i].wait()
        L[6][:, halves[i]] = dot_nn(L[0][...], L[12][:, halves[i]]).astype(BF16)
    wq_load += [
        copies.start(r.qkv_oth.at[j - 3], L[12].at[:, halves[j % 2]]) for j in range(4, 6)
    ]
    if reduce:
        if layer == 0:
            s_old.step()
        s_dn.step()
    o_load.wait()
    weight_grad(L[0][...], L[13][:, halves[0]], r.out_g, slice(0, cols))
    if reduce:
        s_out.send()

    to = [(1, 0), (1, 1), (2, 0), (2, 1), (7, 0), (7, 1)]

    def attend(group, start, stop):
        n = 3 * group
        steps = range(rows // TILE)

        def body(head, carry):
            c = [
                pl.ds(pl.multiple_of(side * cols + head * HEAD_DIM, HEAD_DIM), HEAD_DIM)
                for side in range(pieces)
            ]
            mine = c[group]
            q = [L[3 + n // 2][own_rows(i), c[n % 2]] for i in steps]
            k = [L[3 + (n + 1) // 2][key_rows(i), c[(n + 1) % 2]] for i in steps]
            v = [L[3 + (n + 2) // 2][key_rows(i), c[(n + 2) % 2]] for i in steps]
            do = [L[6][own_rows(i), mine] for i in steps]
            p = [L[14][own_rows(i), mine] for i in steps]
            dp = [dot_nt(x, y) for x, y in zip(do, v)]
            wide_p = [x.astype(F32) for x in p]
            inner = [jnp.sum(x * y, axis=-1, keepdims=True) for x, y in zip(dp, wide_p)]
            ds = [(y * (x - z)).astype(BF16) for x, y, z in zip(dp, wide_p, inner)]
            dq = [dot_nn(x, y) for x, y in zip(ds, k)]
            dk = [dot_tn(x, y) for x, y in zip(ds, q)]
            dv = [dot_tn(x, y) for x, y in zip(p, do)]
            (sq, hq), (sk, hk), (sv, hv) = to[n : n + 3]
            for i in steps:
                L[sq][own_rows(i), c[hq]] = (dq[i] * SCALE).astype(BF16)
                if i == 0:
                    own_k, own_v = dk[0][:TILE], dv[0][:TILE]
                else:
                    own_k, own_v = dk[i][TILE:], dv[i][TILE:]
                if i + 1 < len(steps):
                    own_k = own_k + dk[i + 1][:TILE]
                    own_v = own_v + dv[i + 1][:TILE]
                L[sk][own_rows(i), c[hk]] = (own_k * SCALE).astype(BF16)
                L[sv][own_rows(i), c[hv]] = own_v.astype(BF16)
            return carry

        lax.fori_loop(start, stop, body, 0)

    for load in (*qkv_load, *p_load):
        load.wait()
    attend(0, 0, heads // 2)
    if reduce:
        s_up.step()
        s_out.step()
    attend(0, heads // 2, heads)
    h1_load.wait()
    for j in range(3):
        slot, side = to[j]
        weight_grad(L[8][...], L[slot][:, halves[side]], r.qkv_g, slice(j * cols, (j + 1) * cols))
    if reduce:
        s_qkv.send()
        s_dn.step()
        if layer == 0:
            finish_old = s_old.last()
            for j in range(3):
                r.old_f[j] = finish_old[:, j * cols : (j + 1) * cols]
            copies.save(r.old_f, r.old_out)

    attend(1, 0, heads // 2)
    if reduce:
        s_out.step()
        if layer == 0:
            s_qkv.step()
        else:
            s_qkv.add()
            copies.save(r.qkv_g.at[pl.ds(s_qkv.base, 8)], r.qkv_out)
        s_up.step()
        r.dn_f[...] = s_dn.last()
        copies.save(r.dn_f, r.dn_out)
    attend(1, heads // 2, heads)
    if reduce:
        s_out.step()
    for load in wq_load:
        load.wait()

    def dh1(n, carry):
        at = rows_at(n, cols)
        dh[:, at] = (
            dot_nt(L[1][...], L[9][at, :]) + dot_nt(L[2][...], L[10][at, :]) + dot_nt(L[7][...], L[12][at, :])
        )
        return carry

    lax.fori_loop(0, pieces, dh1, 0)
    if reduce:
        if layer == 0:
            s_qkv.step()
        r.up_f[...] = s_up.last()
        copies.save(r.up_f, r.up_out)
    xh1_load.wait()
    r1_load.wait()
    norm_back(0, r.spread)
    copies.save(g, r.g_out)
    for k in range(4):
        r.flat[k : k + 1, :] = jnp.sum(r.sums[k], axis=0, keepdims=True)
    if not reduce:
        copies.save(r.dn_g, r.dn_out)
        copies.save(r.up_g, r.up_out)
        copies.save(r.out_g, r.out_out)
        copies.save(r.qkv_g, r.qkv_out)
        copies.save(r.flat, r.flat_out)
        copies.finish()
        return
    r.out_f[...] = s_out.last()
    copies.save(r.out_f, r.out_out)
    if layer == 1:
        copies.save(r.flat, r.flat_out)
    else:
        r.both[0:4, :] = r.flat[...]
        r.both[4:8, :] = r.flat_in[...]
        sends = []
        for o in range(1, GROUP):
            to_dev = lax.rem(low + o, GROUP)
            sends.append(
                remote.start(
                    r.both.at[:, rows_at(to_dev // 2, 128)],
                    r.slots.at[o],
                    (me - low + to_dev, t),
                )
            )
        s_qkv.step()
        total = r.both[:, rows_at(low // 2, 128)]
        for o, copy in enumerate(sends):
            copy.wait_recv()
            total = total + r.slots[o + 1]
        r.flat_f[...] = total
        copies.save(r.flat_f, r.flat_out)
        done = s_qkv.last()
        for j in range(3):
            r.qkv_f[j] = done[:, j * cols : (j + 1) * cols]
        copies.save(r.qkv_f, r.qkv_out)
    copies.finish()
    remote.finish()


def call(kernel, ins, outs, scratch, name, collective, flops):
    split = lambda v: v if isinstance(v, tuple) else (v, ANY)
    in_items = {k: split(v) for k, v in ins.items()}
    out_items = {k: split(v) for k, v in outs.items()}
    names = (*in_items, *out_items, *scratch)
    params = dict(vmem_limit_bytes=VMEM_LIMIT, has_side_effects=True)
    if collective is not None:
        params.update(collective_id=collective)
    made = pl.pallas_call(
        functools.partial(kernel, names),
        out_shape=tuple(v for v, _ in out_items.values()),
        in_specs=[pl.BlockSpec(memory_space=s) for _, s in in_items.values()],
        out_specs=tuple(pl.BlockSpec(memory_space=s) for _, s in out_items.values()),
        scratch_shapes=list(scratch.values()),
        compiler_params=pltpu.CompilerParams(**params),
        cost_estimate=pl.CostEstimate(flops=flops, bytes_accessed=60 << 20, transcendentals=0),
        name=name,
    )(*(v for v, _ in in_items.values()))
    return SimpleNamespace(**dict(zip(out_items, made)))


def forward(layer, x, bias, gain, shift, weights, other):
    rows, width = x.shape
    w_qkv, w_out, w_up, w_dn = weights
    cols, half = w_qkv.shape[-1], w_up.shape[-1]
    shape = jax.ShapeDtypeStruct
    wide, slab = (rows, width), (rows, cols)
    ins = dict(
        x_in=x, bias=bias, gain=(gain, VMEM), shift=(shift, VMEM),
        qkv_own=w_qkv, out_own=w_out, up_own=w_up, dn_own=w_dn,
    )
    outs = {}
    qkv_s, out_s = shape(w_qkv.shape[1:], BF16), shape(w_out.shape[1:], BF16)
    up_s, dn_s = shape(w_up.shape[1:], BF16), shape(w_dn.shape[1:], BF16)
    if layer == 0:
        outs.update(qkv_oth=qkv_s, out_oth=out_s, qkv_nxt=qkv_s, out_nxt=out_s)
    else:
        ins.update(qkv_oth=other.qkv_nxt, out_oth=other.out_nxt)
    outs.update(
        up_oth=up_s, dn_oth=dn_s,
        h1_out=shape(wide, BF16), xh1_out=shape(wide, BF16), r1_out=shape((rows, 128), F32),
        qkv_out=shape((6, *slab), BF16), p_out=shape((2, *slab), BF16), o_out=shape(slab, BF16),
        h2_out=shape(wide, BF16), xh2_out=shape(wide, BF16), r2_out=shape((rows, 128), F32),
        a_out=shape((rows, half), BF16), d_out=shape((2, rows, half), BF16),
        y_out=shape(wide, F32 if layer == 0 else BF16),
    )
    copies = 128 if layer == 0 else 16
    scratch = dict(
        x=VMEM(wide, F32), h1=VMEM(wide, BF16), xh1=VMEM(wide, BF16), r1=VMEM((rows, 128), F32),
        h2=VMEM(wide, BF16), xh2=VMEM(wide, BF16), r2=VMEM((rows, 128), F32),
        qkv=VMEM((6, *slab), BF16), o=VMEM((2, *slab), BF16), p=VMEM((2, *slab), BF16),
        mask=VMEM((rows, 128), F32), u=VMEM(slab, F32),
        a=VMEM((2, rows, half), BF16), d=VMEM((2, rows, half), BF16),
        wq=VMEM((6, width, cols), BF16), wo=VMEM((2, width, cols), BF16),
        wu=VMEM((2, width, half), BF16), wd=VMEM((2, width, half), BF16),
        sem=pltpu.SemaphoreType.DMA((40,)),
        send=pltpu.SemaphoreType.DMA((copies,)), recv=pltpu.SemaphoreType.DMA((copies,)),
    )
    if layer == 0:
        scratch.update(x_raw=VMEM(wide, BF16))
    flops = 2 * rows * (6 * cols * width + 2 * cols * width + 4 * half * width)
    return call(
        functools.partial(forward_kernel, layer), ins, outs, scratch, "forward", layer, flops
    )


def backward(layer, reduce, g, gain, weights, other, kept, before):
    rows, width = g.shape
    w_qkv, w_out, w_up, w_dn = weights
    cols, half = w_qkv.shape[-1], w_up.shape[-1]
    shape = jax.ShapeDtypeStruct
    wide = (rows, width)
    block = width // GROUP
    ins = dict(
        g_in=g, gain=(gain, VMEM),
        qkv_own=w_qkv, out_own=w_out, up_own=w_up, dn_own=w_dn,
        qkv_oth=other.qkv, out_oth=other.out, up_oth=other.up, dn_oth=other.dn,
    )
    ins.update(
        h1=kept.h1_out, xh1=kept.xh1_out, r1=kept.r1_out, qkv=kept.qkv_out, p=kept.p_out, o=kept.o_out,
        h2=kept.h2_out, xh2=kept.xh2_out, r2=kept.r2_out, a=kept.a_out, d=kept.d_out,
    )
    outs = dict(g_out=shape(wide, F32))
    grad = lambda n: VMEM((GROUP, block, n), BF16)
    recv = lambda k, n: VMEM((GROUP >> (k + 1), block, n), BF16)
    done = lambda n: VMEM((block, n), F32)
    all3 = 3 * cols
    scratch = dict(
        g=VMEM(wide, F32), dh=VMEM(wide, F32), spread=VMEM((rows, 128), F32),
        sums=VMEM((4, 8, width), F32), flat=VMEM((4, width), F32),
        sem=pltpu.SemaphoreType.DMA((56,)),
        dn_g=grad(half), up_g=grad(half), out_g=grad(cols), qkv_g=grad(all3),
    )
    scratch.update({f"{SLOT}{i}": VMEM(wide, BF16) for i in range(15)})
    if not reduce:
        full = lambda n: shape((GROUP, block, n), BF16)
        outs.update(dn_out=full(half), up_out=full(half), out_out=full(cols), qkv_out=full(all3))
        outs.update(flat_out=shape((4, width), F32))
    else:
        copies = 4 * 4 + 3 + GROUP
        part = lambda n: shape((block, n), F32)
        outs.update(dn_out=part(half), up_out=part(half), out_out=part(cols))
        scratch.update(
            send=pltpu.SemaphoreType.DMA((copies,)), recv=pltpu.SemaphoreType.DMA((copies,)),
            dn_f=done(half), up_f=done(half), out_f=done(cols), qkv_r0=recv(0, all3),
            dn_r0=recv(0, half), dn_r1=recv(1, half), dn_r2=recv(2, half), dn_r3=recv(3, half),
            up_r0=recv(0, half), up_r1=recv(1, half), up_r2=recv(2, half), up_r3=recv(3, half),
            out_r0=recv(0, cols), out_r1=recv(1, cols), out_r2=recv(2, cols), out_r3=recv(3, cols),
        )
        if layer == 1:
            outs.update(flat_out=shape((4, width), F32), qkv_out=shape((8, block, all3), BF16))
        else:
            three = shape((3, block, cols), F32)
            outs.update(flat_out=shape((8, 128), F32), qkv_out=three, old_out=three)
            ins.update(old_in=before.qkv_out, flat_in=(before.flat_out, VMEM))
            scratch.update(
                qkv_r1=recv(1, all3), qkv_r2=recv(2, all3), qkv_r3=recv(3, all3),
                old_g=VMEM((8, block, all3), BF16),
                old_r1=recv(1, all3), old_r2=recv(2, all3), old_r3=recv(3, all3),
                old_f=VMEM((3, block, cols), F32), qkv_f=VMEM((3, block, cols), F32),
                both=VMEM((8, width), F32), slots=VMEM((GROUP, 8, 128), F32), flat_f=VMEM((8, 128), F32),
            )
    flops = 2 * rows * (2 * 6 * cols * width + 3 * cols * width + 6 * half * width)
    return call(
        functools.partial(backward_kernel, layer, reduce), ins, outs, scratch,
        "backward", 2 + layer if reduce else None, flops,
    )


def local(n_dp, tokens, lengths, w_qkv, w_out, w_up, w_down, norm_gain, norm_bias, cotangent):
    rows, width = tokens.shape
    cols = w_qkv.shape[3]
    items = lengths.shape[1]
    order = jnp.arange(items, dtype=jnp.int32)
    ends = jnp.sum(jnp.where(order[:, None] >= order[None, :], lengths, 0), axis=1)
    place = jnp.arange(rows, dtype=jnp.int32)
    start = jnp.max(jnp.where(ends[None, :] <= place[:, None], ends[None, :], 0), axis=1)
    window = jnp.maximum(place // TILE - 1, 0) * TILE
    key = window[:, None] + jnp.arange(2 * TILE, dtype=jnp.int32)[None, :]
    allowed = (key >= start[:, None]) & (key <= place[:, None])
    bias = jnp.where(allowed, 0.0, MASKED).astype(F32)

    weights = (jnp.transpose(w_qkv, (0, 2, 1, 3)), w_out, w_up, w_down)
    f0 = forward(0, tokens, bias, norm_gain[0], norm_bias[0], weights, None)
    f1 = forward(1, f0.y_out, bias, norm_gain[1], norm_bias[1], weights, f0)
    output = f1.y_out
    reduce = n_dp == GROUP
    oth0 = SimpleNamespace(qkv=f0.qkv_oth, out=f0.out_oth, up=f0.up_oth, dn=f0.dn_oth)
    oth1 = SimpleNamespace(qkv=f0.qkv_nxt, out=f0.out_nxt, up=f1.up_oth, dn=f1.dn_oth)
    b1 = backward(1, reduce, cotangent, norm_gain[1], weights, oth1, f1, None)
    b0 = backward(0, reduce, b1.g_out, norm_gain[0], weights, oth0, f0, b1)
    grad = b0.g_out
    out, up, dn = (
        jnp.stack(v)
        for v in ((b0.out_out, b1.out_out), (b0.up_out, b1.up_out), (b0.dn_out, b1.dn_out))
    )
    if reduce:
        qkv = jnp.transpose(jnp.stack([b0.qkv_out, b0.old_out]), (0, 2, 1, 3))
        side = lax.rem(lax.axis_index("dp"), 2)
        block = width // GROUP
        flat = b0.flat_out.reshape(2, 4, 128)
        flat = lax.dynamic_slice_in_dim(flat, side * block, block, axis=2)
    else:

        def total(both):
            n = both.shape[-1]
            both = both.astype(F32).reshape(2, 2, 2, 2, 2, width // GROUP, n)
            both = jnp.transpose(both, (0, 4, 3, 2, 1, 5, 6)).reshape(2, width, n)
            return lax.psum_scatter(both, "dp", scatter_dimension=1, tiled=True)

        out, up, dn = total(out), total(up), total(dn)
        qkv = total(jnp.stack([b0.qkv_out, b1.qkv_out]))
        qkv = qkv.reshape(*qkv.shape[:2], 3, cols)
        flat = jnp.stack([b0.flat_out, b1.flat_out])
        flat = lax.psum_scatter(flat, "dp", scatter_dimension=2, tiled=True)
    gain, shift = flat[:, :2], flat[:, 2:]
    return (output, grad, qkv, out, up, dn, gain, shift)


def solution(mesh):
    placed = (
        P("dp", None),
        P("dp", None),
        P(None, None, None, "tensor"),
        P(None, None, "tensor"),
        P(None, None, "tensor"),
        P(None, None, "tensor"),
        P(),
        P(),
        P("dp", None),
    )
    return jax.shard_map(
        functools.partial(local, mesh.shape["dp"]),
        mesh=mesh,
        in_specs=placed,
        out_specs=(
            P("dp", None),
            P("dp", None),
            P(None, "dp", None, "tensor"),
            P(None, "dp", "tensor"),
            P(None, "dp", "tensor"),
            P(None, "dp", "tensor"),
            P(None, None, "dp"),
            P(None, None, "dp"),
        ),
        check_vma=False,
    )
```

```python
import functools
from types import SimpleNamespace

import jax
import jax.numpy as jnp
from jax import lax
from jax.experimental import pallas as pl
from jax.experimental.pallas import tpu as pltpu
from jax.sharding import PartitionSpec as P

HEAD_DIM = 128
TILE = 64
EPS = 1e-05
MASKED = -1e30
MESH = pl.DeviceIdType.MESH
VMEM = pltpu.VMEM
ANY = pl.ANY
F32 = jnp.float32
BF16 = jnp.bfloat16
SCALE = HEAD_DIM**-0.5
VMEM_LIMIT = 62 << 20
SLOT = "L"
GROUP = 16
CHUNK = 256

FORWARD_ORDERS = ((4, 2, 1), (2, 4, 1), (4, 2, 1), (2, 4, 1), (4, 2, 1), (4, 1), (4, 1), (4, 2, 1), (2, 1), (1,), (4, 1), (1,))
FORWARD_PLAN = ((0, 1), (2,), (0,), (3,), (1,), (0, 4), (2,), (), (1,), (3,), (2, 5, 0, 4, 1, 0, 3), (1,), (2, 4, 6, 5, 2), (3, 7, 8), (), (6,), (3,), (), (7, 9, 4), (), (4, 5, 8), (), (5, 6, 7, 10), (6, 8, 9), (8,), (7, 9), (11,), (7,), (), (10,), (), (), (), (), (), (), (), (), (), (), (), (10,), (), (), (10,), (11,), (), (11,), (), (),)
BACKWARD_ORDERS = ((1, 4, 2, 8), (1, 4, 2, 8), (1, 2, 4, 8), (1, 4, 8, 2), (1, 2, 4, 8), (1, 8, 2, 4), (1, 2, 4, 8), (1, 2, 4, 8), (1, 2, 8, 4), (1, 2, 4, 8), (1, 8, 4, 2), (1, 2, 4, 8), (1, 2, 8, 4), (1, 2, 8, 4), (1, 2, 4, 8), (1, 4, 2, 8))
BACKWARD_PLAN = ((), (), (), (), (), (), (0,), (1,), (2, 3), (0,), (), (), (2, 1), (0,), (), (4, 1, 3), (), (2,), (), (0,), (4, 5, 1), (6,), (7,), (), (3,), (2, 4, 6), (), (7, 3), (), (5,), (), (4, 6), (7, 5), (), (8, 6), (5, 9, 7, 10), (11,), (8,), (), (), (9,), (), (10,), (11, 12, 9), (), (8, 10), (), (11,), (12, 13, 9, 8, 10, 14), (15, 11), (), (), (), (13, 12, 15), (14,), (15, 12, 13), (14, 15, 13, 14),)

ERFC = (
    0.22567586600780487,
    0.22566960752010345,
    0.20784251391887665,
    0.16854380071163177,
    0.14142295718193054,
    -0.005586510524153709,
    0.1690569967031479,
    -0.18288171291351318,
    0.05025661736726761,
)


def dot_nn(a, b):
    return lax.dot_general(a, b, (((1,), (0,)), ((), ())), preferred_element_type=F32)


def dot_nt(a, b):
    return lax.dot_general(a, b, (((1,), (1,)), ((), ())), preferred_element_type=F32)


def dot_tn(a, b):
    return lax.dot_general(a, b, (((0,), (0,)), ((), ())), preferred_element_type=F32)


def rows_at(index, size):
    return pl.ds(pl.multiple_of(index * size, size), size)


def own_rows(step):
    return slice(step * TILE, (step + 1) * TILE)


def key_rows(step):
    first = max(step - 1, 0) * TILE
    return slice(first, first + 2 * TILE)


def flip(value, bit):
    return value + bit * (1 - 2 * lax.rem(value // bit, 2))


def normalize(x):
    center = x - jnp.mean(x, axis=-1, keepdims=True)
    spread = lax.rsqrt(jnp.mean(center * center, axis=-1, keepdims=True) + EPS)
    return center * spread, spread


def gelu_parts(u):
    t = 1.0 / (1.0 + (0.4 * 0.7071067811865476) * jnp.abs(u))
    q = jnp.full_like(t, ERFC[-1])
    for c in ERFC[-2::-1]:
        q = q * t + c
    e = jnp.exp(-0.5 * (u * u))
    tail = 0.5 * (t * q) * e
    cdf = jnp.where(u >= 0, 1.0 - tail, tail)
    return u * cdf, cdf + u * (e * 0.3989422804014327)


class Copies:
    def __init__(self, sems):
        self.sems, self.n, self.open = sems, 0, []

    def start(self, src, dst):
        assert self.n < self.sems.shape[0]
        copy = pltpu.make_async_copy(src, dst, self.sems.at[self.n])
        self.n += 1
        copy.start()
        return copy

    def save(self, src, dst):
        self.open.append(self.start(src, dst))
        return self.open[-1]

    def settle(self, copy):
        self.open = [c for c in self.open if c is not copy]
        copy.wait()

    def finish(self):
        for copy in self.open:
            copy.wait()


class Remote:
    def __init__(self, send, recv):
        self.send, self.recv, self.n, self.sent = send, recv, 0, []

    def start(self, src, dst, device):
        assert self.n < self.send.shape[0]
        copy = pltpu.make_async_remote_copy(
            src_ref=src,
            dst_ref=dst,
            send_sem=self.send.at[self.n],
            recv_sem=self.recv.at[self.n],
            device_id=device,
            device_id_type=MESH,
        )
        self.n += 1
        copy.start()
        self.sent.append(copy)
        return copy

    def settle(self, copies):
        for copy in copies:
            copy.wait_send()
            self.sent = [c for c in self.sent if c is not copy]

    def finish(self):
        for copy in self.sent:
            copy.wait_send()


def greet(devices):
    barrier = pltpu.get_barrier_semaphore()
    for device in devices:
        pl.semaphore_signal(barrier, inc=1, device_id=device, device_id_type=MESH)
    pl.semaphore_wait(barrier, len(devices))


class Gather:
    def __init__(self, remote, own, other, order):
        self.remote, self.own, self.other, self.order = remote, own, other, order
        me, t = lax.axis_index("dp"), lax.axis_index("tensor")
        self.me, self.t = me, t
        self.have = [lax.rem(me, 8)]
        for bit in (1, 2, 4):
            if bit not in order:
                self.have += [flip(b, bit) for b in self.have]
        self.stage, self.flying, self.done = -1, [], False

    def block(self, ref, index):
        return ref.at[rows_at(index, ref.shape[0] // 8), :]

    def step(self):
        for copy in self.flying:
            copy.wait_recv()
        if self.stage == len(self.order):
            self.done = True
            return
        source = self.other
        if self.stage < 0:
            source, device = self.own, (self.me, 1 - self.t)
        else:
            if self.stage > 0:
                self.have = self.have + [flip(b, self.order[self.stage - 1]) for b in self.have]
            device = (flip(self.me, self.order[self.stage]), self.t)
        self.stage += 1
        self.flying = [
            self.remote.start(self.block(source, b), self.block(self.other, b), device)
            for b in self.have
        ]


class Scatter:
    def __init__(self, remote, grad, recvs, order, finish):
        self.remote, self.grad, self.recvs, self.order = remote, grad, recvs, order
        self.finish = finish
        self.me, self.t = lax.axis_index("dp"), lax.axis_index("tensor")
        self.base, self.count, self.stage, self.done, self.sent = 0, GROUP, -1, False, []

    def step(self):
        if self.stage >= 0:
            self.flying.wait_recv()
            recv = self.recvs[self.stage]
            if self.count == 1:
                self.finish(self.grad[self.base].astype(F32) + recv[0].astype(F32))
                self.done = True
                return

            def body(i, carry):
                at = self.base + i
                self.grad[at] = (self.grad[at].astype(F32) + recv[i].astype(F32)).astype(BF16)
                return carry

            lax.fori_loop(0, self.count, body, 0)
        self.stage += 1
        bit = self.order[self.stage]
        mine = lax.rem(self.me // bit, 2)
        half = self.count // 2
        out = self.base + (1 - mine) * half
        self.base = self.base + mine * half
        self.count = half
        self.flying = self.remote.start(
            self.grad.at[pl.ds(out, half)],
            self.recvs[self.stage],
            (flip(self.me, bit), self.t),
        )
        self.sent.append(self.flying)


def position(block, order):
    pos = 0
    for bit in order:
        pos = 2 * pos + block // bit % 2
    return pos


class Pump:
    def __init__(self, items, plan, before=None, after=None):
        self.items, self.plan, self.at = items, plan, 0
        self.before, self.after = before, after

    def step(self, i):
        if not self.items[i].done:
            if self.before is not None:
                self.before(i)
            self.items[i].step()
            if self.after is not None and self.items[i].done:
                self.after(i)

    def tick(self):
        if self.at < len(self.plan):
            for i in self.plan[self.at]:
                self.step(i)
        self.at += 1

    def need(self, i):
        while not self.items[i].done:
            self.step(i)


def forward_kernel(names, *args):
    r = SimpleNamespace(**dict(zip(names, args)))
    copies = Copies(r.sem)
    remote = Remote(r.send, r.recv)
    me, t = lax.axis_index("dp"), lax.axis_index("tensor")
    rows, width = r.x.shape
    cols = r.qkv_own.shape[-1]
    heads = cols // HEAD_DIM
    half = r.up_own.shape[-1]
    pieces = width // cols
    x, qkv, wq = r.x, r.qkv, r.wq

    x_load = copies.start(r.x_in, r.x_raw)
    greet([(me, 1 - t), (flip(me, 2), t), (flip(me, 4), t), (flip(me, 1), t)])

    def stored(layer, kind, side):
        if kind < 3:
            return (r.qkv_oth if side else r.qkv_own).at[layer, kind]
        pair = ((r.out_own, r.out_oth), (r.up_own, r.up_oth), (r.dn_own, r.dn_oth))[kind - 3]
        return pair[side].at[layer]

    def buffer(kind, side):
        if kind < 3:
            return wq.at[3 * side + kind]
        return (r.wo, r.wu, r.wd)[kind - 3].at[side]

    gathers = [
        Gather(remote, stored(i // 6, i % 6, 0), stored(i // 6, i % 6, 1), FORWARD_ORDERS[i])
        for i in range(12)
    ]
    loads, free = {}, {(kind, side): 0 for kind in range(6) for side in range(2)}

    def load(layer, kind, side):
        if (layer, kind, side) in loads or free[kind, side] < layer:
            return
        if side == 0 or gathers[6 * layer + kind].done:
            loads[layer, kind, side] = copies.start(
                stored(layer, kind, side), buffer(kind, side)
            )

    pump = Pump(gathers, FORWARD_PLAN, after=lambda i: load(i // 6, i % 6, 1))

    def get(layer, kind, side):
        if side:
            pump.need(6 * layer + kind)
        load(layer, kind, side)
        loads[layer, kind, side].wait()

    def used(kind, side):
        free[kind, side] += 1
        if free[kind, side] < 2:
            load(free[kind, side], kind, side)

    pump.tick()
    for kind in range(3):
        load(0, kind, 0)
    mask_load = copies.start(r.bias, r.mask)
    for kind in range(3, 6):
        load(0, kind, 0)
    pump.tick()
    saves = {}

    def save(src, dst, part=None):
        saves[id(src)] = copies.save(src if part is None else src.at[part], dst)

    def reuse(src):
        if id(src) in saves:
            copies.settle(saves.pop(id(src)))

    def norm(layer, which, h, xh, spread, source=None):
        gain = r.gain[layer, which : which + 1, :]
        shift = r.shift[layer, which : which + 1, :]
        for ref in (h, xh, spread):
            reuse(ref)

        def body(i, carry):
            at = rows_at(i, CHUNK)
            if source is not None:
                values = source[at, :].astype(F32)
                x[at, :] = values
            else:
                values = x[at, :]
            hat, rs = normalize(values)
            xh[at, :] = hat.astype(BF16)
            h[at, :] = (hat * gain + shift).astype(BF16)
            spread[at, :] = jnp.broadcast_to(rs, (CHUNK, HEAD_DIM))
            return carry

        lax.fori_loop(0, rows // CHUNK, body, 0)

    def project(layer, side):
        for kind in range(3):
            get(layer, kind, side)
            j = 3 * side + kind
            qkv[j] = dot_nn(r.h1[...], wq[j]).astype(BF16)
            used(kind, side)
            pump.tick()

    def attend(group):
        q_ref, k_ref, v_ref = (qkv.at[3 * group + j] for j in range(3))
        steps = range(rows // TILE)
        for head in range(heads):
            c = slice(head * HEAD_DIM, (head + 1) * HEAD_DIM)
            s = [
                dot_nt(q_ref[own_rows(i), c], k_ref[key_rows(i), c]) * SCALE + r.mask[own_rows(i), :]
                for i in steps
            ]
            top = [jnp.max(v, axis=-1, keepdims=True) for v in s]
            e = [jnp.exp(v - m) for v, m in zip(s, top)]
            total = [jnp.sum(v, axis=-1, keepdims=True) for v in e]
            p = [(v * (1.0 / m)).astype(BF16) for v, m in zip(e, total)]
            mixed = [dot_nn(v, v_ref[key_rows(i), c]) for v, i in zip(p, steps)]
            for i in steps:
                r.p[group, own_rows(i), c] = p[i]
                r.o[group, own_rows(i), c] = mixed[i].astype(BF16)
            pump.tick()

    def add_product(ref, weight, side):
        def body(n, carry):
            at = rows_at(n, cols)
            x[:, at] += dot_nt(ref[side], weight[side, at, :])
            return carry

        lax.fori_loop(0, pieces, body, 0)

    def up(layer, side):
        get(layer, 4, side)
        for n in range(half // cols):
            at = slice(n * cols, (n + 1) * cols)
            r.u[...] = dot_nn(r.h2[...], r.wu[side, :, at])

            def inner(i, carry):
                i_at = rows_at(i, CHUNK // 2)
                a, d = gelu_parts(r.u[i_at, :])
                r.a[side, i_at, at] = a.astype(BF16)
                r.d[side, i_at, at] = d.astype(BF16)
                return carry

            lax.fori_loop(0, 2 * rows // CHUNK, inner, 0)
            pump.tick()
        used(4, side)

    x_load.wait()
    for layer in range(2):
        norm(layer, 0, r.h1, r.xh1, r.r1, None if layer else r.x_raw)
        save(r.h1, r.h1_out.at[layer])
        save(r.xh1, r.xh1_out.at[layer])
        save(r.r1, r.r1_out.at[layer])
        pump.tick()
        for ref in (qkv, r.o, r.p):
            reuse(ref)
        project(layer, 0)
        if layer == 0:
            mask_load.wait()
        attend(0)
        get(layer, 3, 0)
        add_product(r.o, r.wo, 0)
        used(3, 0)
        pump.tick()
        project(layer, 1)
        save(qkv, r.qkv_out.at[layer])
        attend(1)
        save(r.p, r.p_out.at[layer])
        save(r.o, r.o_out.at[layer], 0)
        get(layer, 3, 1)
        add_product(r.o, r.wo, 1)
        used(3, 1)
        pump.tick()
        norm(layer, 1, r.h2, r.xh2, r.r2)
        save(r.h2, r.h2_out.at[layer])
        save(r.xh2, r.xh2_out.at[layer])
        save(r.r2, r.r2_out.at[layer])
        pump.tick()
        reuse(r.a)
        reuse(r.d)
        up(layer, 0)
        up(layer, 1)
        save(r.a, r.a_out.at[layer], 0)
        save(r.d, r.d_out.at[layer])
        for side in range(2):
            get(layer, 5, side)
            add_product(r.a, r.wd, side)
            used(5, side)
            pump.tick()

    def finish(i, carry):
        at = rows_at(i, CHUNK)
        r.x_raw[at, :] = x[at, :].astype(BF16)
        return carry

    lax.fori_loop(0, rows // CHUNK, finish, 0)
    copies.save(r.x_raw, r.y_out)
    copies.finish()
    remote.finish()


def backward_kernel(reduce, names, *args):
    r = SimpleNamespace(**dict(zip(names, args)))
    copies = Copies(r.sem)
    me, t = lax.axis_index("dp"), lax.axis_index("tensor")
    g, dh = r.g, r.dh
    L = [v for k, v in zip(names, args) if k[0] == SLOT]
    rows, width = g.shape
    cols = r.qkv_own.shape[-1]
    heads = cols // HEAD_DIM
    half = r.up_own.shape[-1]
    pieces = width // cols
    halves = [slice(i * cols, (i + 1) * cols) for i in range(pieces)]

    def target(layer, i):
        if i < 2:
            return r.dn_out.at[layer, :, halves[i]]
        if i < 4:
            return r.up_out.at[layer, :, halves[i - 2]]
        return r.out_out.at[layer] if i == 4 else r.qkv_out.at[layer, i - 5]

    if reduce:
        remote = Remote(r.send, r.recv)
        low = lax.rem(me, GROUP)
        greet([(me - low + lax.rem(low + o, GROUP), t) for o in range(1, GROUP)])

        def ending(n):
            def finish(value):
                r.final[n] = value
                copies.save(r.final.at[n], target(1 - n // 8, n % 8))

            return finish

        pump = Pump(
            [
                Scatter(
                    remote, r.grad.at[n % 8], [ref.at[n % 8] for ref in (r.r0, r.r1_, r.r2_, r.r3)],
                    BACKWARD_ORDERS[n], ending(n),
                )
                for n in range(16)
            ],
            BACKWARD_PLAN,
            before=lambda n: order_layers(n),
        )

        def order_layers(n):
            if n < 8 or pump.items[n].stage == 3:
                return
            bit = BACKWARD_ORDERS[n][pump.items[n].stage + 1]
            for m in range(8):
                while not pump.items[m].done and (
                    BACKWARD_ORDERS[m].index(bit) >= pump.items[m].stage
                ):
                    pump.step(m)

        tick = pump.tick
    else:
        tick = lambda: None
        spare = []

    g_load = copies.start(r.g_in, L[0])

    def load_first(layer):
        wd = [copies.start(r.dn_own.at[layer], L[3]), copies.start(r.dn_oth.at[layer], L[4])]
        d = [copies.start(r.d.at[layer, i], L[5 + i]) for i in range(2)]
        return wd, d

    def load_second(layer):
        a = copies.start(r.a.at[layer], L[7])
        wu = [copies.start(r.up_own.at[layer], L[9]), copies.start(r.up_oth.at[layer], L[10])]
        wo = [
            copies.start(r.out_own.at[layer], L[12].at[:, halves[0]]),
            copies.start(r.out_oth.at[layer], L[12].at[:, halves[1]]),
        ]
        return a, wu, wo

    def load_third(layer):
        h2 = copies.start(r.h2.at[layer], L[8])
        o = copies.start(r.o.at[layer], L[13].at[:, halves[0]])
        p = [copies.start(r.p.at[layer, i], L[14].at[:, halves[i]]) for i in range(2)]
        return h2, o, p

    def load_norm(layer, which):
        pair = ((r.xh1, r.r1), (r.xh2, r.r2))[which]
        return [copies.start(pair[0].at[layer], L[11]), copies.start(pair[1].at[layer], r.spread)]

    first = load_first(1)
    second = load_second(1)
    third = load_third(1)
    norm_load = load_norm(1, 1)

    def zero(i, carry):
        r.sums[i] = jnp.zeros((8, width), F32)
        return carry

    lax.fori_loop(0, 8, zero, 0)
    g_load.wait()

    def begin(i, carry):
        at = rows_at(i, CHUNK)
        g[at, :] = L[0][at, :].astype(F32)
        return carry

    lax.fori_loop(0, rows // CHUNK, begin, 0)

    def weight_grad(n, lhs, rhs):
        if reduce:
            if n >= 8:
                pump.need(n - 8)
                remote.settle(pump.items[n - 8].sent)
        elif n >= 8:
            copies.settle(spare[n - 8])
        full = dot_tn(lhs, rhs)
        size = width // GROUP
        for d in range(GROUP):
            r.grad[n % 8, position(d, BACKWARD_ORDERS[n])] = full[d * size : (d + 1) * size].astype(
                BF16
            )
        if not reduce:
            spare.append(copies.save(r.grad.at[n % 8], r.grad_out.at[1 - n // 8, n % 8]))
            return
        pump.step(n)
        tick()

    def norm_back(layer, which, loads):
        gain = r.gain[layer, which : which + 1, :]
        row = 4 * layer + which
        for load in loads:
            load.wait()

        def body(i, carry):
            at = rows_at(i, CHUNK)
            hat = L[11][at, :].astype(F32)
            grad = dh[at, :]
            rs = r.spread[at, 0:1]
            e = grad * gain
            prod = grad * hat
            m1 = jnp.mean(e, axis=-1, keepdims=True)
            m2 = jnp.mean(e * hat, axis=-1, keepdims=True)
            new = g[at, :] + rs * (e - m1 - hat * m2)
            g[at, :] = new
            L[0][at, :] = new.astype(BF16)
            r.sums[row] += jnp.sum(prod.reshape(CHUNK // 8, 8, width), axis=0)
            r.sums[row + 2] += jnp.sum(grad.reshape(CHUNK // 8, 8, width), axis=0)
            return carry

        lax.fori_loop(0, rows // CHUNK, body, 0)

    to = [(1, 0), (1, 1), (2, 0), (2, 1), (7, 0), (7, 1)]

    def attend(group):
        n = 3 * group
        steps = range(rows // TILE)
        for head in range(heads):
            c = [
                slice(side * cols + head * HEAD_DIM, side * cols + (head + 1) * HEAD_DIM)
                for side in range(pieces)
            ]
            mine = c[group]
            q = [L[3 + n // 2][own_rows(i), c[n % 2]] for i in steps]
            k = [L[3 + (n + 1) // 2][key_rows(i), c[(n + 1) % 2]] for i in steps]
            v = [L[3 + (n + 2) // 2][key_rows(i), c[(n + 2) % 2]] for i in steps]
            do = [L[6][own_rows(i), mine] for i in steps]
            p = [L[14][own_rows(i), mine] for i in steps]
            dp = [dot_nt(x, y) for x, y in zip(do, v)]
            wide_p = [x.astype(F32) for x in p]
            inner = [jnp.sum(x * y, axis=-1, keepdims=True) for x, y in zip(dp, wide_p)]
            ds = [(y * (x - z)).astype(BF16) for x, y, z in zip(dp, wide_p, inner)]
            dq = [dot_nn(x, y) for x, y in zip(ds, k)]
            dk = [dot_tn(x, y) for x, y in zip(ds, q)]
            dv = [dot_tn(x, y) for x, y in zip(p, do)]
            (sq, hq), (sk, hk), (sv, hv) = to[n : n + 3]
            for i in steps:
                L[sq][own_rows(i), c[hq]] = (dq[i] * SCALE).astype(BF16)
                if i == 0:
                    own_k, own_v = dk[0][:TILE], dv[0][:TILE]
                else:
                    own_k, own_v = dk[i][TILE:], dv[i][TILE:]
                if i + 1 < len(steps):
                    own_k = own_k + dk[i + 1][:TILE]
                    own_v = own_v + dv[i + 1][:TILE]
                L[sk][own_rows(i), c[hk]] = (own_k * SCALE).astype(BF16)
                L[sv][own_rows(i), c[hv]] = own_v.astype(BF16)
            tick()

    for layer in (1, 0):
        base = 8 * (1 - layer)
        wd_load, d_load = first
        a_load, wu_load, wo_load = second
        h2_load, o_load, p_load = third
        for i in range(2):
            wd_load[i].wait()
            d_load[i].wait()
            for at in halves:
                da = dot_nn(L[0][...], L[3 + i][:, at])
                L[1 + i][:, at] = (da * L[5 + i][:, at].astype(F32)).astype(BF16)
                tick()
        qkv_load = [
            copies.start(r.qkv.at[layer, j], L[3 + j // 2].at[:, halves[j % 2]]) for j in range(6)
        ]
        a_load.wait()
        for i in range(2):
            weight_grad(base + i, L[0][...], L[7][:, halves[i]])
        h2_load.wait()
        for i in range(2):
            weight_grad(base + 2 + i, L[8][...], L[1][:, halves[i]])
        h1_load = copies.start(r.h1.at[layer], L[8])
        for load in wu_load:
            load.wait()
        for at in halves:
            dh[:, at] = dot_nt(L[1][...], L[9][at, :]) + dot_nt(L[2][...], L[10][at, :])
            tick()

        def load_wq(some):
            return [
                copies.start(
                    r.qkv_own.at[layer, j] if j < 3 else r.qkv_oth.at[layer, j - 3],
                    L[(9, 10, 12)[j // 2]].at[:, halves[j % 2]],
                )
                for j in some
            ]

        wq_load = load_wq(range(4))
        norm_back(layer, 1, norm_load)
        norm_load = load_norm(layer, 0)
        tick()
        for i in range(2):
            wo_load[i].wait()
            L[6][:, halves[i]] = dot_nn(L[0][...], L[12][:, halves[i]]).astype(BF16)
            tick()
        wq_load += load_wq(range(4, 6))
        o_load.wait()
        weight_grad(base + 4, L[0][...], L[13][:, halves[0]])
        for load in (*qkv_load, *p_load):
            load.wait()
        attend(0)
        h1_load.wait()
        for j in range(3):
            slot, side = to[j]
            weight_grad(base + 5 + j, L[8][...], L[slot][:, halves[side]])
        attend(1)
        if layer == 1:
            first = load_first(0)
            third = load_third(0)
        for load in wq_load:
            load.wait()
        for at in halves:
            dh[:, at] = (
                dot_nt(L[1][...], L[9][at, :])
                + dot_nt(L[2][...], L[10][at, :])
                + dot_nt(L[7][...], L[12][at, :])
            )
            tick()
        if layer == 1:
            second = load_second(0)
        norm_back(layer, 0, norm_load)
        if layer == 1:
            norm_load = load_norm(0, 1)
        tick()
    copies.save(g, r.g_out)
    for k in range(8):
        r.flat[k : k + 1, :] = jnp.sum(r.sums[k], axis=0, keepdims=True)
    if not reduce:
        copies.save(r.flat, r.flat_out)
        copies.finish()
        return
    sends = []
    for o in range(1, GROUP):
        to_dev = lax.rem(low + o, GROUP)
        sends.append(
            remote.start(
                r.flat.at[:, rows_at(to_dev // 2, 128)], r.slots.at[o], (me - low + to_dev, t)
            )
        )
    tick()
    while pump.at < len(BACKWARD_PLAN):
        tick()
    for n in range(16):
        pump.need(n)
    total = r.flat[:, rows_at(low // 2, 128)]
    for o, copy in enumerate(sends):
        copy.wait_recv()
        total = total + r.slots[o + 1]
    r.flat_f[...] = total
    copies.save(r.flat_f, r.flat_out)
    copies.finish()
    remote.finish()


def call(kernel, ins, outs, scratch, name, collective, flops):
    split = lambda v: v if isinstance(v, tuple) else (v, ANY)
    in_items = {k: split(v) for k, v in ins.items()}
    out_items = {k: split(v) for k, v in outs.items()}
    names = (*in_items, *out_items, *scratch)
    params = dict(vmem_limit_bytes=VMEM_LIMIT, has_side_effects=True)
    if collective is not None:
        params.update(collective_id=collective)
    made = pl.pallas_call(
        functools.partial(kernel, names),
        out_shape=tuple(v for v, _ in out_items.values()),
        in_specs=[pl.BlockSpec(memory_space=s) for _, s in in_items.values()],
        out_specs=tuple(pl.BlockSpec(memory_space=s) for _, s in out_items.values()),
        scratch_shapes=list(scratch.values()),
        compiler_params=pltpu.CompilerParams(**params),
        cost_estimate=pl.CostEstimate(flops=flops, bytes_accessed=60 << 20, transcendentals=0),
        name=name,
    )(*(v for v, _ in in_items.values()))
    return SimpleNamespace(**dict(zip(out_items, made)))


def forward(x, bias, gain, shift, weights):
    rows, width = x.shape
    w_qkv, w_out, w_up, w_dn = weights
    cols, half = w_qkv.shape[-1], w_up.shape[-1]
    shape = jax.ShapeDtypeStruct
    wide, slab = (rows, width), (rows, cols)
    like = lambda w: shape(w.shape, BF16)
    two = lambda *dims, dtype=BF16: shape((2, *dims), dtype)
    ins = dict(
        x_in=x, bias=bias, gain=(gain, VMEM), shift=(shift, VMEM),
        qkv_own=w_qkv, out_own=w_out, up_own=w_up, dn_own=w_dn,
    )
    outs = dict(
        qkv_oth=like(w_qkv), out_oth=like(w_out), up_oth=like(w_up), dn_oth=like(w_dn),
        h1_out=two(*wide), xh1_out=two(*wide), r1_out=two(rows, 128, dtype=F32),
        qkv_out=two(6, *slab), p_out=two(2, *slab), o_out=two(*slab),
        h2_out=two(*wide), xh2_out=two(*wide), r2_out=two(rows, 128, dtype=F32),
        a_out=two(rows, half), d_out=two(2, rows, half),
        y_out=shape(wide, BF16),
    )
    copies = 12 * 8
    scratch = dict(
        x=VMEM(wide, F32), x_raw=VMEM(wide, BF16),
        h1=VMEM(wide, BF16), xh1=VMEM(wide, BF16), r1=VMEM((rows, 128), F32),
        h2=VMEM(wide, BF16), xh2=VMEM(wide, BF16), r2=VMEM((rows, 128), F32),
        qkv=VMEM((6, *slab), BF16), o=VMEM((2, *slab), BF16), p=VMEM((2, *slab), BF16),
        mask=VMEM((rows, 128), F32), u=VMEM(slab, F32),
        a=VMEM((2, rows, half), BF16), d=VMEM((2, rows, half), BF16),
        wq=VMEM((6, width, cols), BF16), wo=VMEM((2, width, cols), BF16),
        wu=VMEM((2, width, half), BF16), wd=VMEM((2, width, half), BF16),
        sem=pltpu.SemaphoreType.DMA((64,)),
        send=pltpu.SemaphoreType.DMA((copies,)), recv=pltpu.SemaphoreType.DMA((copies,)),
    )
    flops = 4 * rows * (6 * cols * width + 2 * cols * width + 4 * half * width)
    return call(forward_kernel, ins, outs, scratch, "forward", 0, flops)


def backward(reduce, g, gain, weights, kept):
    rows, width = g.shape
    w_qkv, w_out, w_up, w_dn = weights
    cols, half = w_qkv.shape[-1], w_up.shape[-1]
    shape = jax.ShapeDtypeStruct
    wide = (rows, width)
    block = width // GROUP
    ins = dict(
        g_in=g, gain=(gain, VMEM),
        qkv_own=w_qkv, out_own=w_out, up_own=w_up, dn_own=w_dn,
        qkv_oth=kept.qkv_oth, out_oth=kept.out_oth, up_oth=kept.up_oth, dn_oth=kept.dn_oth,
        h1=kept.h1_out, xh1=kept.xh1_out, r1=kept.r1_out, qkv=kept.qkv_out, p=kept.p_out, o=kept.o_out,
        h2=kept.h2_out, xh2=kept.xh2_out, r2=kept.r2_out, a=kept.a_out, d=kept.d_out,
    )
    outs = dict(g_out=shape(wide, F32))
    recv = lambda k: VMEM((8, GROUP >> (k + 1), block, cols), BF16)
    scratch = dict(
        g=VMEM(wide, F32), dh=VMEM(wide, F32), spread=VMEM((rows, 128), F32),
        sums=VMEM((8, 8, width), F32), flat=VMEM((8, width), F32),
        sem=pltpu.SemaphoreType.DMA((96,)),
        grad=VMEM((8, GROUP, block, cols), BF16),
    )
    scratch.update({f"{SLOT}{i}": VMEM(wide, BF16) for i in range(15)})
    if not reduce:
        outs.update(flat_out=shape((8, width), F32), grad_out=shape((2, 8, GROUP, block, cols), BF16))
    else:
        copies = 16 * 4 + GROUP
        part = lambda *dims: shape((2, *dims), F32)
        outs.update(
            dn_out=part(block, half), up_out=part(block, half), out_out=part(block, cols),
            qkv_out=part(3, block, cols), flat_out=shape((8, 128), F32),
        )
        scratch.update(
            send=pltpu.SemaphoreType.DMA((copies,)), recv=pltpu.SemaphoreType.DMA((copies,)),
            r0=recv(0), r1_=recv(1), r2_=recv(2), r3=recv(3), final=VMEM((16, block, cols), F32),
            slots=VMEM((GROUP, 8, 128), F32), flat_f=VMEM((8, 128), F32),
        )
    flops = 4 * rows * (2 * 6 * cols * width + 3 * cols * width + 6 * half * width)
    return call(
        functools.partial(backward_kernel, reduce), ins, outs, scratch,
        "backward", 1 if reduce else None, flops,
    )


def local(n_dp, tokens, lengths, w_qkv, w_out, w_up, w_down, norm_gain, norm_bias, cotangent):
    rows, width = tokens.shape
    cols = w_qkv.shape[3]
    items = lengths.shape[1]
    order = jnp.arange(items, dtype=jnp.int32)
    ends = jnp.sum(jnp.where(order[:, None] >= order[None, :], lengths, 0), axis=1)
    place = jnp.arange(rows, dtype=jnp.int32)
    start = jnp.max(jnp.where(ends[None, :] <= place[:, None], ends[None, :], 0), axis=1)
    window = jnp.maximum(place // TILE - 1, 0) * TILE
    key = window[:, None] + jnp.arange(2 * TILE, dtype=jnp.int32)[None, :]
    allowed = (key >= start[:, None]) & (key <= place[:, None])
    bias = jnp.where(allowed, 0.0, MASKED).astype(F32)

    weights = (jnp.transpose(w_qkv, (0, 2, 1, 3)), w_out, w_up, w_down)
    kept = forward(tokens, bias, norm_gain, norm_bias, weights)
    reduce = n_dp == GROUP
    back = backward(reduce, cotangent, norm_gain, weights, kept)
    if reduce:
        qkv, out, up, dn = back.qkv_out, back.out_out, back.up_out, back.dn_out
        side = lax.rem(lax.axis_index("dp"), 2)
        block = width // GROUP
        flat = back.flat_out.reshape(2, 4, 128)
        flat = lax.dynamic_slice_in_dim(flat, side * block, block, axis=2)
    else:

        def total(*parts):
            layers = []
            for layer in range(2):
                found = []
                for i in parts:
                    n = 8 * (1 - layer) + i
                    places = [position(d, BACKWARD_ORDERS[n]) for d in range(GROUP)]
                    piece = back.grad_out[layer, i].astype(F32)
                    found.append(jnp.concatenate([piece[at] for at in places]))
                layers.append(jnp.concatenate(found, axis=1))
            return lax.psum_scatter(jnp.stack(layers), "dp", scatter_dimension=1, tiled=True)

        dn, up, out = total(0, 1), total(2, 3), total(4)
        qkv = jnp.stack([total(5), total(6), total(7)], axis=1)
        flat = back.flat_out.reshape(2, 4, width)
        flat = lax.psum_scatter(flat, "dp", scatter_dimension=2, tiled=True)
    gain, shift = flat[:, :2], flat[:, 2:]
    qkv = jnp.transpose(qkv, (0, 2, 1, 3))
    return (kept.y_out, back.g_out, qkv, out, up, dn, gain, shift)


def solution(mesh):
    placed = (
        P("dp", None),
        P("dp", None),
        P(None, None, None, "tensor"),
        P(None, None, "tensor"),
        P(None, None, "tensor"),
        P(None, None, "tensor"),
        P(),
        P(),
        P("dp", None),
    )
    return jax.shard_map(
        functools.partial(local, mesh.shape["dp"]),
        mesh=mesh,
        in_specs=placed,
        out_specs=(
            P("dp", None),
            P("dp", None),
            P(None, "dp", None, "tensor"),
            P(None, "dp", "tensor"),
            P(None, "dp", "tensor"),
            P(None, "dp", "tensor"),
            P(None, None, "dp"),
            P(None, None, "dp"),
        ),
        check_vma=False,
    )
```

```python
import functools
from types import SimpleNamespace

import jax
import jax.numpy as jnp
from jax import lax
from jax.experimental import pallas as pl
from jax.experimental.pallas import tpu as pltpu
from jax.sharding import PartitionSpec as P

HEAD_DIM = 128
TILE = 64
EPS = 1e-05
MASKED = -1e30
MESH = pl.DeviceIdType.MESH
VMEM = pltpu.VMEM
ANY = pl.ANY
F32 = jnp.float32
BF16 = jnp.bfloat16
SCALE = HEAD_DIM**-0.5
VMEM_LIMIT = 62 << 20
SLOT = "L"
GROUP = 16
CHUNK = 256

FORWARD_ORDERS = ((2, 4, 1), (4, 2, 1), (2, 4, 1), (2, 4, 1), (4, 2, 1), (2, 4, 1), (4, 2, 1), (2, 4, 1), (2, 4, 1), (2, 1), (4, 2, 1), (4, 1), (2, 4, 1), (2, 1), (4, 1), (1,))
FORWARD_PLAN = ((0, 1, 2), (3, 4), (0, 5), (1, 6), (2, 7), (0, 3, 8), (1, 4), (), (2, 5), (3, 6), (0, 7, 4, 9, 1, 5, 0, 1), (2, 7, 8, 3, 4, 2, 6, 3), (4, 5, 8, 10, 5), (7, 11), (6, 9), (), (7,), (6,), (10, 12), (13,), (8, 11), (10, 12, 14, 9, 8), (9, 13), (10, 11), (12,), (10, 11, 15), (), (14,), (13,), (12,), (), (13,), (), (12,), (), (), (), (), (), (14,), (), (), (), (14,), (), (15,), (), (15,), (), (),)
BACKWARD_ORDERS = ((1, 2, 8, 4), (1, 8, 4, 2), (1, 4, 8, 2), (1, 2, 4, 8), (1, 2, 4, 8), (1, 4, 2, 8), (1, 2, 4, 8), (1, 2, 4, 8), (1, 2, 4, 8), (1, 2, 8, 4), (1, 4, 2, 8), (1, 2, 4, 8), (1, 2, 4, 8), (1, 2, 4, 8), (1, 8, 2, 4), (1, 2, 4, 8))
BACKWARD_PLAN = ((), (), (), (0,), (1,), (), (), (2,), (3,), (0,), (), (), (), (1, 2, 3), (), (), (), (4, 0), (1,), (), (), (), (5,), (2, 3, 6), (0, 7, 4), (1, 2), (5,), (6, 3), (4,), (), (7,), (8, 6), (9,), (4,), (7,), (10,), (5, 11, 8), (6,), (7,), (9,), (10,), (), (8,), (11,), (), (12,), (10,), (9,), (), (8, 11, 13), (), (14, 10, 9), (15, 12), (11,), (13,), (), (12, 15, 13, 14, 12, 15, 14, 13, 14, 15),)

ERFC = (
    0.22567586600780487,
    0.22566960752010345,
    0.20784251391887665,
    0.16854380071163177,
    0.14142295718193054,
    -0.005586510524153709,
    0.1690569967031479,
    -0.18288171291351318,
    0.05025661736726761,
)


def dot_nn(a, b):
    return lax.dot_general(a, b, (((1,), (0,)), ((), ())), preferred_element_type=F32)


def dot_nt(a, b):
    return lax.dot_general(a, b, (((1,), (1,)), ((), ())), preferred_element_type=F32)


def dot_tn(a, b):
    return lax.dot_general(a, b, (((0,), (0,)), ((), ())), preferred_element_type=F32)


def rows_at(index, size):
    return pl.ds(pl.multiple_of(index * size, size), size)


def own_rows(step):
    return slice(step * TILE, (step + 1) * TILE)


def key_rows(step):
    first = max(step - 1, 0) * TILE
    return slice(first, first + 2 * TILE)


def flip(value, bit):
    return value + bit * (1 - 2 * lax.rem(value // bit, 2))


def normalize(x):
    center = x - jnp.mean(x, axis=-1, keepdims=True)
    spread = lax.rsqrt(jnp.mean(center * center, axis=-1, keepdims=True) + EPS)
    return center * spread, spread


def gelu_parts(u):
    t = 1.0 / (1.0 + (0.4 * 0.7071067811865476) * jnp.abs(u))
    q = jnp.full_like(t, ERFC[-1])
    for c in ERFC[-2::-1]:
        q = q * t + c
    e = jnp.exp(-0.5 * (u * u))
    tail = 0.5 * (t * q) * e
    cdf = jnp.where(u >= 0, 1.0 - tail, tail)
    return u * cdf, cdf + u * (e * 0.3989422804014327)


class Copies:
    def __init__(self, sems):
        self.sems, self.n, self.open = sems, 0, []

    def start(self, src, dst):
        assert self.n < self.sems.shape[0]
        copy = pltpu.make_async_copy(src, dst, self.sems.at[self.n])
        self.n += 1
        copy.start()
        return copy

    def save(self, src, dst):
        self.open.append(self.start(src, dst))
        return self.open[-1]

    def settle(self, copy):
        self.open = [c for c in self.open if c is not copy]
        copy.wait()

    def finish(self):
        for copy in self.open:
            copy.wait()


class Remote:
    def __init__(self, send, recv):
        self.send, self.recv, self.n, self.sent = send, recv, 0, []

    def start(self, src, dst, device):
        assert self.n < self.send.shape[0]
        copy = pltpu.make_async_remote_copy(
            src_ref=src,
            dst_ref=dst,
            send_sem=self.send.at[self.n],
            recv_sem=self.recv.at[self.n],
            device_id=device,
            device_id_type=MESH,
        )
        self.n += 1
        copy.start()
        self.sent.append(copy)
        return copy

    def settle(self, copies):
        for copy in copies:
            copy.wait_send()
            self.sent = [c for c in self.sent if c is not copy]

    def finish(self):
        for copy in self.sent:
            copy.wait_send()


def greet(devices):
    barrier = pltpu.get_barrier_semaphore()
    for device in devices:
        pl.semaphore_signal(barrier, inc=1, device_id=device, device_id_type=MESH)
    pl.semaphore_wait(barrier, len(devices))


class Gather:
    def __init__(self, remote, own, other, order):
        self.remote, self.own, self.other, self.order = remote, own, other, order
        me, t = lax.axis_index("dp"), lax.axis_index("tensor")
        self.me, self.t = me, t
        self.have = [lax.rem(me, 8)]
        for bit in (1, 2, 4):
            if bit not in order:
                self.have += [flip(b, bit) for b in self.have]
        self.stage, self.flying, self.done = -1, [], False

    def block(self, ref, index):
        return ref.at[rows_at(index, ref.shape[0] // 8), :]

    def step(self):
        for copy in self.flying:
            copy.wait_recv()
        if self.stage == len(self.order):
            self.done = True
            return
        source = self.other
        if self.stage < 0:
            source, device = self.own, (self.me, 1 - self.t)
        else:
            if self.stage > 0:
                self.have = self.have + [flip(b, self.order[self.stage - 1]) for b in self.have]
            device = (flip(self.me, self.order[self.stage]), self.t)
        self.stage += 1
        self.flying = [
            self.remote.start(self.block(source, b), self.block(self.other, b), device)
            for b in self.have
        ]


class Scatter:
    def __init__(self, remote, grad, recvs, order, finish):
        self.remote, self.grad, self.recvs, self.order = remote, grad, recvs, order
        self.finish = finish
        self.me, self.t = lax.axis_index("dp"), lax.axis_index("tensor")
        self.base, self.count, self.stage, self.done, self.sent = 0, GROUP, -1, False, []

    def step(self):
        if self.stage >= 0:
            self.flying.wait_recv()
            recv = self.recvs[self.stage]
            if self.count == 1:
                self.finish(self.grad[self.base].astype(F32) + recv[0].astype(F32))
                self.done = True
                return

            def body(i, carry):
                at = self.base + i
                self.grad[at] = (self.grad[at].astype(F32) + recv[i].astype(F32)).astype(BF16)
                return carry

            lax.fori_loop(0, self.count, body, 0)
        self.stage += 1
        bit = self.order[self.stage]
        mine = lax.rem(self.me // bit, 2)
        half = self.count // 2
        out = self.base + (1 - mine) * half
        self.base = self.base + mine * half
        self.count = half
        self.flying = self.remote.start(
            self.grad.at[pl.ds(out, half)],
            self.recvs[self.stage],
            (flip(self.me, bit), self.t),
        )
        self.sent.append(self.flying)


def position(block, order):
    pos = 0
    for bit in order:
        pos = 2 * pos + block // bit % 2
    return pos


class Pump:
    def __init__(self, items, plan, before=None, after=None):
        self.items, self.plan, self.at = items, plan, 0
        self.before, self.after = before, after

    def step(self, i):
        if not self.items[i].done:
            if self.before is not None:
                self.before(i)
            self.items[i].step()
            if self.after is not None and self.items[i].done:
                self.after(i)

    def tick(self):
        if self.at < len(self.plan):
            for i in self.plan[self.at]:
                self.step(i)
        self.at += 1

    def need(self, i):
        while not self.items[i].done:
            self.step(i)


def pieces_of(layer, kind):
    return 2 if layer == 0 and kind < 4 else 1


def forward_kernel(names, *args):
    r = SimpleNamespace(**dict(zip(names, args)))
    copies = Copies(r.sem)
    remote = Remote(r.send, r.recv)
    me, t = lax.axis_index("dp"), lax.axis_index("tensor")
    rows, width = r.x.shape
    cols = r.qkv_own.shape[-1]
    heads = cols // HEAD_DIM
    half = r.up_own.shape[-1]
    pieces = width // cols
    x, qkv, wq = r.x, r.qkv, r.wq

    x_load = copies.start(r.x_in, r.x_raw)
    greet([(me, 1 - t), (flip(me, 2), t), (flip(me, 4), t), (flip(me, 1), t)])

    def stored(layer, kind, side):
        if kind < 3:
            return (r.qkv_oth if side else r.qkv_own).at[layer, kind]
        pair = ((r.out_own, r.out_oth), (r.up_own, r.up_oth), (r.dn_own, r.dn_oth))[kind - 3]
        return pair[side].at[layer]

    def buffer(kind, side):
        if kind < 3:
            return wq.at[3 * side + kind]
        return (r.wo, r.wu, r.wd)[kind - 3].at[side]

    parts = [
        (layer, kind, part)
        for layer in range(2)
        for kind in range(6)
        for part in range(pieces_of(layer, kind))
    ]

    def part_of(ref, layer, kind, part):
        size = ref.shape[0] // pieces_of(layer, kind)
        return ref.at[part * size : (part + 1) * size, :]

    gathers = [
        Gather(
            remote,
            part_of(stored(layer, kind, 0), layer, kind, part),
            part_of(stored(layer, kind, 1), layer, kind, part),
            FORWARD_ORDERS[i],
        )
        for i, (layer, kind, part) in enumerate(parts)
    ]
    loads, free = {}, {(kind, side): 0 for kind in range(6) for side in range(2)}

    def load_part(i):
        layer, kind, part = parts[i]
        if i not in loads and free[kind, 1] >= layer and gathers[i].done:
            loads[i] = copies.start(
                part_of(stored(layer, kind, 1), layer, kind, part),
                part_of(buffer(kind, 1), layer, kind, part),
            )

    def load(layer, kind, side):
        if side:
            for i, of in enumerate(parts):
                if of[:2] == (layer, kind):
                    load_part(i)
        elif (layer, kind) not in loads and free[kind, 0] >= layer:
            loads[layer, kind] = copies.start(stored(layer, kind, 0), buffer(kind, 0))

    pump = Pump(gathers, FORWARD_PLAN, after=load_part)

    def get(layer, kind, side):
        mine = [i for i, of in enumerate(parts) if of[:2] == (layer, kind)] if side else []
        for i in mine:
            pump.need(i)
        load(layer, kind, side)
        for i in mine if side else [(layer, kind)]:
            loads[i].wait()

    def used(kind, side):
        free[kind, side] += 1
        if free[kind, side] < 2:
            load(free[kind, side], kind, side)

    pump.tick()
    for kind in range(3):
        load(0, kind, 0)
    for kind in range(3, 6):
        load(0, kind, 0)
    pump.tick()
    saves = {}

    def save(src, dst, part=None):
        saves[id(src)] = copies.save(src if part is None else src.at[part], dst)

    def reuse(src):
        if id(src) in saves:
            copies.settle(saves.pop(id(src)))

    def norm(layer, which, h, xh, spread, source=None):
        gain = r.gain[layer, which : which + 1, :]
        shift = r.shift[layer, which : which + 1, :]
        for ref in (h, xh, spread):
            reuse(ref)

        def body(i, carry):
            at = rows_at(i, CHUNK)
            if source is not None:
                values = source[at, :].astype(F32)
                x[at, :] = values
            else:
                values = x[at, :]
            hat, rs = normalize(values)
            xh[at, :] = hat.astype(BF16)
            h[at, :] = (hat * gain + shift).astype(BF16)
            spread[at, :] = jnp.broadcast_to(rs, (CHUNK, HEAD_DIM))
            return carry

        lax.fori_loop(0, rows // CHUNK, body, 0)

    def project(layer, side):
        for kind in range(3):
            get(layer, kind, side)
            j = 3 * side + kind
            qkv[j] = dot_nn(r.h1[...], wq[j]).astype(BF16)
            used(kind, side)
            pump.tick()

    def attend(group):
        q_ref, k_ref, v_ref = (qkv.at[3 * group + j] for j in range(3))
        steps = range(rows // TILE)
        for head in range(heads):
            c = slice(head * HEAD_DIM, (head + 1) * HEAD_DIM)
            s = [
                dot_nt(q_ref[own_rows(i), c], k_ref[key_rows(i), c]) * SCALE + r.mask[own_rows(i), :]
                for i in steps
            ]
            top = [jnp.max(v, axis=-1, keepdims=True) for v in s]
            e = [jnp.exp(v - m) for v, m in zip(s, top)]
            total = [jnp.sum(v, axis=-1, keepdims=True) for v in e]
            p = [(v * (1.0 / m)).astype(BF16) for v, m in zip(e, total)]
            mixed = [dot_nn(v, v_ref[key_rows(i), c]) for v, i in zip(p, steps)]
            for i in steps:
                r.p[group, own_rows(i), c] = p[i]
                r.o[group, own_rows(i), c] = mixed[i].astype(BF16)
            pump.tick()

    def add_product(ref, weight, side):
        def body(n, carry):
            at = rows_at(n, cols)
            x[:, at] += dot_nt(ref[side], weight[side, at, :])
            return carry

        lax.fori_loop(0, pieces, body, 0)

    def up(layer, side):
        get(layer, 4, side)
        for n in range(half // cols):
            at = slice(n * cols, (n + 1) * cols)
            r.u[...] = dot_nn(r.h2[...], r.wu[side, :, at])

            def inner(i, carry):
                i_at = rows_at(i, CHUNK // 2)
                a, d = gelu_parts(r.u[i_at, :])
                r.a[side, i_at, at] = a.astype(BF16)
                r.d[side, i_at, at] = d.astype(BF16)
                return carry

            lax.fori_loop(0, 2 * rows // CHUNK, inner, 0)
            pump.tick()
        used(4, side)

    items = r.lengths.shape[1]
    counts = jnp.broadcast_to(r.lengths[...].astype(F32), (8, items)).astype(BF16)
    earlier = lax.broadcasted_iota(jnp.int32, (items, items), 0)
    upto = jnp.where(earlier <= lax.broadcasted_iota(jnp.int32, (items, items), 1), 1.0, 0.0)
    ends = dot_nn(counts, upto.astype(BF16))[0:1, :].astype(jnp.int32)

    def make_mask(i, carry):
        place = i * CHUNK + lax.broadcasted_iota(jnp.int32, (CHUNK, 1), 0)
        start = jnp.max(jnp.where(ends <= place, ends, 0), axis=1, keepdims=True)
        key = jnp.maximum(place // TILE - 1, 0) * TILE
        key = key + lax.broadcasted_iota(jnp.int32, (CHUNK, 2 * TILE), 1)
        allowed = (key >= start) & (key <= place)
        r.mask[rows_at(i, CHUNK), :] = jnp.where(allowed, 0.0, MASKED)
        return carry

    lax.fori_loop(0, rows // CHUNK, make_mask, 0)
    x_load.wait()
    for layer in range(2):
        norm(layer, 0, r.h1, r.xh1, r.r1, None if layer else r.x_raw)
        save(r.h1, r.h1_out.at[layer])
        save(r.xh1, r.xh1_out.at[layer])
        save(r.r1, r.r1_out.at[layer])
        pump.tick()
        for ref in (qkv, r.o, r.p):
            reuse(ref)
        project(layer, 0)
        attend(0)
        get(layer, 3, 0)
        add_product(r.o, r.wo, 0)
        used(3, 0)
        pump.tick()
        project(layer, 1)
        save(qkv, r.qkv_out.at[layer])
        attend(1)
        save(r.p, r.p_out.at[layer])
        save(r.o, r.o_out.at[layer], 0)
        get(layer, 3, 1)
        add_product(r.o, r.wo, 1)
        used(3, 1)
        pump.tick()
        norm(layer, 1, r.h2, r.xh2, r.r2)
        save(r.h2, r.h2_out.at[layer])
        save(r.xh2, r.xh2_out.at[layer])
        save(r.r2, r.r2_out.at[layer])
        pump.tick()
        reuse(r.a)
        reuse(r.d)
        up(layer, 0)
        up(layer, 1)
        save(r.a, r.a_out.at[layer], 0)
        save(r.d, r.d_out.at[layer])
        for side in range(2):
            get(layer, 5, side)
            add_product(r.a, r.wd, side)
            used(5, side)
            pump.tick()

    def finish(i, carry):
        at = rows_at(i, CHUNK)
        r.x_raw[at, :] = x[at, :].astype(BF16)
        return carry

    lax.fori_loop(0, rows // CHUNK, finish, 0)
    copies.save(r.x_raw, r.y_out)
    copies.finish()
    remote.finish()


def backward_kernel(reduce, names, *args):
    r = SimpleNamespace(**dict(zip(names, args)))
    copies = Copies(r.sem)
    me, t = lax.axis_index("dp"), lax.axis_index("tensor")
    g, dh = r.g, r.dh
    L = [v for k, v in zip(names, args) if k[0] == SLOT]
    rows, width = g.shape
    cols = r.qkv_own.shape[-1]
    heads = cols // HEAD_DIM
    half = r.up_own.shape[-1]
    pieces = width // cols
    halves = [slice(i * cols, (i + 1) * cols) for i in range(pieces)]

    def target(layer, i):
        if i < 2:
            return r.dn_out.at[layer, :, halves[i]]
        if i < 4:
            return r.up_out.at[layer, :, halves[i - 2]]
        return r.out_out.at[layer] if i == 4 else r.qkv_out.at[layer, i - 5]

    if reduce:
        remote = Remote(r.send, r.recv)
        low = lax.rem(me, GROUP)
        greet([(me - low + lax.rem(low + o, GROUP), t) for o in range(1, GROUP)])

        def ending(n):
            def finish(value):
                r.final[n] = value
                copies.save(r.final.at[n], target(1 - n // 8, n % 8))

            return finish

        pump = Pump(
            [
                Scatter(
                    remote, r.grad.at[n % 8], [ref.at[n % 8] for ref in (r.r0, r.r1_, r.r2_, r.r3)],
                    BACKWARD_ORDERS[n], ending(n),
                )
                for n in range(16)
            ],
            BACKWARD_PLAN,
            before=lambda n: order_layers(n),
        )

        def order_layers(n):
            if n < 8 or pump.items[n].stage == 3:
                return
            bit = BACKWARD_ORDERS[n][pump.items[n].stage + 1]
            for m in range(8):
                while not pump.items[m].done and (
                    BACKWARD_ORDERS[m].index(bit) >= pump.items[m].stage
                ):
                    pump.step(m)

        tick = pump.tick
    else:
        tick = lambda: None
        spare = []

    g_load = copies.start(r.g_in, L[0])

    def load_first(layer):
        wd = [copies.start(r.dn_own.at[layer], L[3]), copies.start(r.dn_oth.at[layer], L[4])]
        d = [copies.start(r.d.at[layer, i], L[5 + i]) for i in range(2)]
        return wd, d

    def load_second(layer, a):
        a = a or copies.start(r.a.at[layer], L[7])
        wu = [copies.start(r.up_own.at[layer], L[9]), copies.start(r.up_oth.at[layer], L[10])]
        wo = [
            copies.start(r.out_own.at[layer], L[12].at[:, halves[0]]),
            copies.start(r.out_oth.at[layer], L[12].at[:, halves[1]]),
        ]
        return a, wu, wo

    def load_third(layer):
        h2 = copies.start(r.h2.at[layer], L[8])
        o = copies.start(r.o.at[layer], L[13].at[:, halves[0]])
        p = [copies.start(r.p.at[layer, i], L[14].at[:, halves[i]]) for i in range(2)]
        return h2, o, p

    def load_norm(layer, which):
        pair = ((r.xh1, r.r1), (r.xh2, r.r2))[which]
        return [copies.start(pair[0].at[layer], L[11]), copies.start(pair[1].at[layer], r.spread)]

    a_first = copies.start(r.a.at[1], L[7])
    first = load_first(1)
    second = load_second(1, a_first)
    third = load_third(1)
    norm_load = load_norm(1, 1)

    def zero(i, carry):
        r.sums[i] = jnp.zeros((8, width), F32)
        return carry

    lax.fori_loop(0, 8, zero, 0)
    g_load.wait()

    def begin(i, carry):
        at = rows_at(i, CHUNK)
        g[at, :] = L[0][at, :].astype(F32)
        return carry

    lax.fori_loop(0, rows // CHUNK, begin, 0)

    def weight_grad(n, lhs, rhs):
        if reduce:
            if n >= 8:
                pump.need(n - 8)
                remote.settle(pump.items[n - 8].sent)
        elif n >= 8:
            copies.settle(spare[n - 8])
        full = dot_tn(lhs, rhs)
        size = width // GROUP
        for d in range(GROUP):
            r.grad[n % 8, position(d, BACKWARD_ORDERS[n])] = full[d * size : (d + 1) * size].astype(
                BF16
            )
        if not reduce:
            spare.append(copies.save(r.grad.at[n % 8], r.grad_out.at[1 - n // 8, n % 8]))
            return
        pump.step(n)
        tick()

    def norm_back(layer, which, loads):
        gain = r.gain[layer, which : which + 1, :]
        row = 4 * layer + which
        for load in loads:
            load.wait()

        def body(i, carry):
            at = rows_at(i, CHUNK)
            hat = L[11][at, :].astype(F32)
            grad = dh[at, :]
            rs = r.spread[at, 0:1]
            e = grad * gain
            prod = grad * hat
            m1 = jnp.mean(e, axis=-1, keepdims=True)
            m2 = jnp.mean(e * hat, axis=-1, keepdims=True)
            new = g[at, :] + rs * (e - m1 - hat * m2)
            g[at, :] = new
            L[0][at, :] = new.astype(BF16)
            r.sums[row] += jnp.sum(prod.reshape(CHUNK // 8, 8, width), axis=0)
            r.sums[row + 2] += jnp.sum(grad.reshape(CHUNK // 8, 8, width), axis=0)
            return carry

        lax.fori_loop(0, rows // CHUNK, body, 0)

    to = [(1, 0), (1, 1), (2, 0), (2, 1), (7, 0), (7, 1)]

    def attend(group):
        n = 3 * group
        steps = range(rows // TILE)
        for head in range(heads):
            c = [
                slice(side * cols + head * HEAD_DIM, side * cols + (head + 1) * HEAD_DIM)
                for side in range(pieces)
            ]
            mine = c[group]
            q = [L[3 + n // 2][own_rows(i), c[n % 2]] for i in steps]
            k = [L[3 + (n + 1) // 2][key_rows(i), c[(n + 1) % 2]] for i in steps]
            v = [L[3 + (n + 2) // 2][key_rows(i), c[(n + 2) % 2]] for i in steps]
            do = [L[6][own_rows(i), mine] for i in steps]
            p = [L[14][own_rows(i), mine] for i in steps]
            dp = [dot_nt(x, y) for x, y in zip(do, v)]
            wide_p = [x.astype(F32) for x in p]
            inner = [jnp.sum(x * y, axis=-1, keepdims=True) for x, y in zip(dp, wide_p)]
            ds = [(y * (x - z)).astype(BF16) for x, y, z in zip(dp, wide_p, inner)]
            dq = [dot_nn(x, y) for x, y in zip(ds, k)]
            dk = [dot_tn(x, y) for x, y in zip(ds, q)]
            dv = [dot_tn(x, y) for x, y in zip(p, do)]
            (sq, hq), (sk, hk), (sv, hv) = to[n : n + 3]
            for i in steps:
                L[sq][own_rows(i), c[hq]] = (dq[i] * SCALE).astype(BF16)
                if i == 0:
                    own_k, own_v = dk[0][:TILE], dv[0][:TILE]
                else:
                    own_k, own_v = dk[i][TILE:], dv[i][TILE:]
                if i + 1 < len(steps):
                    own_k = own_k + dk[i + 1][:TILE]
                    own_v = own_v + dv[i + 1][:TILE]
                L[sk][own_rows(i), c[hk]] = (own_k * SCALE).astype(BF16)
                L[sv][own_rows(i), c[hv]] = own_v.astype(BF16)
            tick()

    for layer in (1, 0):
        base = 8 * (1 - layer)
        wd_load, d_load = first
        a_load, wu_load, wo_load = second
        h2_load, o_load, p_load = third
        a_load.wait()
        for i in range(2):
            weight_grad(base + i, L[0][...], L[7][:, halves[i]])
        for i in range(2):
            wd_load[i].wait()
            d_load[i].wait()
            for at in halves:
                da = dot_nn(L[0][...], L[3 + i][:, at])
                L[1 + i][:, at] = (da * L[5 + i][:, at].astype(F32)).astype(BF16)
                tick()
            if i == 0:
                h2_load.wait()
                for j in range(2):
                    weight_grad(base + 2 + j, L[8][...], L[1][:, halves[j]])
        qkv_load = [
            copies.start(r.qkv.at[layer, j], L[3 + j // 2].at[:, halves[j % 2]]) for j in range(6)
        ]
        h1_load = copies.start(r.h1.at[layer], L[8])
        for load in wu_load:
            load.wait()
        for at in halves:
            dh[:, at] = dot_nt(L[1][...], L[9][at, :]) + dot_nt(L[2][...], L[10][at, :])
            tick()

        def load_wq(some):
            return [
                copies.start(
                    r.qkv_own.at[layer, j] if j < 3 else r.qkv_oth.at[layer, j - 3],
                    L[(9, 10, 12)[j // 2]].at[:, halves[j % 2]],
                )
                for j in some
            ]

        wq_load = load_wq(range(4))
        norm_back(layer, 1, norm_load)
        norm_load = load_norm(layer, 0)
        tick()
        for i in range(2):
            wo_load[i].wait()
            L[6][:, halves[i]] = dot_nn(L[0][...], L[12][:, halves[i]]).astype(BF16)
            tick()
        wq_load += load_wq(range(4, 6))
        o_load.wait()
        weight_grad(base + 4, L[0][...], L[13][:, halves[0]])
        for load in (*qkv_load, *p_load):
            load.wait()
        attend(0)
        h1_load.wait()
        for j in range(3):
            slot, side = to[j]
            weight_grad(base + 5 + j, L[8][...], L[slot][:, halves[side]])
        attend(1)
        if layer == 1:
            first = load_first(0)
            third = load_third(0)
        for load in wq_load:
            load.wait()
        for at in halves:
            dh[:, at] = (
                dot_nt(L[1][...], L[9][at, :])
                + dot_nt(L[2][...], L[10][at, :])
                + dot_nt(L[7][...], L[12][at, :])
            )
            tick()
        if layer == 1:
            second = load_second(0, None)
        norm_back(layer, 0, norm_load)
        if layer == 1:
            norm_load = load_norm(0, 1)
        tick()
    copies.save(g, r.g_out)
    for k in range(8):
        r.flat[k : k + 1, :] = jnp.sum(r.sums[k], axis=0, keepdims=True)
    if not reduce:
        copies.save(r.flat, r.flat_out)
        copies.finish()
        return
    sends = []
    for o in range(1, GROUP):
        to_dev = lax.rem(low + o, GROUP)
        sends.append(
            remote.start(
                r.flat.at[:, rows_at(to_dev // 2, 128)], r.slots.at[o], (me - low + to_dev, t)
            )
        )
    tick()
    while pump.at < len(BACKWARD_PLAN):
        tick()
    for n in range(16):
        pump.need(n)
    total = r.flat[:, rows_at(low // 2, 128)]
    for o, copy in enumerate(sends):
        copy.wait_recv()
        total = total + r.slots[o + 1]
    r.flat_f[...] = total
    copies.save(r.flat_f, r.flat_out)
    copies.finish()
    remote.finish()


def call(kernel, ins, outs, scratch, name, collective, flops):
    split = lambda v: v if isinstance(v, tuple) else (v, ANY)
    in_items = {k: split(v) for k, v in ins.items()}
    out_items = {k: split(v) for k, v in outs.items()}
    names = (*in_items, *out_items, *scratch)
    params = dict(vmem_limit_bytes=VMEM_LIMIT, has_side_effects=True)
    if collective is not None:
        params.update(collective_id=collective)
    made = pl.pallas_call(
        functools.partial(kernel, names),
        out_shape=tuple(v for v, _ in out_items.values()),
        in_specs=[pl.BlockSpec(memory_space=s) for _, s in in_items.values()],
        out_specs=tuple(pl.BlockSpec(memory_space=s) for _, s in out_items.values()),
        scratch_shapes=list(scratch.values()),
        compiler_params=pltpu.CompilerParams(**params),
        cost_estimate=pl.CostEstimate(flops=flops, bytes_accessed=60 << 20, transcendentals=0),
        name=name,
    )(*(v for v, _ in in_items.values()))
    return SimpleNamespace(**dict(zip(out_items, made)))


def forward(x, lengths, gain, shift, weights):
    rows, width = x.shape
    w_qkv, w_out, w_up, w_dn = weights
    cols, half = w_qkv.shape[-1], w_up.shape[-1]
    shape = jax.ShapeDtypeStruct
    wide, slab = (rows, width), (rows, cols)
    like = lambda w: shape(w.shape, BF16)
    two = lambda *dims, dtype=BF16: shape((2, *dims), dtype)
    ins = dict(
        x_in=x, lengths=(lengths, VMEM), gain=(gain, VMEM), shift=(shift, VMEM),
        qkv_own=w_qkv, out_own=w_out, up_own=w_up, dn_own=w_dn,
    )
    outs = dict(
        qkv_oth=like(w_qkv), out_oth=like(w_out), up_oth=like(w_up), dn_oth=like(w_dn),
        h1_out=two(*wide), xh1_out=two(*wide), r1_out=two(rows, 128, dtype=F32),
        qkv_out=two(6, *slab), p_out=two(2, *slab), o_out=two(*slab),
        h2_out=two(*wide), xh2_out=two(*wide), r2_out=two(rows, 128, dtype=F32),
        a_out=two(rows, half), d_out=two(2, rows, half),
        y_out=shape(wide, BF16),
    )
    copies = 16 * 8
    scratch = dict(
        x=VMEM(wide, F32), x_raw=VMEM(wide, BF16),
        h1=VMEM(wide, BF16), xh1=VMEM(wide, BF16), r1=VMEM((rows, 128), F32),
        h2=VMEM(wide, BF16), xh2=VMEM(wide, BF16), r2=VMEM((rows, 128), F32),
        qkv=VMEM((6, *slab), BF16), o=VMEM((2, *slab), BF16), p=VMEM((2, *slab), BF16),
        mask=VMEM((rows, 128), F32), u=VMEM(slab, F32),
        a=VMEM((2, rows, half), BF16), d=VMEM((2, rows, half), BF16),
        wq=VMEM((6, width, cols), BF16), wo=VMEM((2, width, cols), BF16),
        wu=VMEM((2, width, half), BF16), wd=VMEM((2, width, half), BF16),
        sem=pltpu.SemaphoreType.DMA((80,)),
        send=pltpu.SemaphoreType.DMA((copies,)), recv=pltpu.SemaphoreType.DMA((copies,)),
    )
    flops = 4 * rows * (6 * cols * width + 2 * cols * width + 4 * half * width)
    return call(forward_kernel, ins, outs, scratch, "forward", 0, flops)


def backward(reduce, g, gain, weights, kept):
    rows, width = g.shape
    w_qkv, w_out, w_up, w_dn = weights
    cols, half = w_qkv.shape[-1], w_up.shape[-1]
    shape = jax.ShapeDtypeStruct
    wide = (rows, width)
    block = width // GROUP
    ins = dict(
        g_in=g, gain=(gain, VMEM),
        qkv_own=w_qkv, out_own=w_out, up_own=w_up, dn_own=w_dn,
        qkv_oth=kept.qkv_oth, out_oth=kept.out_oth, up_oth=kept.up_oth, dn_oth=kept.dn_oth,
        h1=kept.h1_out, xh1=kept.xh1_out, r1=kept.r1_out, qkv=kept.qkv_out, p=kept.p_out, o=kept.o_out,
        h2=kept.h2_out, xh2=kept.xh2_out, r2=kept.r2_out, a=kept.a_out, d=kept.d_out,
    )
    outs = dict(g_out=shape(wide, F32))
    recv = lambda k: VMEM((8, GROUP >> (k + 1), block, cols), BF16)
    scratch = dict(
        g=VMEM(wide, F32), dh=VMEM(wide, F32), spread=VMEM((rows, 128), F32),
        sums=VMEM((8, 8, width), F32), flat=VMEM((8, width), F32),
        sem=pltpu.SemaphoreType.DMA((96,)),
        grad=VMEM((8, GROUP, block, cols), BF16),
    )
    scratch.update({f"{SLOT}{i}": VMEM(wide, BF16) for i in range(15)})
    if not reduce:
        outs.update(flat_out=shape((8, width), F32), grad_out=shape((2, 8, GROUP, block, cols), BF16))
    else:
        copies = 16 * 4 + GROUP
        part = lambda *dims: shape((2, *dims), F32)
        outs.update(
            dn_out=part(block, half), up_out=part(block, half), out_out=part(block, cols),
            qkv_out=part(3, block, cols), flat_out=shape((8, 128), F32),
        )
        scratch.update(
            send=pltpu.SemaphoreType.DMA((copies,)), recv=pltpu.SemaphoreType.DMA((copies,)),
            r0=recv(0), r1_=recv(1), r2_=recv(2), r3=recv(3), final=VMEM((16, block, cols), F32),
            slots=VMEM((GROUP, 8, 128), F32), flat_f=VMEM((8, 128), F32),
        )
    flops = 4 * rows * (2 * 6 * cols * width + 3 * cols * width + 6 * half * width)
    return call(
        functools.partial(backward_kernel, reduce), ins, outs, scratch,
        "backward", 1 if reduce else None, flops,
    )


def deliver_kernel(block, *args):
    ins, outs, held, sems = args[:6], args[7:13], args[15:21], args[21]
    parts = []
    for n, ref in enumerate(ins):
        pieces = 4 if ref.shape[0] > 2 else 2
        size = ref.shape[0] // pieces
        parts += [(n, slice(i * size, (i + 1) * size)) for i in range(pieces)]
    arrive = [
        pltpu.make_async_copy(ins[n].at[at], held[n].at[at], sems.at[0, k])
        for k, (n, at) in enumerate(parts)
    ]
    leave = [
        pltpu.make_async_copy(held[n].at[at], outs[n].at[at], sems.at[1, k])
        for k, (n, at) in enumerate(parts)
    ]
    for copy in arrive:
        copy.start()
    flat = args[6][...]
    odd = lax.rem(lax.axis_index("dp"), 2) == 1
    flat = jnp.where(odd, flat[:, block : 2 * block], flat[:, :block])
    for layer in range(2):
        args[13][layer] = flat[4 * layer : 4 * layer + 2]
        args[14][layer] = flat[4 * layer + 2 : 4 * layer + 4]
    for come, go in zip(arrive, leave):
        come.wait()
        go.start()
    for copy in leave:
        copy.wait()


def deliver(kept, back):
    given = (kept.y_out, back.g_out, back.qkv_out, back.out_out, back.up_out, back.dn_out)
    shape = jax.ShapeDtypeStruct
    block = kept.y_out.shape[1] // GROUP
    small = shape((2, 2, block), F32)
    return pl.pallas_call(
        functools.partial(deliver_kernel, block),
        out_shape=(*(shape(v.shape, v.dtype) for v in given), small, small),
        in_specs=[pl.BlockSpec(memory_space=ANY)] * 6 + [pl.BlockSpec(memory_space=VMEM)],
        out_specs=(*[pl.BlockSpec(memory_space=ANY)] * 6, *[pl.BlockSpec(memory_space=VMEM)] * 2),
        scratch_shapes=[VMEM(v.shape, v.dtype) for v in given] + [pltpu.SemaphoreType.DMA((2, 16))],
        compiler_params=pltpu.CompilerParams(vmem_limit_bytes=VMEM_LIMIT),
        name="deliver",
    )(*given, back.flat_out)


def local(n_dp, tokens, lengths, w_qkv, w_out, w_up, w_down, norm_gain, norm_bias, cotangent):
    rows, width = tokens.shape
    cols = w_qkv.shape[3]
    weights = (jnp.transpose(w_qkv, (0, 2, 1, 3)), w_out, w_up, w_down)
    kept = forward(tokens, lengths, norm_gain, norm_bias, weights)
    reduce = n_dp == GROUP
    back = backward(reduce, cotangent, norm_gain, weights, kept)
    if reduce:
        y, grad, qkv, out, up, dn, gain, shift = deliver(kept, back)
        return (y, grad, jnp.transpose(qkv, (0, 2, 1, 3)), out, up, dn, gain, shift)

    def total(*parts):
        layers = []
        for layer in range(2):
            found = []
            for i in parts:
                n = 8 * (1 - layer) + i
                places = [position(d, BACKWARD_ORDERS[n]) for d in range(GROUP)]
                piece = back.grad_out[layer, i].astype(F32)
                found.append(jnp.concatenate([piece[at] for at in places]))
            layers.append(jnp.concatenate(found, axis=1))
        return lax.psum_scatter(jnp.stack(layers), "dp", scatter_dimension=1, tiled=True)

    dn, up, out = total(0, 1), total(2, 3), total(4)
    qkv = jnp.stack([total(5), total(6), total(7)], axis=1)
    flat = back.flat_out.reshape(2, 4, width)
    flat = lax.psum_scatter(flat, "dp", scatter_dimension=2, tiled=True)
    gain, shift = flat[:, :2], flat[:, 2:]
    qkv = jnp.transpose(qkv, (0, 2, 1, 3))
    return (kept.y_out, back.g_out, qkv, out, up, dn, gain, shift)


def solution(mesh):
    placed = (
        P("dp", None),
        P("dp", None),
        P(None, None, None, "tensor"),
        P(None, None, "tensor"),
        P(None, None, "tensor"),
        P(None, None, "tensor"),
        P(),
        P(),
        P("dp", None),
    )
    return jax.shard_map(
        functools.partial(local, mesh.shape["dp"]),
        mesh=mesh,
        in_specs=placed,
        out_specs=(
            P("dp", None),
            P("dp", None),
            P(None, "dp", None, "tensor"),
            P(None, "dp", "tensor"),
            P(None, "dp", "tensor"),
            P(None, "dp", "tensor"),
            P(None, None, "dp"),
            P(None, None, "dp"),
        ),
        check_vma=False,
    )
```

```python
import functools
from types import SimpleNamespace

import jax
import jax.numpy as jnp
from jax import lax
from jax.experimental import pallas as pl
from jax.experimental.pallas import tpu as pltpu
from jax.sharding import PartitionSpec as P

HEAD_DIM = 128
TILE = 64
EPS = 1e-05
MASKED = -1e30
MESH = pl.DeviceIdType.MESH
VMEM = pltpu.VMEM
ANY = pl.ANY
F32 = jnp.float32
BF16 = jnp.bfloat16
SCALE = HEAD_DIM**-0.5
VMEM_LIMIT = 62 << 20
SLOT = "L"
HEADS_AT_ONCE = 2
GROUP = 16
CHUNK = 256

FORWARD_ORDERS = ((2, 4, 1), (2, 4, 1), (4, 2, 1), (4, 2, 1), (2, 4, 1), (4, 2, 1), (4, 2, 1), (2, 4, 1), (2, 4, 1), (4, 2, 1), (2, 4, 1), (4, 2, 1), (2, 1), (4, 2, 1), (4, 1), (1,))
FORWARD_PLAN = ((0, 1, 2), (3, 4), (0, 1, 5), (2, 6), (3, 7), (0, 4, 8), (1, 2, 5), (3,), (4, 6, 7, 0, 2, 9, 0, 1, 2, 5, 3, 8, 1), (3, 7, 10), (4, 5, 6, 11, 9, 7, 12, 4, 5), (7, 8, 10), (), (11, 13, 6, 9, 6), (10, 12, 14), (), (13, 8, 9, 11, 15, 8), (), (9, 14), (10, 12), (13,), (10,), (11, 12), (), (), (11,), (13,), (), (), (13, 14), (), (), (), (14,), (15,), (), (), (15,), (),)
BACKWARD_ORDERS = ((1, 4, 8, 2), (1, 2, 8, 4), (1, 2, 8, 4), (1, 2, 4, 8), (1, 2, 8, 4), (1, 2, 4, 8), (1, 2, 4, 8), (1, 4, 2, 8), (1, 2, 4, 8), (1, 2, 8, 4), (1, 2, 4, 8), (1, 4, 2, 8), (1, 2, 8, 4), (1, 2, 8, 4), (1, 2, 4, 8), (1, 4, 2, 8))
BACKWARD_PLAN = ((), (), (), (0,), (1,), (), (), (2,), (3, 0), (1,), (), (), (2,), (0,), (), (4,), (3, 0), (1,), (5,), (6, 7, 3, 2), (4, 1), (5,), (7,), (), (2, 3, 6), (8,), (9,), (4, 5), (), (10, 6), (11, 7, 8), (5,), (), (6, 9), (), (11,), (10,), (12, 8), (), (11,), (13, 9, 10), (14, 15, 8), (12, 9, 11), (10, 13), (15, 14, 12, 15, 14, 12, 13, 15, 13, 14),)

ERFC = (
    0.22567586600780487,
    0.22566960752010345,
    0.20784251391887665,
    0.16854380071163177,
    0.14142295718193054,
    -0.005586510524153709,
    0.1690569967031479,
    -0.18288171291351318,
    0.05025661736726761,
)


def dot_nn(a, b):
    return lax.dot_general(a, b, (((1,), (0,)), ((), ())), preferred_element_type=F32)


def dot_nt(a, b):
    return lax.dot_general(a, b, (((1,), (1,)), ((), ())), preferred_element_type=F32)


def dot_tn(a, b):
    return lax.dot_general(a, b, (((0,), (0,)), ((), ())), preferred_element_type=F32)


def rows_at(index, size):
    return pl.ds(pl.multiple_of(index * size, size), size)


def own_rows(step):
    return slice(step * TILE, (step + 1) * TILE)


def key_rows(step):
    first = max(step - 1, 0) * TILE
    return slice(first, first + 2 * TILE)


def flip(value, bit):
    return value + bit * (1 - 2 * lax.rem(value // bit, 2))


def normalize(x):
    center = x - jnp.mean(x, axis=-1, keepdims=True)
    spread = lax.rsqrt(jnp.mean(center * center, axis=-1, keepdims=True) + EPS)
    return center * spread, spread


def gelu_parts(u):
    t = 1.0 / (1.0 + (0.4 * 0.7071067811865476) * jnp.abs(u))
    q = jnp.full_like(t, ERFC[-1])
    for c in ERFC[-2::-1]:
        q = q * t + c
    e = jnp.exp(-0.5 * (u * u))
    tail = 0.5 * (t * q) * e
    cdf = jnp.where(u >= 0, 1.0 - tail, tail)
    return u * cdf, cdf + u * (e * 0.3989422804014327)


class Copies:
    def __init__(self, sems):
        self.sems, self.n, self.open = sems, 0, []

    def start(self, src, dst):
        assert self.n < self.sems.shape[0]
        copy = pltpu.make_async_copy(src, dst, self.sems.at[self.n])
        self.n += 1
        copy.start()
        return copy

    def save(self, src, dst):
        self.open.append(self.start(src, dst))
        return self.open[-1]

    def settle(self, copy):
        self.open = [c for c in self.open if c is not copy]
        copy.wait()

    def finish(self):
        for copy in self.open:
            copy.wait()


class Remote:
    def __init__(self, send, recv):
        self.send, self.recv, self.n, self.sent = send, recv, 0, []

    def start(self, src, dst, device):
        assert self.n < self.send.shape[0]
        copy = pltpu.make_async_remote_copy(
            src_ref=src,
            dst_ref=dst,
            send_sem=self.send.at[self.n],
            recv_sem=self.recv.at[self.n],
            device_id=device,
            device_id_type=MESH,
        )
        self.n += 1
        copy.start()
        self.sent.append(copy)
        return copy

    def settle(self, copies):
        for copy in copies:
            copy.wait_send()
            self.sent = [c for c in self.sent if c is not copy]

    def finish(self):
        for copy in self.sent:
            copy.wait_send()


def greet(devices):
    barrier = pltpu.get_barrier_semaphore()
    for device in devices:
        pl.semaphore_signal(barrier, inc=1, device_id=device, device_id_type=MESH)
    pl.semaphore_wait(barrier, len(devices))


class Gather:
    def __init__(self, remote, own, other, order):
        self.remote, self.own, self.other, self.order = remote, own, other, order
        me, t = lax.axis_index("dp"), lax.axis_index("tensor")
        self.me, self.t = me, t
        self.have = [lax.rem(me, 8)]
        for bit in (1, 2, 4):
            if bit not in order:
                self.have += [flip(b, bit) for b in self.have]
        self.stage, self.flying, self.done = -1, [], False

    def block(self, ref, index):
        return ref.at[rows_at(index, ref.shape[0] // 8), :]

    def step(self):
        for copy in self.flying:
            copy.wait_recv()
        if self.stage == len(self.order):
            self.done = True
            return
        source = self.other
        if self.stage < 0:
            source, device = self.own, (self.me, 1 - self.t)
        else:
            if self.stage > 0:
                self.have = self.have + [flip(b, self.order[self.stage - 1]) for b in self.have]
            device = (flip(self.me, self.order[self.stage]), self.t)
        self.stage += 1
        self.flying = [
            self.remote.start(self.block(source, b), self.block(self.other, b), device)
            for b in self.have
        ]


class Scatter:
    def __init__(self, remote, grad, recvs, order, finish):
        self.remote, self.grad, self.recvs, self.order = remote, grad, recvs, order
        self.finish = finish
        self.me, self.t = lax.axis_index("dp"), lax.axis_index("tensor")
        self.base, self.count, self.stage, self.done, self.sent = 0, GROUP, -1, False, []

    def step(self):
        if self.stage >= 0:
            self.flying.wait_recv()
            recv = self.recvs[self.stage]
            if self.count == 1:
                self.finish(self.grad[self.base].astype(F32) + recv[0].astype(F32))
                self.done = True
                return

            def body(i, carry):
                at = self.base + i
                self.grad[at] = (self.grad[at].astype(F32) + recv[i].astype(F32)).astype(BF16)
                return carry

            lax.fori_loop(0, self.count, body, 0)
        self.stage += 1
        bit = self.order[self.stage]
        mine = lax.rem(self.me // bit, 2)
        half = self.count // 2
        out = self.base + (1 - mine) * half
        self.base = self.base + mine * half
        self.count = half
        self.flying = self.remote.start(
            self.grad.at[pl.ds(out, half)],
            self.recvs[self.stage],
            (flip(self.me, bit), self.t),
        )
        self.sent.append(self.flying)


def position(block, order):
    pos = 0
    for bit in order:
        pos = 2 * pos + block // bit % 2
    return pos


class Pump:
    def __init__(self, items, plan, before=None, after=None):
        self.items, self.plan, self.at = items, plan, 0
        self.before, self.after = before, after

    def step(self, i):
        if not self.items[i].done:
            if self.before is not None:
                self.before(i)
            self.items[i].step()
            if self.after is not None and self.items[i].done:
                self.after(i)

    def tick(self):
        if self.at < len(self.plan):
            for i in self.plan[self.at]:
                self.step(i)
        self.at += 1

    def need(self, i):
        while not self.items[i].done:
            self.step(i)


def pieces_of(layer, kind):
    return 2 if layer == 0 and kind < 4 else 1


def forward_kernel(names, *args):
    r = SimpleNamespace(**dict(zip(names, args)))
    copies = Copies(r.sem)
    remote = Remote(r.send, r.recv)
    me, t = lax.axis_index("dp"), lax.axis_index("tensor")
    rows, width = r.x.shape
    cols = r.qkv_own.shape[-1]
    heads = cols // HEAD_DIM
    half = r.up_own.shape[-1]
    pieces = width // cols
    x, qkv, wq = r.x, r.qkv, r.wq

    x_load = copies.start(r.x_in, r.x_raw)
    greet([(me, 1 - t), (flip(me, 2), t), (flip(me, 4), t), (flip(me, 1), t)])

    def stored(layer, kind, side):
        if kind < 3:
            return (r.qkv_oth if side else r.qkv_own).at[layer, kind]
        pair = ((r.out_own, r.out_oth), (r.up_own, r.up_oth), (r.dn_own, r.dn_oth))[kind - 3]
        return pair[side].at[layer]

    def buffer(kind, side):
        if kind < 3:
            return wq.at[3 * side + kind]
        return (r.wo, r.wu, r.wd)[kind - 3].at[side]

    parts = [
        (layer, kind, part)
        for layer in range(2)
        for kind in range(6)
        for part in range(pieces_of(layer, kind))
    ]

    def part_of(ref, layer, kind, part):
        size = ref.shape[0] // pieces_of(layer, kind)
        return ref.at[part * size : (part + 1) * size, :]

    gathers = [
        Gather(
            remote,
            part_of(stored(layer, kind, 0), layer, kind, part),
            part_of(stored(layer, kind, 1), layer, kind, part),
            FORWARD_ORDERS[i],
        )
        for i, (layer, kind, part) in enumerate(parts)
    ]
    loads, free = {}, {(kind, side): 0 for kind in range(6) for side in range(2)}

    def load_part(i):
        layer, kind, part = parts[i]
        if i not in loads and free[kind, 1] >= layer and gathers[i].done:
            loads[i] = copies.start(
                part_of(stored(layer, kind, 1), layer, kind, part),
                part_of(buffer(kind, 1), layer, kind, part),
            )

    def load(layer, kind, side):
        if side:
            for i, of in enumerate(parts):
                if of[:2] == (layer, kind):
                    load_part(i)
        elif (layer, kind) not in loads and free[kind, 0] >= layer:
            loads[layer, kind] = copies.start(stored(layer, kind, 0), buffer(kind, 0))

    pump = Pump(gathers, FORWARD_PLAN, after=load_part)

    def get(layer, kind, side):
        mine = [i for i, of in enumerate(parts) if of[:2] == (layer, kind)] if side else []
        for i in mine:
            pump.need(i)
        load(layer, kind, side)
        for i in mine if side else [(layer, kind)]:
            loads[i].wait()

    def used(kind, side):
        free[kind, side] += 1
        if free[kind, side] < 2:
            load(free[kind, side], kind, side)

    pump.tick()
    for kind in range(3):
        load(0, kind, 0)
    for kind in range(3, 6):
        load(0, kind, 0)
    pump.tick()
    saves = {}

    def save(src, dst, part=None):
        saves[id(src)] = copies.save(src if part is None else src.at[part], dst)

    def reuse(src):
        if id(src) in saves:
            copies.settle(saves.pop(id(src)))

    def norm_chunk(layer, which, h, xh, spread, at, values):
        hat, rs = normalize(values)
        xh[at, :] = hat.astype(BF16)
        h[at, :] = (hat * r.gain[layer, which : which + 1, :] + r.shift[layer, which : which + 1, :]).astype(BF16)
        spread[at, :] = jnp.broadcast_to(rs, (CHUNK, HEAD_DIM))

    def first_norm(i, carry):
        at = rows_at(i, CHUNK)
        values = r.x_raw[at, :].astype(F32)
        x[at, :] = values
        norm_chunk(0, 0, r.h1, r.xh1, r.r1, at, values)
        return carry

    def project(layer, side):
        for kind in range(3):
            get(layer, kind, side)
            j = 3 * side + kind
            qkv[j] = dot_nn(r.h1[...], wq[j]).astype(BF16)
            used(kind, side)
            pump.tick()

    def attend(group):
        q_ref, k_ref, v_ref = (qkv.at[3 * group + j] for j in range(3))
        for pair in range(0, heads, 2):
            steps = [
                (i, slice(head * HEAD_DIM, (head + 1) * HEAD_DIM))
                for head in range(pair, min(pair + 2, heads))
                for i in range(rows // TILE)
            ]
            s = [
                dot_nt(q_ref[own_rows(i), c], k_ref[key_rows(i), c]) * SCALE + r.mask[own_rows(i), :]
                for i, c in steps
            ]
            top = [jnp.max(v, axis=-1, keepdims=True) for v in s]
            e = [jnp.exp(v - m) for v, m in zip(s, top)]
            total = [jnp.sum(v, axis=-1, keepdims=True) for v in e]
            p = [(v * (1.0 / m)).astype(BF16) for v, m in zip(e, total)]
            mixed = [dot_nn(v, v_ref[key_rows(i), c]) for v, (i, c) in zip(p, steps)]
            for v, m, (i, c) in zip(p, mixed, steps):
                r.p[group, own_rows(i), c] = v
                r.o[group, own_rows(i), c] = m.astype(BF16)
            pump.tick()

    def add_product(ref, weight, side, then=None):
        for i in range(rows // CHUNK):
            at = slice(i * CHUNK, (i + 1) * CHUNK)
            values = x[at, :] + dot_nt(ref[side, at, :], weight[side])
            x[at, :] = values
            if then is not None:
                then(at, values)

    def norm_next(layer, which):
        h, xh, spread = ((r.h1, r.xh1, r.r1), (r.h2, r.xh2, r.r2))[which]
        for ref in (h, xh, spread):
            reuse(ref)
        return functools.partial(norm_chunk, layer, which, h, xh, spread)

    def save_norm(layer, which):
        for ref, to in (
            ((r.h1, r.h1_out), (r.xh1, r.xh1_out), (r.r1, r.r1_out)),
            ((r.h2, r.h2_out), (r.xh2, r.xh2_out), (r.r2, r.r2_out)),
        )[which]:
            save(ref, to.at[layer])

    def up(layer, side):
        get(layer, 4, side)
        for n in range(half // cols):
            at = slice(n * cols, (n + 1) * cols)
            a, d = gelu_parts(dot_nn(r.h2[...], r.wu[side, :, at]))
            r.a[side, :, at] = a.astype(BF16)
            r.d[side, :, at] = d.astype(BF16)
            pump.tick()
        used(4, side)

    items = r.lengths.shape[1]
    counts = jnp.broadcast_to(r.lengths[...].astype(F32), (8, items)).astype(BF16)
    earlier = lax.broadcasted_iota(jnp.int32, (items, items), 0)
    upto = jnp.where(earlier <= lax.broadcasted_iota(jnp.int32, (items, items), 1), 1.0, 0.0)
    ends = dot_nn(counts, upto.astype(BF16))[0:1, :].astype(jnp.int32)

    def make_mask(i, carry):
        place = i * CHUNK + lax.broadcasted_iota(jnp.int32, (CHUNK, 1), 0)
        start = jnp.max(jnp.where(ends <= place, ends, 0), axis=1, keepdims=True)
        key = jnp.maximum(place // TILE - 1, 0) * TILE
        key = key + lax.broadcasted_iota(jnp.int32, (CHUNK, 2 * TILE), 1)
        allowed = (key >= start) & (key <= place)
        r.mask[rows_at(i, CHUNK), :] = jnp.where(allowed, 0.0, MASKED)
        return carry

    lax.fori_loop(0, rows // CHUNK, make_mask, 0)
    x_load.wait()
    lax.fori_loop(0, rows // CHUNK, first_norm, 0)
    pump.tick()

    def put_out(at, values):
        r.x_raw[at, :] = values.astype(BF16)

    for layer in range(2):
        save_norm(layer, 0)
        for ref in (qkv, r.o, r.p):
            reuse(ref)
        project(layer, 0)
        attend(0)
        get(layer, 3, 0)
        add_product(r.o, r.wo, 0)
        used(3, 0)
        pump.tick()
        project(layer, 1)
        save(qkv, r.qkv_out.at[layer])
        attend(1)
        save(r.p, r.p_out.at[layer])
        save(r.o, r.o_out.at[layer], 0)
        get(layer, 3, 1)
        add_product(r.o, r.wo, 1, norm_next(layer, 1))
        used(3, 1)
        pump.tick()
        save_norm(layer, 1)
        reuse(r.a)
        reuse(r.d)
        up(layer, 0)
        up(layer, 1)
        save(r.a, r.a_out.at[layer], 0)
        save(r.d, r.d_out.at[layer])
        get(layer, 5, 0)
        add_product(r.a, r.wd, 0)
        used(5, 0)
        pump.tick()
        get(layer, 5, 1)
        add_product(r.a, r.wd, 1, put_out if layer else norm_next(1, 0))
        used(5, 1)
        pump.tick()
    copies.save(r.x_raw, r.y_out)
    copies.finish()
    remote.finish()


def backward_kernel(reduce, names, *args):
    r = SimpleNamespace(**dict(zip(names, args)))
    copies = Copies(r.sem)
    me, t = lax.axis_index("dp"), lax.axis_index("tensor")
    g = r.g
    L = [v for k, v in zip(names, args) if k[0] == SLOT]
    rows, width = g.shape
    cols = r.qkv_own.shape[-1]
    heads = cols // HEAD_DIM
    half = r.up_own.shape[-1]
    pieces = width // cols
    halves = [slice(i * cols, (i + 1) * cols) for i in range(pieces)]

    def target(layer, i):
        if i < 2:
            return r.dn_out.at[layer, :, halves[i]]
        if i < 4:
            return r.up_out.at[layer, :, halves[i - 2]]
        return r.out_out.at[layer] if i == 4 else r.qkv_out.at[layer, i - 5]

    if reduce:
        remote = Remote(r.send, r.recv)
        low = lax.rem(me, GROUP)
        greet([(me - low + lax.rem(low + o, GROUP), t) for o in range(1, GROUP)])

        def ending(n):
            def finish(value):
                r.final[n] = value
                copies.save(r.final.at[n], target(1 - n // 8, n % 8))

            return finish

        pump = Pump(
            [
                Scatter(
                    remote, r.grad.at[n % 8], [ref.at[n % 8] for ref in (r.r0, r.r1_, r.r2_, r.r3)],
                    BACKWARD_ORDERS[n], ending(n),
                )
                for n in range(16)
            ],
            BACKWARD_PLAN,
            before=lambda n: order_layers(n),
        )

        def order_layers(n):
            if n < 8 or pump.items[n].stage == 3:
                return
            bit = BACKWARD_ORDERS[n][pump.items[n].stage + 1]
            for m in range(8):
                while not pump.items[m].done and (
                    BACKWARD_ORDERS[m].index(bit) >= pump.items[m].stage
                ):
                    pump.step(m)

        tick = pump.tick
    else:
        tick = lambda: None
        spare = []

    g_load = copies.start(r.g_in, L[0])

    def load_first(layer):
        wd = [copies.start(r.dn_own.at[layer], L[3]), copies.start(r.dn_oth.at[layer], L[4])]
        d = [copies.start(r.d.at[layer, i], L[5 + i]) for i in range(2)]
        return wd, d

    def load_second(layer, a):
        a = a or copies.start(r.a.at[layer], L[7])
        wu = [copies.start(r.up_own.at[layer], L[9]), copies.start(r.up_oth.at[layer], L[10])]
        wo = [
            copies.start(r.out_own.at[layer], L[12].at[:, halves[0]]),
            copies.start(r.out_oth.at[layer], L[12].at[:, halves[1]]),
        ]
        return a, wu, wo

    def load_third(layer):
        h2 = copies.start(r.h2.at[layer], L[8])
        o = copies.start(r.o.at[layer], L[13].at[:, halves[0]])
        p = [copies.start(r.p.at[layer, i], L[14].at[:, halves[i]]) for i in range(2)]
        return h2, o, p

    def load_norm(layer, which):
        pair = ((r.xh1, r.r1), (r.xh2, r.r2))[which]
        return [copies.start(pair[0].at[layer], L[11]), copies.start(pair[1].at[layer], r.spread)]

    a_first = copies.start(r.a.at[1], L[7])
    first = load_first(1)
    second = load_second(1, a_first)
    third = load_third(1)
    norm_load = load_norm(1, 1)

    def zero(i, carry):
        r.sums[i] = jnp.zeros((8, width), F32)
        return carry

    lax.fori_loop(0, 8, zero, 0)
    g_load.wait()

    def begin(i, carry):
        at = rows_at(i, CHUNK)
        g[at, :] = L[0][at, :].astype(F32)
        return carry

    lax.fori_loop(0, rows // CHUNK, begin, 0)

    def weight_grad(n, lhs, rhs):
        if reduce:
            if n >= 8:
                pump.need(n - 8)
                remote.settle(pump.items[n - 8].sent)
        elif n >= 8:
            copies.settle(spare[n - 8])
        full = dot_tn(lhs, rhs)
        size = width // GROUP
        for d in range(GROUP):
            r.grad[n % 8, position(d, BACKWARD_ORDERS[n])] = full[d * size : (d + 1) * size].astype(
                BF16
            )
        if not reduce:
            spare.append(copies.save(r.grad.at[n % 8], r.grad_out.at[1 - n // 8, n % 8]))
            return
        pump.step(n)
        tick()

    def norm_back(layer, which, loads, pairs):
        gain = r.gain[layer, which : which + 1, :]
        row = 4 * layer + which
        for load in loads:
            load.wait()
        count = rows // CHUNK
        for i in range(count):
            at = slice(i * CHUNK, (i + 1) * CHUNK)
            grad = dot_nt(L[pairs[0][0]][at, :], L[pairs[0][1]][...])
            for left, right in pairs[1:]:
                grad = grad + dot_nt(L[left][at, :], L[right][...])
            hat = L[11][at, :].astype(F32)
            rs = r.spread[at, 0:1]
            e = grad * gain
            prod = grad * hat
            m1 = jnp.mean(e, axis=-1, keepdims=True)
            m2 = jnp.mean(e * hat, axis=-1, keepdims=True)
            new = g[at, :] + rs * (e - m1 - hat * m2)
            g[at, :] = new
            L[0][at, :] = new.astype(BF16)
            r.sums[row] += jnp.sum(prod.reshape(CHUNK // 8, 8, width), axis=0)
            r.sums[row + 2] += jnp.sum(grad.reshape(CHUNK // 8, 8, width), axis=0)
            if i + 1 in (count // 2, count):
                tick()

    to = [(1, 0), (1, 1), (2, 0), (2, 1), (7, 0), (7, 1)]

    def attend(group):
        n = 3 * group
        count = rows // TILE
        (sq, hq), (sk, hk), (sv, hv) = to[n : n + 3]

        def lanes(side, head):
            return slice(side * cols + head * HEAD_DIM, side * cols + (head + 1) * HEAD_DIM)

        def part(j, head):
            return L[3 + (n + j) // 2], lanes((n + j) % 2, head)

        for first_head in range(0, heads, HEADS_AT_ONCE):
            both = range(first_head, min(first_head + HEADS_AT_ONCE, heads))
            steps = [(i, head) for head in both for i in range(count)]
            q, k, v = (
                [part(j, head)[0][rows_of(i), part(j, head)[1]] for i, head in steps]
                for j, rows_of in enumerate((own_rows, key_rows, key_rows))
            )
            do = [L[6][own_rows(i), lanes(group, head)] for i, head in steps]
            p = [L[14][own_rows(i), lanes(group, head)] for i, head in steps]
            dp = [dot_nt(x, y) for x, y in zip(do, v)]
            wide_p = [x.astype(F32) for x in p]
            inner = [jnp.sum(x * y, axis=-1, keepdims=True) for x, y in zip(dp, wide_p)]
            ds = [(y * (x - z)).astype(BF16) for x, y, z in zip(dp, wide_p, inner)]
            dq = [dot_nn(x, y) for x, y in zip(ds, k)]
            dk = [dot_tn(x, y) for x, y in zip(ds, q)]
            dv = [dot_tn(x, y) for x, y in zip(p, do)]
            for m, (i, head) in enumerate(steps):
                L[sq][own_rows(i), lanes(hq, head)] = (dq[m] * SCALE).astype(BF16)
                if i == 0:
                    own_k, own_v = dk[m][:TILE], dv[m][:TILE]
                else:
                    own_k, own_v = dk[m][TILE:], dv[m][TILE:]
                if i + 1 < count:
                    own_k = own_k + dk[m + 1][:TILE]
                    own_v = own_v + dv[m + 1][:TILE]
                L[sk][own_rows(i), lanes(hk, head)] = (own_k * SCALE).astype(BF16)
                L[sv][own_rows(i), lanes(hv, head)] = own_v.astype(BF16)
            tick()

    for layer in (1, 0):
        base = 8 * (1 - layer)
        wd_load, d_load = first
        a_load, wu_load, wo_load = second
        h2_load, o_load, p_load = third
        a_load.wait()
        for i in range(2):
            weight_grad(base + i, L[0][...], L[7][:, halves[i]])
        for i in range(2):
            wd_load[i].wait()
            d_load[i].wait()
            for at in halves:
                da = dot_nn(L[0][...], L[3 + i][:, at])
                L[1 + i][:, at] = (da * L[5 + i][:, at].astype(F32)).astype(BF16)
                tick()
            if i == 0:
                h2_load.wait()
                for j in range(2):
                    weight_grad(base + 2 + j, L[8][...], L[1][:, halves[j]])
        qkv_load = [
            copies.start(r.qkv.at[layer, j], L[3 + j // 2].at[:, halves[j % 2]]) for j in range(6)
        ]
        h1_load = copies.start(r.h1.at[layer], L[8])
        for load in wu_load:
            load.wait()
        norm_back(layer, 1, norm_load, ((1, 9), (2, 10)))

        def load_wq(some):
            return [
                copies.start(
                    r.qkv_own.at[layer, j] if j < 3 else r.qkv_oth.at[layer, j - 3],
                    L[(9, 10, 12)[j // 2]].at[:, halves[j % 2]],
                )
                for j in some
            ]

        wq_load = load_wq(range(4))
        norm_load = load_norm(layer, 0)
        for i in range(2):
            wo_load[i].wait()
            L[6][:, halves[i]] = dot_nn(L[0][...], L[12][:, halves[i]]).astype(BF16)
            tick()
        wq_load += load_wq(range(4, 6))
        o_load.wait()
        weight_grad(base + 4, L[0][...], L[13][:, halves[0]])
        for load in (*qkv_load, *p_load):
            load.wait()
        attend(0)
        h1_load.wait()
        for j in range(3):
            slot, side = to[j]
            weight_grad(base + 5 + j, L[8][...], L[slot][:, halves[side]])
        attend(1)
        if layer == 1:
            first = load_first(0)
            third = load_third(0)
        for load in wq_load:
            load.wait()
        norm_back(layer, 0, norm_load, ((1, 9), (2, 10), (7, 12)))
        if layer == 1:
            second = load_second(0, None)
            norm_load = load_norm(0, 1)
    copies.save(g, r.g_out)
    for k in range(8):
        r.flat[k : k + 1, :] = jnp.sum(r.sums[k], axis=0, keepdims=True)
    if not reduce:
        copies.save(r.flat, r.flat_out)
        copies.finish()
        return
    sends = []
    for o in range(1, GROUP):
        to_dev = lax.rem(low + o, GROUP)
        sends.append(
            remote.start(
                r.flat.at[:, rows_at(to_dev // 2, 128)], r.slots.at[o], (me - low + to_dev, t)
            )
        )
    tick()
    while pump.at < len(BACKWARD_PLAN):
        tick()
    for n in range(16):
        pump.need(n)
    total = r.flat[:, rows_at(low // 2, 128)]
    for o, copy in enumerate(sends):
        copy.wait_recv()
        total = total + r.slots[o + 1]
    r.flat_f[...] = total
    copies.save(r.flat_f, r.flat_out)
    copies.finish()
    remote.finish()


def call(kernel, ins, outs, scratch, name, collective, flops):
    split = lambda v: v if isinstance(v, tuple) else (v, ANY)
    in_items = {k: split(v) for k, v in ins.items()}
    out_items = {k: split(v) for k, v in outs.items()}
    names = (*in_items, *out_items, *scratch)
    params = dict(vmem_limit_bytes=VMEM_LIMIT, has_side_effects=True)
    if collective is not None:
        params.update(collective_id=collective)
    made = pl.pallas_call(
        functools.partial(kernel, names),
        out_shape=tuple(v for v, _ in out_items.values()),
        in_specs=[pl.BlockSpec(memory_space=s) for _, s in in_items.values()],
        out_specs=tuple(pl.BlockSpec(memory_space=s) for _, s in out_items.values()),
        scratch_shapes=list(scratch.values()),
        compiler_params=pltpu.CompilerParams(**params),
        cost_estimate=pl.CostEstimate(flops=flops, bytes_accessed=60 << 20, transcendentals=0),
        name=name,
    )(*(v for v, _ in in_items.values()))
    return SimpleNamespace(**dict(zip(out_items, made)))


def forward(x, lengths, gain, shift, weights):
    rows, width = x.shape
    w_qkv, w_out, w_up, w_dn = weights
    cols, half = w_qkv.shape[-1], w_up.shape[-1]
    shape = jax.ShapeDtypeStruct
    wide, slab = (rows, width), (rows, cols)
    like = lambda w: shape(w.shape, BF16)
    two = lambda *dims, dtype=BF16: shape((2, *dims), dtype)
    ins = dict(
        x_in=x, lengths=(lengths, VMEM), gain=(gain, VMEM), shift=(shift, VMEM),
        qkv_own=w_qkv, out_own=w_out, up_own=w_up, dn_own=w_dn,
    )
    outs = dict(
        qkv_oth=like(w_qkv), out_oth=like(w_out), up_oth=like(w_up), dn_oth=like(w_dn),
        h1_out=two(*wide), xh1_out=two(*wide), r1_out=two(rows, 128, dtype=F32),
        qkv_out=two(6, *slab), p_out=two(2, *slab), o_out=two(*slab),
        h2_out=two(*wide), xh2_out=two(*wide), r2_out=two(rows, 128, dtype=F32),
        a_out=two(rows, half), d_out=two(2, rows, half),
        y_out=shape(wide, BF16),
    )
    copies = 16 * 8
    scratch = dict(
        x=VMEM(wide, F32), x_raw=VMEM(wide, BF16),
        h1=VMEM(wide, BF16), xh1=VMEM(wide, BF16), r1=VMEM((rows, 128), F32),
        h2=VMEM(wide, BF16), xh2=VMEM(wide, BF16), r2=VMEM((rows, 128), F32),
        qkv=VMEM((6, *slab), BF16), o=VMEM((2, *slab), BF16), p=VMEM((2, *slab), BF16),
        mask=VMEM((rows, 128), F32),
        a=VMEM((2, rows, half), BF16), d=VMEM((2, rows, half), BF16),
        wq=VMEM((6, width, cols), BF16), wo=VMEM((2, width, cols), BF16),
        wu=VMEM((2, width, half), BF16), wd=VMEM((2, width, half), BF16),
        sem=pltpu.SemaphoreType.DMA((80,)),
        send=pltpu.SemaphoreType.DMA((copies,)), recv=pltpu.SemaphoreType.DMA((copies,)),
    )
    flops = 4 * rows * (6 * cols * width + 2 * cols * width + 4 * half * width)
    return call(forward_kernel, ins, outs, scratch, "forward", 0, flops)


def backward(reduce, g, gain, weights, kept):
    rows, width = g.shape
    w_qkv, w_out, w_up, w_dn = weights
    cols, half = w_qkv.shape[-1], w_up.shape[-1]
    shape = jax.ShapeDtypeStruct
    wide = (rows, width)
    block = width // GROUP
    ins = dict(
        g_in=g, gain=(gain, VMEM),
        qkv_own=w_qkv, out_own=w_out, up_own=w_up, dn_own=w_dn,
        qkv_oth=kept.qkv_oth, out_oth=kept.out_oth, up_oth=kept.up_oth, dn_oth=kept.dn_oth,
        h1=kept.h1_out, xh1=kept.xh1_out, r1=kept.r1_out, qkv=kept.qkv_out, p=kept.p_out, o=kept.o_out,
        h2=kept.h2_out, xh2=kept.xh2_out, r2=kept.r2_out, a=kept.a_out, d=kept.d_out,
    )
    outs = dict(g_out=shape(wide, F32))
    recv = lambda k: VMEM((8, GROUP >> (k + 1), block, cols), BF16)
    scratch = dict(
        g=VMEM(wide, F32), spread=VMEM((rows, 128), F32),
        sums=VMEM((8, 8, width), F32), flat=VMEM((8, width), F32),
        sem=pltpu.SemaphoreType.DMA((96,)),
        grad=VMEM((8, GROUP, block, cols), BF16),
    )
    scratch.update({f"{SLOT}{i}": VMEM(wide, BF16) for i in range(15)})
    if not reduce:
        outs.update(flat_out=shape((8, width), F32), grad_out=shape((2, 8, GROUP, block, cols), BF16))
    else:
        copies = 16 * 4 + GROUP
        part = lambda *dims: shape((2, *dims), F32)
        outs.update(
            dn_out=part(block, half), up_out=part(block, half), out_out=part(block, cols),
            qkv_out=part(3, block, cols), flat_out=shape((8, 128), F32),
        )
        scratch.update(
            send=pltpu.SemaphoreType.DMA((copies,)), recv=pltpu.SemaphoreType.DMA((copies,)),
            r0=recv(0), r1_=recv(1), r2_=recv(2), r3=recv(3), final=VMEM((16, block, cols), F32),
            slots=VMEM((GROUP, 8, 128), F32), flat_f=VMEM((8, 128), F32),
        )
    flops = 4 * rows * (2 * 6 * cols * width + 3 * cols * width + 6 * half * width)
    return call(
        functools.partial(backward_kernel, reduce), ins, outs, scratch,
        "backward", 1 if reduce else None, flops,
    )


def deliver_kernel(block, *args):
    ins, outs, held, sems = args[:6], args[7:13], args[15:21], args[21]
    parts = []
    for n, ref in enumerate(ins):
        pieces = 4 if ref.shape[0] > 2 else 2
        size = ref.shape[0] // pieces
        parts += [(n, slice(i * size, (i + 1) * size)) for i in range(pieces)]
    arrive = [
        pltpu.make_async_copy(ins[n].at[at], held[n].at[at], sems.at[0, k])
        for k, (n, at) in enumerate(parts)
    ]
    leave = [
        pltpu.make_async_copy(held[n].at[at], outs[n].at[at], sems.at[1, k])
        for k, (n, at) in enumerate(parts)
    ]
    for copy in arrive:
        copy.start()
    flat = args[6][...]
    odd = lax.rem(lax.axis_index("dp"), 2) == 1
    flat = jnp.where(odd, flat[:, block : 2 * block], flat[:, :block])
    for layer in range(2):
        args[13][layer] = flat[4 * layer : 4 * layer + 2]
        args[14][layer] = flat[4 * layer + 2 : 4 * layer + 4]
    for come, go in zip(arrive, leave):
        come.wait()
        go.start()
    for copy in leave:
        copy.wait()


def deliver(kept, back):
    given = (kept.y_out, back.g_out, back.qkv_out, back.out_out, back.up_out, back.dn_out)
    shape = jax.ShapeDtypeStruct
    block = kept.y_out.shape[1] // GROUP
    small = shape((2, 2, block), F32)
    return pl.pallas_call(
        functools.partial(deliver_kernel, block),
        out_shape=(*(shape(v.shape, v.dtype) for v in given), small, small),
        in_specs=[pl.BlockSpec(memory_space=ANY)] * 6 + [pl.BlockSpec(memory_space=VMEM)],
        out_specs=(*[pl.BlockSpec(memory_space=ANY)] * 6, *[pl.BlockSpec(memory_space=VMEM)] * 2),
        scratch_shapes=[VMEM(v.shape, v.dtype) for v in given] + [pltpu.SemaphoreType.DMA((2, 16))],
        compiler_params=pltpu.CompilerParams(vmem_limit_bytes=VMEM_LIMIT),
        name="deliver",
    )(*given, back.flat_out)


def local(n_dp, tokens, lengths, w_qkv, w_out, w_up, w_down, norm_gain, norm_bias, cotangent):
    rows, width = tokens.shape
    cols = w_qkv.shape[3]
    weights = (jnp.transpose(w_qkv, (0, 2, 1, 3)), w_out, w_up, w_down)
    kept = forward(tokens, lengths, norm_gain, norm_bias, weights)
    reduce = n_dp == GROUP
    back = backward(reduce, cotangent, norm_gain, weights, kept)
    if reduce:
        y, grad, qkv, out, up, dn, gain, shift = deliver(kept, back)
        return (y, grad, jnp.transpose(qkv, (0, 2, 1, 3)), out, up, dn, gain, shift)

    def total(*parts):
        layers = []
        for layer in range(2):
            found = []
            for i in parts:
                n = 8 * (1 - layer) + i
                places = [position(d, BACKWARD_ORDERS[n]) for d in range(GROUP)]
                piece = back.grad_out[layer, i].astype(F32)
                found.append(jnp.concatenate([piece[at] for at in places]))
            layers.append(jnp.concatenate(found, axis=1))
        return lax.psum_scatter(jnp.stack(layers), "dp", scatter_dimension=1, tiled=True)

    dn, up, out = total(0, 1), total(2, 3), total(4)
    qkv = jnp.stack([total(5), total(6), total(7)], axis=1)
    flat = back.flat_out.reshape(2, 4, width)
    flat = lax.psum_scatter(flat, "dp", scatter_dimension=2, tiled=True)
    gain, shift = flat[:, :2], flat[:, 2:]
    qkv = jnp.transpose(qkv, (0, 2, 1, 3))
    return (kept.y_out, back.g_out, qkv, out, up, dn, gain, shift)


def solution(mesh):
    placed = (
        P("dp", None),
        P("dp", None),
        P(None, None, None, "tensor"),
        P(None, None, "tensor"),
        P(None, None, "tensor"),
        P(None, None, "tensor"),
        P(),
        P(),
        P("dp", None),
    )
    return jax.shard_map(
        functools.partial(local, mesh.shape["dp"]),
        mesh=mesh,
        in_specs=placed,
        out_specs=(
            P("dp", None),
            P("dp", None),
            P(None, "dp", None, "tensor"),
            P(None, "dp", "tensor"),
            P(None, "dp", "tensor"),
            P(None, "dp", "tensor"),
            P(None, None, "dp"),
            P(None, None, "dp"),
        ),
        check_vma=False,
    )
```

```python
import functools
from types import SimpleNamespace

import jax
import jax.numpy as jnp
from jax import lax
from jax.experimental import pallas as pl
from jax.experimental.pallas import tpu as pltpu
from jax.sharding import PartitionSpec as P

HEAD_DIM = 128
TILE = 64
EPS = 1e-05
MASKED = -1e30
MESH = pl.DeviceIdType.MESH
VMEM = pltpu.VMEM
ANY = pl.ANY
F32 = jnp.float32
BF16 = jnp.bfloat16
SCALE = HEAD_DIM**-0.5
VMEM_LIMIT = 62 << 20
SLOT = "L"
HEADS_AT_ONCE = 2
GROUP = 16
CHUNK = 256

FORWARD_ORDERS = ((2, 4, 1), (2, 4, 1), (4, 2, 1), (4, 2, 1), (2, 4, 1), (4, 2, 1), (4, 2, 1), (2, 4, 1), (2, 4, 1), (4, 2, 1), (2, 4, 1), (4, 2, 1), (2, 1), (4, 2, 1), (4, 1), (1,))
FORWARD_PLAN = ((0, 1, 2), (3, 4), (0, 1, 5), (2, 6), (3, 7), (0, 4, 8), (1, 2, 5), (3,), (4, 6, 7, 0, 2, 9, 0, 1, 2, 5, 3, 8, 1), (3, 7, 10), (4, 5, 6, 11, 9, 7, 12, 4, 5), (7, 8, 10), (), (11, 13, 6, 9, 6), (10, 12, 14), (), (13, 8, 9, 11, 15, 8), (), (9, 14), (10, 12), (13,), (10,), (11, 12), (), (), (11,), (13,), (), (), (13, 14), (), (), (), (14,), (15,), (), (), (15,), (),)
BACKWARD_ORDERS = ((1, 2, 4, 8), (1, 8, 2, 4), (1, 2, 4, 8), (1, 2, 4, 8), (1, 2, 4, 8), (1, 2, 8, 4), (1, 4, 2, 8), (1, 2, 4, 8), (1, 2, 4, 8), (1, 2, 4, 8), (1, 2, 4, 8), (1, 4, 8, 2), (1, 2, 8, 4), (1, 2, 4, 8), (1, 2, 4, 8), (1, 4, 2, 8))
BACKWARD_PLAN = ((), (), (), (0,), (1,), (), (), (2,), (3, 0), (), (), (2,), (0, 1), (), (), (4, 3, 2), (1, 0), (), (5,), (6, 3, 7), (4, 1, 2), (5,), (6,), (), (3, 7), (4, 8), (9,), (), (5, 7), (10,), (4, 11, 8), (6,), (7,), (9,), (), (11,), (10,), (12, 8), (9,), (), (13,), (14, 15, 10, 11), (12, 8), (9, 13), (15, 10, 14, 11, 13, 15, 12, 14, 13, 12, 15, 14),)

ERFC = (
    0.22567586600780487,
    0.22566960752010345,
    0.20784251391887665,
    0.16854380071163177,
    0.14142295718193054,
    -0.005586510524153709,
    0.1690569967031479,
    -0.18288171291351318,
    0.05025661736726761,
)


def dot_nn(a, b):
    return lax.dot_general(a, b, (((1,), (0,)), ((), ())), preferred_element_type=F32)


def dot_nt(a, b):
    return lax.dot_general(a, b, (((1,), (1,)), ((), ())), preferred_element_type=F32)


def dot_tn(a, b):
    return lax.dot_general(a, b, (((0,), (0,)), ((), ())), preferred_element_type=F32)


def rows_at(index, size):
    return pl.ds(pl.multiple_of(index * size, size), size)


def own_rows(step):
    return slice(step * TILE, (step + 1) * TILE)


def key_rows(step):
    first = max(step - 1, 0) * TILE
    return slice(first, first + 2 * TILE)


def flip(value, bit):
    return value + bit * (1 - 2 * lax.rem(value // bit, 2))


def normalize(x):
    center = x - jnp.mean(x, axis=-1, keepdims=True)
    spread = lax.rsqrt(jnp.mean(center * center, axis=-1, keepdims=True) + EPS)
    return center * spread, spread


def gelu_parts(u):
    t = 1.0 / (1.0 + (0.4 * 0.7071067811865476) * jnp.abs(u))
    q = jnp.full_like(t, ERFC[-1])
    for c in ERFC[-2::-1]:
        q = q * t + c
    e = jnp.exp(-0.5 * (u * u))
    tail = 0.5 * (t * q) * e
    cdf = jnp.where(u >= 0, 1.0 - tail, tail)
    return u * cdf, cdf + u * (e * 0.3989422804014327)


class Copies:
    def __init__(self, sems):
        self.sems, self.n, self.open = sems, 0, []

    def start(self, src, dst):
        assert self.n < self.sems.shape[0]
        copy = pltpu.make_async_copy(src, dst, self.sems.at[self.n])
        self.n += 1
        copy.start()
        return copy

    def save(self, src, dst):
        self.open.append(self.start(src, dst))
        return self.open[-1]

    def settle(self, copy):
        self.open = [c for c in self.open if c is not copy]
        copy.wait()

    def finish(self):
        for copy in self.open:
            copy.wait()


class Remote:
    def __init__(self, send, recv):
        self.send, self.recv, self.n, self.sent = send, recv, 0, []

    def start(self, src, dst, device):
        assert self.n < self.send.shape[0]
        copy = pltpu.make_async_remote_copy(
            src_ref=src,
            dst_ref=dst,
            send_sem=self.send.at[self.n],
            recv_sem=self.recv.at[self.n],
            device_id=device,
            device_id_type=MESH,
        )
        self.n += 1
        copy.start()
        self.sent.append(copy)
        return copy

    def settle(self, copies):
        for copy in copies:
            copy.wait_send()
            self.sent = [c for c in self.sent if c is not copy]

    def finish(self):
        for copy in self.sent:
            copy.wait_send()


def greet(devices):
    barrier = pltpu.get_barrier_semaphore()
    for device in devices:
        pl.semaphore_signal(barrier, inc=1, device_id=device, device_id_type=MESH)
    pl.semaphore_wait(barrier, len(devices))


class Gather:
    def __init__(self, remote, own, other, order):
        self.remote, self.own, self.other, self.order = remote, own, other, order
        me, t = lax.axis_index("dp"), lax.axis_index("tensor")
        self.me, self.t = me, t
        self.have = [lax.rem(me, 8)]
        for bit in (1, 2, 4):
            if bit not in order:
                self.have += [flip(b, bit) for b in self.have]
        self.stage, self.flying, self.done = -1, [], False

    def block(self, ref, index):
        return ref.at[rows_at(index, ref.shape[0] // 8), :]

    def step(self):
        for copy in self.flying:
            copy.wait_recv()
        if self.stage == len(self.order):
            self.done = True
            return
        source = self.other
        if self.stage < 0:
            source, device = self.own, (self.me, 1 - self.t)
        else:
            if self.stage > 0:
                self.have = self.have + [flip(b, self.order[self.stage - 1]) for b in self.have]
            device = (flip(self.me, self.order[self.stage]), self.t)
        self.stage += 1
        self.flying = [
            self.remote.start(self.block(source, b), self.block(self.other, b), device)
            for b in self.have
        ]


class Scatter:
    def __init__(self, remote, grad, recvs, order, finish):
        self.remote, self.grad, self.recvs, self.order = remote, grad, recvs, order
        self.finish = finish
        self.me, self.t = lax.axis_index("dp"), lax.axis_index("tensor")
        self.base, self.count, self.stage, self.done, self.sent = 0, GROUP, -1, False, []

    def step(self):
        if self.stage >= 0:
            self.flying.wait_recv()
            recv = self.recvs[self.stage]
            if self.count == 1:
                self.finish(self.grad[self.base].astype(F32) + recv[0].astype(F32))
                self.done = True
                return

            def body(i, carry):
                at = self.base + i
                self.grad[at] = (self.grad[at].astype(F32) + recv[i].astype(F32)).astype(BF16)
                return carry

            lax.fori_loop(0, self.count, body, 0)
        self.stage += 1
        bit = self.order[self.stage]
        mine = lax.rem(self.me // bit, 2)
        half = self.count // 2
        out = self.base + (1 - mine) * half
        self.base = self.base + mine * half
        self.count = half
        self.flying = self.remote.start(
            self.grad.at[pl.ds(out, half)],
            self.recvs[self.stage],
            (flip(self.me, bit), self.t),
        )
        self.sent.append(self.flying)


def position(block, order):
    pos = 0
    for bit in order:
        pos = 2 * pos + block // bit % 2
    return pos


class Pump:
    def __init__(self, items, plan, before=None, after=None):
        self.items, self.plan, self.at = items, plan, 0
        self.before, self.after = before, after

    def step(self, i):
        if not self.items[i].done:
            if self.before is not None:
                self.before(i)
            self.items[i].step()
            if self.after is not None and self.items[i].done:
                self.after(i)

    def tick(self):
        if self.at < len(self.plan):
            for i in self.plan[self.at]:
                self.step(i)
        self.at += 1

    def need(self, i):
        while not self.items[i].done:
            self.step(i)


def pieces_of(layer, kind):
    return 2 if layer == 0 and kind < 4 else 1


def forward_kernel(names, *args):
    r = SimpleNamespace(**dict(zip(names, args)))
    copies = Copies(r.sem)
    remote = Remote(r.send, r.recv)
    me, t = lax.axis_index("dp"), lax.axis_index("tensor")
    rows, width = r.x.shape
    cols = r.qkv_own.shape[-1]
    heads = cols // HEAD_DIM
    half = r.up_own.shape[-1]
    pieces = width // cols
    x, qkv, wq = r.x, r.qkv, r.wq

    x_load = copies.start(r.x_in, r.x_raw)
    greet([(me, 1 - t), (flip(me, 2), t), (flip(me, 4), t), (flip(me, 1), t)])

    def stored(layer, kind, side):
        if kind < 3:
            return (r.qkv_oth if side else r.qkv_own).at[layer, kind]
        pair = ((r.out_own, r.out_oth), (r.up_own, r.up_oth), (r.dn_own, r.dn_oth))[kind - 3]
        return pair[side].at[layer]

    def buffer(kind, side):
        if kind < 3:
            return wq.at[3 * side + kind]
        return (r.wo, r.wu, r.wd)[kind - 3].at[side]

    parts = [
        (layer, kind, part)
        for layer in range(2)
        for kind in range(6)
        for part in range(pieces_of(layer, kind))
    ]

    def part_of(ref, layer, kind, part):
        size = ref.shape[0] // pieces_of(layer, kind)
        return ref.at[part * size : (part + 1) * size, :]

    gathers = [
        Gather(
            remote,
            part_of(stored(layer, kind, 0), layer, kind, part),
            part_of(stored(layer, kind, 1), layer, kind, part),
            FORWARD_ORDERS[i],
        )
        for i, (layer, kind, part) in enumerate(parts)
    ]
    loads, free = {}, {(kind, side): 0 for kind in range(6) for side in range(2)}

    def load_part(i):
        layer, kind, part = parts[i]
        if i not in loads and free[kind, 1] >= layer and gathers[i].done:
            loads[i] = copies.start(
                part_of(stored(layer, kind, 1), layer, kind, part),
                part_of(buffer(kind, 1), layer, kind, part),
            )

    def load(layer, kind, side):
        if side:
            for i, of in enumerate(parts):
                if of[:2] == (layer, kind):
                    load_part(i)
        elif (layer, kind) not in loads and free[kind, 0] >= layer:
            loads[layer, kind] = copies.start(stored(layer, kind, 0), buffer(kind, 0))

    pump = Pump(gathers, FORWARD_PLAN, after=load_part)

    def get(layer, kind, side):
        mine = [i for i, of in enumerate(parts) if of[:2] == (layer, kind)] if side else []
        for i in mine:
            pump.need(i)
        load(layer, kind, side)
        for i in mine if side else [(layer, kind)]:
            loads[i].wait()

    def used(kind, side):
        free[kind, side] += 1
        if free[kind, side] < 2:
            load(free[kind, side], kind, side)

    pump.tick()
    for kind in range(3):
        load(0, kind, 0)
    for kind in range(3, 6):
        load(0, kind, 0)
    pump.tick()
    saves = {}

    def save(src, dst, part=None):
        saves[id(src)] = copies.save(src if part is None else src.at[part], dst)

    def reuse(src):
        if id(src) in saves:
            copies.settle(saves.pop(id(src)))

    def norm_chunk(layer, which, h, xh, spread, at, values):
        hat, rs = normalize(values)
        xh[at, :] = hat.astype(BF16)
        h[at, :] = (hat * r.gain[layer, which : which + 1, :] + r.shift[layer, which : which + 1, :]).astype(BF16)
        spread[at, :] = jnp.broadcast_to(rs, (CHUNK, HEAD_DIM))

    def first_norm(i, carry):
        at = rows_at(i, CHUNK)
        values = r.x_raw[at, :].astype(F32)
        x[at, :] = values
        norm_chunk(0, 0, r.h1, r.xh1, r.r1, at, values)
        return carry

    def project(layer, side):
        for kind in range(3):
            get(layer, kind, side)
            j = 3 * side + kind
            qkv[j] = dot_nn(r.h1[...], wq[j]).astype(BF16)
            used(kind, side)
            pump.tick()

    def attend(group):
        q_ref, k_ref, v_ref = (qkv.at[3 * group + j] for j in range(3))
        for pair in range(0, heads, 2):
            steps = [
                (i, slice(head * HEAD_DIM, (head + 1) * HEAD_DIM))
                for head in range(pair, min(pair + 2, heads))
                for i in range(rows // TILE)
            ]
            s = [
                dot_nt(q_ref[own_rows(i), c], k_ref[key_rows(i), c]) * SCALE + r.mask[own_rows(i), :]
                for i, c in steps
            ]
            top = [jnp.max(v, axis=-1, keepdims=True) for v in s]
            e = [jnp.exp(v - m) for v, m in zip(s, top)]
            total = [jnp.sum(v, axis=-1, keepdims=True) for v in e]
            p = [(v * (1.0 / m)).astype(BF16) for v, m in zip(e, total)]
            mixed = [dot_nn(v, v_ref[key_rows(i), c]) for v, (i, c) in zip(p, steps)]
            for v, m, (i, c) in zip(p, mixed, steps):
                r.p[group, own_rows(i), c] = v
                r.o[group, own_rows(i), c] = m.astype(BF16)
            pump.tick()

    def add_product(ref, weight, side, then=None):
        for i in range(rows // CHUNK):
            at = slice(i * CHUNK, (i + 1) * CHUNK)
            values = x[at, :] + dot_nt(ref[side, at, :], weight[side])
            x[at, :] = values
            if then is not None:
                then(at, values)

    def norm_next(layer, which):
        h, xh, spread = ((r.h1, r.xh1, r.r1), (r.h2, r.xh2, r.r2))[which]
        for ref in (h, xh, spread):
            reuse(ref)
        return functools.partial(norm_chunk, layer, which, h, xh, spread)

    def save_norm(layer, which):
        for ref, to in (
            ((r.h1, r.h1_out), (r.xh1, r.xh1_out), (r.r1, r.r1_out)),
            ((r.h2, r.h2_out), (r.xh2, r.xh2_out), (r.r2, r.r2_out)),
        )[which]:
            save(ref, to.at[layer])

    def up(layer, side):
        get(layer, 4, side)
        for n in range(half // cols):
            at = slice(n * cols, (n + 1) * cols)
            a, d = gelu_parts(dot_nn(r.h2[...], r.wu[side, :, at]))
            r.a[side, :, at] = a.astype(BF16)
            r.d[side, :, at] = d.astype(BF16)
            pump.tick()
        used(4, side)

    items = r.lengths.shape[1]
    counts = jnp.broadcast_to(r.lengths[...].astype(F32), (8, items)).astype(BF16)
    earlier = lax.broadcasted_iota(jnp.int32, (items, items), 0)
    upto = jnp.where(earlier <= lax.broadcasted_iota(jnp.int32, (items, items), 1), 1.0, 0.0)
    ends = dot_nn(counts, upto.astype(BF16))[0:1, :].astype(jnp.int32)

    def make_mask(i, carry):
        place = i * CHUNK + lax.broadcasted_iota(jnp.int32, (CHUNK, 1), 0)
        start = jnp.max(jnp.where(ends <= place, ends, 0), axis=1, keepdims=True)
        key = jnp.maximum(place // TILE - 1, 0) * TILE
        key = key + lax.broadcasted_iota(jnp.int32, (CHUNK, 2 * TILE), 1)
        allowed = (key >= start) & (key <= place)
        r.mask[rows_at(i, CHUNK), :] = jnp.where(allowed, 0.0, MASKED)
        return carry

    lax.fori_loop(0, rows // CHUNK, make_mask, 0)
    x_load.wait()
    lax.fori_loop(0, rows // CHUNK, first_norm, 0)
    pump.tick()

    def put_out(at, values):
        r.x_raw[at, :] = values.astype(BF16)

    for layer in range(2):
        save_norm(layer, 0)
        for ref in (qkv, r.o, r.p):
            reuse(ref)
        project(layer, 0)
        attend(0)
        get(layer, 3, 0)
        add_product(r.o, r.wo, 0)
        used(3, 0)
        pump.tick()
        project(layer, 1)
        save(qkv, r.qkv_out.at[layer])
        attend(1)
        save(r.p, r.p_out.at[layer])
        save(r.o, r.o_out.at[layer], 0)
        get(layer, 3, 1)
        add_product(r.o, r.wo, 1, norm_next(layer, 1))
        used(3, 1)
        pump.tick()
        save_norm(layer, 1)
        reuse(r.a)
        reuse(r.d)
        up(layer, 0)
        up(layer, 1)
        save(r.a, r.a_out.at[layer], 0)
        save(r.d, r.d_out.at[layer])
        get(layer, 5, 0)
        add_product(r.a, r.wd, 0)
        used(5, 0)
        pump.tick()
        get(layer, 5, 1)
        add_product(r.a, r.wd, 1, put_out if layer else norm_next(1, 0))
        used(5, 1)
        pump.tick()
    copies.save(r.x_raw, r.y_out)
    copies.finish()
    remote.finish()


def backward_kernel(reduce, names, *args):
    r = SimpleNamespace(**dict(zip(names, args)))
    copies = Copies(r.sem)
    me, t = lax.axis_index("dp"), lax.axis_index("tensor")
    g = r.g
    L = [v for k, v in zip(names, args) if k[0] == SLOT]
    rows, width = g.shape
    cols = r.qkv_own.shape[-1]
    heads = cols // HEAD_DIM
    half = r.up_own.shape[-1]
    pieces = width // cols
    halves = [slice(i * cols, (i + 1) * cols) for i in range(pieces)]

    def target(layer, i):
        if i < 2:
            return r.dn_out.at[layer, :, halves[i]]
        if i < 4:
            return r.up_out.at[layer, :, halves[i - 2]]
        return r.out_out.at[layer] if i == 4 else r.qkv_out.at[layer, i - 5]

    if reduce:
        remote = Remote(r.send, r.recv)
        low = lax.rem(me, GROUP)
        greet([(me - low + lax.rem(low + o, GROUP), t) for o in range(1, GROUP)])

        def ending(n):
            def finish(value):
                r.final[n] = value
                copies.save(r.final.at[n], target(1 - n // 8, n % 8))

            return finish

        pump = Pump(
            [
                Scatter(
                    remote, r.grad.at[n % 8], [ref.at[n % 8] for ref in (r.r0, r.r1_, r.r2_, r.r3)],
                    BACKWARD_ORDERS[n], ending(n),
                )
                for n in range(16)
            ],
            BACKWARD_PLAN,
            before=lambda n: order_layers(n),
        )

        def order_layers(n):
            if n < 8 or pump.items[n].stage == 3:
                return
            bit = BACKWARD_ORDERS[n][pump.items[n].stage + 1]
            for m in range(8):
                while not pump.items[m].done and (
                    BACKWARD_ORDERS[m].index(bit) >= pump.items[m].stage
                ):
                    pump.step(m)

        tick = pump.tick
    else:
        tick = lambda: None
        spare = []

    g_load = copies.start(r.g_in, L[0])

    def load_first(layer):
        wd = [copies.start(r.dn_own.at[layer], L[3]), copies.start(r.dn_oth.at[layer], L[4])]
        d = [copies.start(r.d.at[layer, i], L[5 + i]) for i in range(2)]
        return wd, d

    def load_second(layer, a):
        a = a or copies.start(r.a.at[layer], L[7])
        wu = [copies.start(r.up_own.at[layer], L[9]), copies.start(r.up_oth.at[layer], L[10])]
        wo = [
            copies.start(r.out_own.at[layer], L[12].at[:, halves[0]]),
            copies.start(r.out_oth.at[layer], L[12].at[:, halves[1]]),
        ]
        return a, wu, wo

    def load_third(layer):
        h2 = copies.start(r.h2.at[layer], L[8])
        o = copies.start(r.o.at[layer], L[13].at[:, halves[0]])
        p = [copies.start(r.p.at[layer, i], L[14].at[:, halves[i]]) for i in range(2)]
        return h2, o, p

    def load_norm(layer, which):
        pair = ((r.xh1, r.r1), (r.xh2, r.r2))[which]
        return [copies.start(pair[0].at[layer], L[11]), copies.start(pair[1].at[layer], r.spread)]

    a_first = copies.start(r.a.at[1], L[7])
    first = load_first(1)
    second = load_second(1, a_first)
    third = load_third(1)
    norm_load = load_norm(1, 1)

    def zero(i, carry):
        r.sums[i] = jnp.zeros((8, width), F32)
        return carry

    lax.fori_loop(0, 8, zero, 0)
    g_load.wait()

    def begin(i, carry):
        at = rows_at(i, CHUNK)
        g[at, :] = L[0][at, :].astype(F32)
        return carry

    lax.fori_loop(0, rows // CHUNK, begin, 0)

    def weight_grad(n, lhs, rhs):
        if reduce:
            if n >= 8:
                pump.need(n - 8)
                remote.settle(pump.items[n - 8].sent)
        elif n >= 8:
            copies.settle(spare[n - 8])
        full = dot_tn(lhs, rhs)
        size = width // GROUP
        for d in range(GROUP):
            r.grad[n % 8, position(d, BACKWARD_ORDERS[n])] = full[d * size : (d + 1) * size].astype(
                BF16
            )
        if not reduce:
            spare.append(copies.save(r.grad.at[n % 8], r.grad_out.at[1 - n // 8, n % 8]))
            return
        pump.step(n)
        tick()

    def norm_back(layer, which, loads, pairs):
        gain = r.gain[layer, which : which + 1, :]
        row = 4 * layer + which
        for load in loads:
            load.wait()
        count = rows // CHUNK
        for i in range(count):
            at = slice(i * CHUNK, (i + 1) * CHUNK)
            grad = dot_nt(L[pairs[0][0]][at, :], L[pairs[0][1]][...])
            for left, right in pairs[1:]:
                grad = grad + dot_nt(L[left][at, :], L[right][...])
            hat = L[11][at, :].astype(F32)
            rs = r.spread[at, 0:1]
            e = grad * gain
            prod = grad * hat
            m1 = jnp.mean(e, axis=-1, keepdims=True)
            m2 = jnp.mean(e * hat, axis=-1, keepdims=True)
            new = g[at, :] + rs * (e - m1 - hat * m2)
            g[at, :] = new
            L[0][at, :] = new.astype(BF16)
            r.sums[row] += jnp.sum(prod.reshape(CHUNK // 8, 8, width), axis=0)
            r.sums[row + 2] += jnp.sum(grad.reshape(CHUNK // 8, 8, width), axis=0)
            if i + 1 in (count // 2, count):
                tick()

    to = [(1, 0), (1, 1), (2, 0), (2, 1), (7, 0), (7, 1)]

    def attend(group):
        n = 3 * group
        count = rows // TILE
        (sq, hq), (sk, hk), (sv, hv) = to[n : n + 3]

        def lanes(side, head):
            return slice(side * cols + head * HEAD_DIM, side * cols + (head + 1) * HEAD_DIM)

        def part(j, head):
            return L[3 + (n + j) // 2], lanes((n + j) % 2, head)

        for first_head in range(0, heads, HEADS_AT_ONCE):
            both = range(first_head, min(first_head + HEADS_AT_ONCE, heads))
            steps = [(i, head) for head in both for i in range(count)]
            q, k, v = (
                [part(j, head)[0][rows_of(i), part(j, head)[1]] for i, head in steps]
                for j, rows_of in enumerate((own_rows, key_rows, key_rows))
            )
            do = [L[6][own_rows(i), lanes(group, head)] for i, head in steps]
            p = [L[14][own_rows(i), lanes(group, head)] for i, head in steps]
            dp = [dot_nt(x, y) for x, y in zip(do, v)]
            wide_p = [x.astype(F32) for x in p]
            inner = [jnp.sum(x * y, axis=-1, keepdims=True) for x, y in zip(dp, wide_p)]
            ds = [(y * (x - z)).astype(BF16) for x, y, z in zip(dp, wide_p, inner)]
            dq = [dot_nn(x, y) for x, y in zip(ds, k)]
            dk = [dot_tn(x, y) for x, y in zip(ds, q)]
            dv = [dot_tn(x, y) for x, y in zip(p, do)]
            for m, (i, head) in enumerate(steps):
                L[sq][own_rows(i), lanes(hq, head)] = (dq[m] * SCALE).astype(BF16)
                if i == 0:
                    own_k, own_v = dk[m][:TILE], dv[m][:TILE]
                else:
                    own_k, own_v = dk[m][TILE:], dv[m][TILE:]
                if i + 1 < count:
                    own_k = own_k + dk[m + 1][:TILE]
                    own_v = own_v + dv[m + 1][:TILE]
                L[sk][own_rows(i), lanes(hk, head)] = (own_k * SCALE).astype(BF16)
                L[sv][own_rows(i), lanes(hv, head)] = own_v.astype(BF16)
            tick()

    for layer in (1, 0):
        base = 8 * (1 - layer)
        wd_load, d_load = first
        a_load, wu_load, wo_load = second
        h2_load, o_load, p_load = third
        a_load.wait()
        for i in range(2):
            weight_grad(base + i, L[0][...], L[7][:, halves[i]])
        for i in range(2):
            wd_load[i].wait()
            d_load[i].wait()
            for at in halves:
                da = dot_nn(L[0][...], L[3 + i][:, at])
                L[1 + i][:, at] = (da * L[5 + i][:, at].astype(F32)).astype(BF16)
                tick()
            if i == 0:
                h2_load.wait()
                for j in range(2):
                    weight_grad(base + 2 + j, L[8][...], L[1][:, halves[j]])
        qkv_load = [
            copies.start(r.qkv.at[layer, j], L[3 + j // 2].at[:, halves[j % 2]]) for j in range(6)
        ]
        h1_load = copies.start(r.h1.at[layer], L[8])
        for load in wu_load:
            load.wait()
        norm_back(layer, 1, norm_load, ((1, 9), (2, 10)))

        def load_wq(some):
            return [
                copies.start(
                    r.qkv_own.at[layer, j] if j < 3 else r.qkv_oth.at[layer, j - 3],
                    L[(9, 10, 12)[j // 2]].at[:, halves[j % 2]],
                )
                for j in some
            ]

        wq_load = load_wq(range(4))
        norm_load = load_norm(layer, 0)
        for i in range(2):
            wo_load[i].wait()
            L[6][:, halves[i]] = dot_nn(L[0][...], L[12][:, halves[i]]).astype(BF16)
            tick()
        wq_load += load_wq(range(4, 6))
        o_load.wait()
        weight_grad(base + 4, L[0][...], L[13][:, halves[0]])
        for load in (*qkv_load, *p_load):
            load.wait()
        attend(0)
        h1_load.wait()
        for j in range(3):
            slot, side = to[j]
            weight_grad(base + 5 + j, L[8][...], L[slot][:, halves[side]])
        attend(1)
        if layer == 1:
            first = load_first(0)
            third = load_third(0)
        for load in wq_load:
            load.wait()
        norm_back(layer, 0, norm_load, ((1, 9), (2, 10), (7, 12)))
        if layer == 1:
            second = load_second(0, None)
            norm_load = load_norm(0, 1)
    copies.save(g, r.g_out)
    for k in range(8):
        r.flat[k : k + 1, :] = jnp.sum(r.sums[k], axis=0, keepdims=True)
    if not reduce:
        copies.save(r.flat, r.flat_out)
        copies.finish()
        return
    sends = []
    for o in range(1, GROUP):
        to_dev = lax.rem(low + o, GROUP)
        sends.append(
            remote.start(
                r.flat.at[:, rows_at(to_dev // 2, 128)], r.slots.at[o], (me - low + to_dev, t)
            )
        )
    tick()
    while pump.at < len(BACKWARD_PLAN):
        tick()
    for n in range(16):
        pump.need(n)
    total = r.flat[:, rows_at(low // 2, 128)]
    for o, copy in enumerate(sends):
        copy.wait_recv()
        total = total + r.slots[o + 1]
    r.flat_f[...] = total
    copies.save(r.flat_f, r.flat_out)
    copies.finish()
    remote.finish()


def call(kernel, ins, outs, scratch, name, collective, flops):
    split = lambda v: v if isinstance(v, tuple) else (v, ANY)
    in_items = {k: split(v) for k, v in ins.items()}
    out_items = {k: split(v) for k, v in outs.items()}
    names = (*in_items, *out_items, *scratch)
    params = dict(vmem_limit_bytes=VMEM_LIMIT, has_side_effects=True)
    if collective is not None:
        params.update(collective_id=collective)
    made = pl.pallas_call(
        functools.partial(kernel, names),
        out_shape=tuple(v for v, _ in out_items.values()),
        in_specs=[pl.BlockSpec(memory_space=s) for _, s in in_items.values()],
        out_specs=tuple(pl.BlockSpec(memory_space=s) for _, s in out_items.values()),
        scratch_shapes=list(scratch.values()),
        compiler_params=pltpu.CompilerParams(**params),
        cost_estimate=pl.CostEstimate(flops=flops, bytes_accessed=60 << 20, transcendentals=0),
        name=name,
    )(*(v for v, _ in in_items.values()))
    return SimpleNamespace(**dict(zip(out_items, made)))


def forward(x, lengths, gain, shift, weights):
    rows, width = x.shape
    w_qkv, w_out, w_up, w_dn = weights
    cols, half = w_qkv.shape[-1], w_up.shape[-1]
    shape = jax.ShapeDtypeStruct
    wide, slab = (rows, width), (rows, cols)
    like = lambda w: shape(w.shape, BF16)
    two = lambda *dims, dtype=BF16: shape((2, *dims), dtype)
    ins = dict(
        x_in=x, lengths=(lengths, VMEM), gain=(gain, VMEM), shift=(shift, VMEM),
        qkv_own=w_qkv, out_own=w_out, up_own=w_up, dn_own=w_dn,
    )
    outs = dict(
        qkv_oth=like(w_qkv), out_oth=like(w_out), up_oth=like(w_up), dn_oth=like(w_dn),
        h1_out=two(*wide), xh1_out=two(*wide), r1_out=two(rows, 128, dtype=F32),
        qkv_out=two(6, *slab), p_out=two(2, *slab), o_out=two(*slab),
        h2_out=two(*wide), xh2_out=two(*wide), r2_out=two(rows, 128, dtype=F32),
        a_out=two(rows, half), d_out=two(2, rows, half),
        y_out=shape(wide, BF16),
    )
    copies = 16 * 8
    scratch = dict(
        x=VMEM(wide, F32), x_raw=VMEM(wide, BF16),
        h1=VMEM(wide, BF16), xh1=VMEM(wide, BF16), r1=VMEM((rows, 128), F32),
        h2=VMEM(wide, BF16), xh2=VMEM(wide, BF16), r2=VMEM((rows, 128), F32),
        qkv=VMEM((6, *slab), BF16), o=VMEM((2, *slab), BF16), p=VMEM((2, *slab), BF16),
        mask=VMEM((rows, 128), F32),
        a=VMEM((2, rows, half), BF16), d=VMEM((2, rows, half), BF16),
        wq=VMEM((6, width, cols), BF16), wo=VMEM((2, width, cols), BF16),
        wu=VMEM((2, width, half), BF16), wd=VMEM((2, width, half), BF16),
        sem=pltpu.SemaphoreType.DMA((80,)),
        send=pltpu.SemaphoreType.DMA((copies,)), recv=pltpu.SemaphoreType.DMA((copies,)),
    )
    flops = 4 * rows * (6 * cols * width + 2 * cols * width + 4 * half * width)
    return call(forward_kernel, ins, outs, scratch, "forward", 0, flops)


def backward(reduce, g, gain, weights, kept):
    rows, width = g.shape
    w_qkv, w_out, w_up, w_dn = weights
    cols, half = w_qkv.shape[-1], w_up.shape[-1]
    shape = jax.ShapeDtypeStruct
    wide = (rows, width)
    block = width // GROUP
    ins = dict(
        g_in=g, gain=(gain, VMEM),
        qkv_own=w_qkv, out_own=w_out, up_own=w_up, dn_own=w_dn,
        qkv_oth=kept.qkv_oth, out_oth=kept.out_oth, up_oth=kept.up_oth, dn_oth=kept.dn_oth,
        h1=kept.h1_out, xh1=kept.xh1_out, r1=kept.r1_out, qkv=kept.qkv_out, p=kept.p_out, o=kept.o_out,
        h2=kept.h2_out, xh2=kept.xh2_out, r2=kept.r2_out, a=kept.a_out, d=kept.d_out,
    )
    outs = dict(g_out=shape(wide, F32))
    recv = lambda k: VMEM((8, GROUP >> (k + 1), block, cols), BF16)
    scratch = dict(
        g=VMEM(wide, F32), spread=VMEM((rows, 128), F32),
        sums=VMEM((8, 8, width), F32), flat=VMEM((8, width), F32),
        sem=pltpu.SemaphoreType.DMA((96,)),
        grad=VMEM((8, GROUP, block, cols), BF16),
    )
    scratch.update({f"{SLOT}{i}": VMEM(wide, BF16) for i in range(15)})
    if not reduce:
        outs.update(flat_out=shape((8, width), F32), grad_out=shape((2, 8, GROUP, block, cols), BF16))
    else:
        copies = 16 * 4 + GROUP
        part = lambda *dims: shape((2, *dims), F32)
        outs.update(
            dn_out=part(block, half), up_out=part(block, half), out_out=part(block, cols),
            qkv_out=part(3, block, cols), flat_out=shape((8, 128), F32),
        )
        scratch.update(
            send=pltpu.SemaphoreType.DMA((copies,)), recv=pltpu.SemaphoreType.DMA((copies,)),
            r0=recv(0), r1_=recv(1), r2_=recv(2), r3=recv(3), final=VMEM((16, block, cols), F32),
            slots=VMEM((GROUP, 8, 128), F32), flat_f=VMEM((8, 128), F32),
        )
    flops = 4 * rows * (2 * 6 * cols * width + 3 * cols * width + 6 * half * width)
    return call(
        functools.partial(backward_kernel, reduce), ins, outs, scratch,
        "backward", 1 if reduce else None, flops,
    )


def deliver_kernel(block, *args):
    ins, outs, held, sems = args[:6], args[7:13], args[15:21], args[21]
    parts = []
    for n, ref in enumerate(ins):
        pieces = 4 if ref.shape[0] > 2 else 2
        size = ref.shape[0] // pieces
        parts += [(n, slice(i * size, (i + 1) * size)) for i in range(pieces)]
    arrive = [
        pltpu.make_async_copy(ins[n].at[at], held[n].at[at], sems.at[0, k])
        for k, (n, at) in enumerate(parts)
    ]
    leave = [
        pltpu.make_async_copy(held[n].at[at], outs[n].at[at], sems.at[1, k])
        for k, (n, at) in enumerate(parts)
    ]
    for copy in arrive:
        copy.start()
    flat = args[6][...]
    odd = lax.rem(lax.axis_index("dp"), 2) == 1
    flat = jnp.where(odd, flat[:, block : 2 * block], flat[:, :block])
    for layer in range(2):
        args[13][layer] = flat[4 * layer : 4 * layer + 2]
        args[14][layer] = flat[4 * layer + 2 : 4 * layer + 4]
    for come, go in zip(arrive, leave):
        come.wait()
        go.start()
    for copy in leave:
        copy.wait()


def deliver(kept, back):
    given = (kept.y_out, back.g_out, back.qkv_out, back.out_out, back.up_out, back.dn_out)
    shape = jax.ShapeDtypeStruct
    block = kept.y_out.shape[1] // GROUP
    small = shape((2, 2, block), F32)
    return pl.pallas_call(
        functools.partial(deliver_kernel, block),
        out_shape=(*(shape(v.shape, v.dtype) for v in given), small, small),
        in_specs=[pl.BlockSpec(memory_space=ANY)] * 6 + [pl.BlockSpec(memory_space=VMEM)],
        out_specs=(*[pl.BlockSpec(memory_space=ANY)] * 6, *[pl.BlockSpec(memory_space=VMEM)] * 2),
        scratch_shapes=[VMEM(v.shape, v.dtype) for v in given] + [pltpu.SemaphoreType.DMA((2, 16))],
        compiler_params=pltpu.CompilerParams(vmem_limit_bytes=VMEM_LIMIT),
        name="deliver",
    )(*given, back.flat_out)


def local(n_dp, tokens, lengths, w_qkv, w_out, w_up, w_down, norm_gain, norm_bias, cotangent):
    rows, width = tokens.shape
    cols = w_qkv.shape[3]
    weights = (jnp.transpose(w_qkv, (0, 2, 1, 3)), w_out, w_up, w_down)
    kept = forward(tokens, lengths, norm_gain, norm_bias, weights)
    reduce = n_dp == GROUP
    back = backward(reduce, cotangent, norm_gain, weights, kept)
    if reduce:
        y, grad, qkv, out, up, dn, gain, shift = deliver(kept, back)
        return (y, grad, jnp.transpose(qkv, (0, 2, 1, 3)), out, up, dn, gain, shift)

    def total(*parts):
        layers = []
        for layer in range(2):
            found = []
            for i in parts:
                n = 8 * (1 - layer) + i
                places = [position(d, BACKWARD_ORDERS[n]) for d in range(GROUP)]
                piece = back.grad_out[layer, i].astype(F32)
                found.append(jnp.concatenate([piece[at] for at in places]))
            layers.append(jnp.concatenate(found, axis=1))
        return lax.psum_scatter(jnp.stack(layers), "dp", scatter_dimension=1, tiled=True)

    dn, up, out = total(0, 1), total(2, 3), total(4)
    qkv = jnp.stack([total(5), total(6), total(7)], axis=1)
    flat = back.flat_out.reshape(2, 4, width)
    flat = lax.psum_scatter(flat, "dp", scatter_dimension=2, tiled=True)
    gain, shift = flat[:, :2], flat[:, 2:]
    qkv = jnp.transpose(qkv, (0, 2, 1, 3))
    return (kept.y_out, back.g_out, qkv, out, up, dn, gain, shift)


def solution(mesh):
    placed = (
        P("dp", None),
        P("dp", None),
        P(None, None, None, "tensor"),
        P(None, None, "tensor"),
        P(None, None, "tensor"),
        P(None, None, "tensor"),
        P(),
        P(),
        P("dp", None),
    )
    return jax.shard_map(
        functools.partial(local, mesh.shape["dp"]),
        mesh=mesh,
        in_specs=placed,
        out_specs=(
            P("dp", None),
            P("dp", None),
            P(None, "dp", None, "tensor"),
            P(None, "dp", "tensor"),
            P(None, "dp", "tensor"),
            P(None, "dp", "tensor"),
            P(None, None, "dp"),
            P(None, None, "dp"),
        ),
        check_vma=False,
    )
```
